256 devices in a mesh: seq: 64 (over x, z, core), head: 4 (over y).
Axes of the slice: x: 4, y: 4, z: 8, core: 2. Of those that a mesh axis runs over, the one named last changes fastest.
Arguments:
- latent: bfloat16 [64, 16, 1024], P('seq'), may hold values from -6 to 6
- stem_weight: bfloat16 [192, 3072], replicated, may hold values from -0.4375 to 0.4375
- stem_bias: float32 [3072], replicated, may hold values from -6 to 6
- mod_shift: float32 [3072], replicated, may hold values from -3 to 3
- mod_scale: float32 [3072], replicated, may hold values from -3 to 3
- qkv_weight: bfloat16 [3072, 3, 12, 128], P(None, None, 'head'), may hold values from -0.109375 to 0.109375
- q_gain: float32 [128], replicated, may hold values from 0.1 to 1.9
- k_gain: float32 [128], replicated, may hold values from 0.1 to 1.9
- tile_lists: int32 [128, 4], replicated, may hold values from 0 to 127, as said below
- out_grad: bfloat16 [16384, 12, 128], P('seq', 'head'), may hold values from -0.125 to 0.125
Outputs:
- qkv_weight_grad: float32 [3072, 3, 12, 128], P('seq', None, 'head')
- stem_weight_grad: float32 [192, 3072], P(None, 'head')
- vector_grad: float32 [3, 3072], P(None, 'head')
The draws below stay inside these ranges and needn't reach their ends.
Inputs may be any that keep to these rules, and one draw needn't show every extreme that they name: `tile_lists`: row b holds 4 different tiles of tile b's own group of 8 tiles (b - b % 8 to b - b % 8 + 7), the first being b itself.
All inputs are finite; a program needn't handle non-finite values.
Results may differ from the reference program's by a relative error of at most 0.0078.
Values may be sent and summed in bfloat16 or wider, within the bound.
No kernel may reach another device: no remote copies, remote signals or barrier semaphores. Data moves between devices by JAX's collectives and lax.ppermute only.
A program may use at most 128 MiB of HBM per device.

```python
import jax
import jax.numpy as jnp
from jax import lax

D = 3072
HEADS = 12
HD = 128
CH = 16
TT = 2
TS = 8
KNB = 4
HG = 32
WG = 16
FRAMES = 32
TOKENS = 16384
PIX = 2048
PIXH = 1024
PIN = 192
TPG = 8
TILE = 128
NTILES = 128


def draw_tile_lists(key, part):
    raw_scores = jax.random.randint(key, (NTILES, TPG), 0, 1 << 20)
    local_ids = jnp.arange(TPG, dtype=jnp.int32)
    own_local = jnp.arange(NTILES, dtype=jnp.int32) % TPG
    scores = raw_scores * TPG + local_ids[None, :]
    scores = jnp.where(local_ids[None, :] == own_local[:, None], -1, scores)
    ordered = jnp.argsort(scores, axis=1, stable=True)[:, :KNB].astype(jnp.int32)
    group_base = jnp.arange(NTILES, dtype=jnp.int32) // TPG * TPG
    return ordered + group_base[:, None]


def block_levels(key, shape, shards, smallest, top_value):
    def one(dim, parts):
        steps = jax.random.uniform(jax.random.fold_in(jax.random.fold_in(key, 6), dim), (parts,), jnp.float32, smallest / len(shards), top_value / len(shards))
        return jnp.repeat(jnp.exp(steps), shape[dim] // parts).reshape((-1,) + (1,) * (len(shape) - dim - 1))

    loudness = one(*shards[0])
    for cut in shards[1:]:
        loudness = loudness * one(*cut)
    return loudness


def scatter_about(own_key, shape, width, bound, shards=(), held_as=jnp.bfloat16):
    values = jax.random.normal(own_key, shape, jnp.float32) * width
    if len(shards) > 0:
        values = block_levels(own_key, shape, shards, -0.22, 0.18) * values
    return jnp.clip(values, min=-bound, max=bound).astype(held_as)


def setup_inputs(seed: int = 0) -> dict:
    seeds = jax.random.split(jax.random.key(seed), 11)
    latent = scatter_about(seeds[0], (2 * FRAMES, CH, PIXH), 1.0, 6.0, ((0, 64),))
    stem_weight = scatter_about(seeds[1], (PIN, D), PIN ** -0.5, 0.4375)
    stem_bias = scatter_about(seeds[2], (D,), 1.0, 6.0, (), jnp.float32)
    mod_shift = scatter_about(seeds[3], (D,), 0.5, 3.0, (), jnp.float32)
    mod_scale = scatter_about(seeds[4], (D,), 0.5, 3.0, (), jnp.float32)
    qkv_weight = scatter_about(seeds[5], (D, 3, HEADS, HD), D ** -0.5, 0.109375, ((2, 4),))
    q_gain = jnp.clip(1.0 + 0.18 * jax.random.normal(seeds[6], (HD,), jnp.float32), 0.1, 1.9)
    k_gain = jnp.clip(1.0 + 0.18 * jax.random.normal(seeds[7], (HD,), jnp.float32), 0.1, 1.9)
    tile_lists = draw_tile_lists(jax.random.fold_in(seeds[10], 71), 0)
    out_grad = scatter_about(seeds[9], (TOKENS, HEADS, HD), (TOKENS ** -0.5), 0.125, ((0, 64), (1, 4)))
    return dict(latent=latent, stem_weight=stem_weight, stem_bias=stem_bias, mod_shift=mod_shift, mod_scale=mod_scale, qkv_weight=qkv_weight, q_gain=q_gain, k_gain=k_gain, tile_lists=tile_lists, out_grad=out_grad)


ln_eps = 1e-06

def frames_to_tiles(blocks, row_total, col_total, tile_side):
    frames = blocks.shape[0]
    remain = blocks.shape[2:]
    shaped = blocks.reshape((frames, row_total // tile_side, tile_side, col_total // tile_side, tile_side) + remain)
    shaped = jnp.transpose(shaped, (1, 3, 0, 2, 4) + tuple(range(5, 5 + len(remain))))
    return shaped.reshape((row_total // tile_side * (col_total // tile_side), frames * tile_side * tile_side) + remain)

def tiles_to_frames(blocks, frames, row_total, col_total, tile_side):
    remain = blocks.shape[2:]
    shaped = blocks.reshape((row_total // tile_side, col_total // tile_side, frames, tile_side, tile_side) + remain)
    shaped = jnp.transpose(shaped, (2, 0, 3, 1, 4) + tuple(range(5, 5 + len(remain))))
    return shaped.reshape((frames, row_total * col_total) + remain)

def qk_norm(raw_values, gain_vector):
    return raw_values * lax.rsqrt(lax.optimization_barrier(jnp.mean(raw_values * raw_values, -1, keepdims=True)) + ln_eps) * gain_vector

def norm_back(feature_grad, normed, inv_std, mod_scale):
    scaled = feature_grad * (1.0 + mod_scale)
    return (scaled - lax.optimization_barrier(jnp.mean(scaled, -1, keepdims=True)) - normed * lax.optimization_barrier(jnp.mean(scaled * normed, -1, keepdims=True))) * inv_std

def attend(queries, out_grads, key_vals, values, score_scale):
    fq = queries.astype(jnp.float32)
    fo = out_grads.astype(jnp.float32)
    fk = key_vals.astype(jnp.float32)
    fv = values.astype(jnp.float32)
    scores = jnp.einsum('brhe,bmhe->bhrm', fq, fk) * score_scale
    weights = jnp.exp(scores)
    probability = weights / lax.optimization_barrier(jnp.sum(weights, axis=-1, keepdims=True))
    rounded = probability.astype(jnp.bfloat16).astype(jnp.float32)
    slopes = jnp.einsum('brhe,bmhe->bhrm', fo, fv)
    centre = lax.optimization_barrier(jnp.sum(probability * slopes, axis=-1, keepdims=True))
    shaped = (probability * (slopes - centre)).astype(jnp.bfloat16).astype(jnp.float32)
    query_grad = jnp.einsum('bhrm,bmhe->brhe', shaped, fk) * score_scale
    key_grad = jnp.einsum('bhrm,brhe->bmhe', shaped, fq) * score_scale
    value_grad = jnp.einsum('bhrm,brhe->bmhe', rounded, fo)
    return (query_grad, key_grad, value_grad)

def reference(latent, stem_weight, stem_bias, mod_shift, mod_scale, qkv_weight, q_gain, k_gain, tile_lists, out_grad):
    frames = FRAMES
    tok_count = HG * WG
    groups = frames // TT
    whole = latent.reshape(frames, 2, CH, PIXH)
    whole = jnp.transpose(whole, (0, 2, 1, 3)).reshape(frames, CH, PIX)
    zero_frame = jnp.zeros((1,) + whole.shape[1:], whole.dtype)
    padded = jnp.concatenate([zero_frame, whole, zero_frame], 0)
    window = jnp.stack([padded[:-2], padded[1:-1], padded[2:]], 1)
    patches = window.reshape(frames, 3, CH, HG, 2, WG, 2)
    patches = jnp.transpose(patches, (0, 3, 5, 1, 2, 4, 6)).reshape(frames * tok_count, PIN)
    embedded = jnp.dot(patches, stem_weight, preferred_element_type=jnp.float32) + stem_bias
    centred = embedded - lax.optimization_barrier(jnp.mean(embedded, -1, keepdims=True))
    inv_std = lax.rsqrt(lax.optimization_barrier(jnp.mean(centred * centred, -1, keepdims=True)) + ln_eps)
    normed = centred * inv_std
    hidden = (normed * (1.0 + mod_scale) + mod_shift).astype(jnp.bfloat16)
    columns = 3 * HEADS * HD
    flat_weight = qkv_weight.reshape(D, columns)
    projected = jnp.dot(hidden, flat_weight, preferred_element_type=jnp.float32).reshape(-1, 3, HEADS, HD)
    q_normed, q_back = jax.vjp(lambda raw_values: qk_norm(raw_values, q_gain), projected[:, 0])
    k_normed, k_back = jax.vjp(lambda raw_values: qk_norm(raw_values, k_gain), projected[:, 1])
    queries = q_normed.astype(jnp.bfloat16)
    key_vals = k_normed.astype(jnp.bfloat16)
    values = projected[:, 2].astype(jnp.bfloat16)

    def to_tiles(tokens_array):
        shaped = tokens_array.reshape((groups, TT, tok_count) + tokens_array.shape[1:])
        tiled = jax.vmap(lambda blocks: frames_to_tiles(blocks, HG, WG, TS))(shaped)
        return tiled.reshape((NTILES, TILE) + tokens_array.shape[1:])

    def from_tiles(tile_array):
        shaped = tile_array.reshape((groups, NTILES // groups, TILE) + tile_array.shape[2:])
        framed = jax.vmap(lambda blocks: tiles_to_frames(blocks, TT, HG, WG, TS))(shaped)
        return framed.reshape((groups * TT * tok_count,) + tile_array.shape[2:])
    q_tiles = to_tiles(queries)
    o_tiles = to_tiles(out_grad)
    k_tiles = to_tiles(key_vals)
    v_tiles = to_tiles(values)
    score_scale = HD ** (-0.5)

    def visit_tile(accumulated, tile_index):
        key_acc, value_acc = accumulated
        chosen = tile_lists[tile_index]
        near_keys = jnp.take(k_tiles, chosen, axis=0).reshape(1, KNB * TILE, HEADS, HD)
        near_values = jnp.take(v_tiles, chosen, axis=0).reshape(1, KNB * TILE, HEADS, HD)
        query_grad, key_grad, value_grad = attend(q_tiles[tile_index][None], o_tiles[tile_index][None], near_keys, near_values, score_scale)
        key_acc = key_acc.at[chosen].add(key_grad.reshape(KNB, TILE, HEADS, HD))
        value_acc = value_acc.at[chosen].add(value_grad.reshape(KNB, TILE, HEADS, HD))
        return ((key_acc, value_acc), query_grad[0])
    zero_tiles = jnp.zeros(k_tiles.shape, jnp.float32)
    (key_acc, value_acc), query_tiles = lax.scan(visit_tile, (zero_tiles, zero_tiles), jnp.arange(NTILES, dtype=jnp.int32))
    raw_q = q_back(from_tiles(query_tiles))[0]
    raw_k = k_back(from_tiles(key_acc))[0]
    mixed_grad = jnp.stack([raw_q, raw_k, from_tiles(value_acc)], 1).astype(jnp.bfloat16).reshape(-1, columns)
    qkv_weight_grad = jnp.dot(hidden.T, mixed_grad, preferred_element_type=jnp.float32).reshape(D, 3, HEADS, HD)
    feature_grad = jnp.dot(mixed_grad, flat_weight.T, preferred_element_type=jnp.float32)
    embed_grad = norm_back(feature_grad, normed, inv_std, mod_scale)
    stem_weight_grad = jnp.dot(patches.astype(jnp.float32).T, embed_grad, precision=lax.Precision.HIGHEST)
    vector_grad = jnp.stack([lax.optimization_barrier(jnp.sum(feature_grad, 0)), lax.optimization_barrier(jnp.sum(feature_grad * normed, 0)), lax.optimization_barrier(jnp.sum(embed_grad, 0))])
    return (qkv_weight_grad, stem_weight_grad, vector_grad)
```

```python
import functools

import jax
import jax.numpy as jnp
from jax import lax
from jax.experimental import pallas as pl
from jax.experimental.pallas import tpu as pltpu
from jax.sharding import PartitionSpec as P

TT = 2
TS = 8
KNB = 4
HG = 32
WG = 16

ln_eps = 1e-06
F32 = jnp.float32
BF16 = jnp.bfloat16

NN = (((1,), (0,)), ((), ()))
NT = (((1,), (1,)), ((), ()))
TN = (((0,), (0,)), ((), ()))


def mm(a, b, dims=NN):
    return lax.dot_general(a, b, dims, preferred_element_type=F32)


def split2(v):
    hi = v.astype(BF16)
    return hi, (v - hi.astype(F32)).astype(BF16)


def split3(v):
    hi = v.astype(BF16)
    return (hi,) + split2(v - hi.astype(F32))


BLOCK = 512


def forward_kernel(
    ids, pext, stem, bias, scale, shift, w9, proj, hid, nrm, inv_out, wv, scale_out, emb, hid_all, sw, w, sc, sh, sems
):
    width, block = emb.shape
    share = hid.shape[0]
    rows = share // 16
    pin = stem.shape[0]
    hd = w9.shape[2]
    j = ids[0]
    first = pl.program_id(0) == 0
    copies = [
        pltpu.make_async_copy(w9.at[n], w.at[:, n * hd : (n + 1) * hd], sems.at[n]) for n in range(w9.shape[0])
    ]

    @pl.when(first)
    def _():
        for copy in copies:
            copy.start()
        row = lax.broadcasted_iota(jnp.int32, (256 - pin, width), 0)
        parts = split3(bias[...])
        fill = jnp.zeros((256 - pin, width), F32)
        for n in range(3):
            fill = jnp.where(row == n, parts[n].astype(F32), fill)
        sw[0:pin, :] = stem[...]
        sw[pin:256, :] = fill.astype(BF16)
        ones = jnp.ones((8, 128), BF16)
        row = lax.broadcasted_iota(jnp.int32, (8, width), 0)
        for value, column in ((1.0 + scale[...], sc), (shift[...], sh)):
            parts = split3(value)
            fill = jnp.zeros((8, width), F32)
            for n in range(3):
                fill = jnp.where(row == n, parts[n].astype(F32), fill)
            column[...] = mm(fill.astype(BF16), ones, TN)
        for g in range(16):
            at = pl.ds(pl.multiple_of(4 * rows * g + rows * j, 16), rows)
            scale_out[g * rows : (g + 1) * rows, :] = sc[at, :]

    step = width // 4
    for n in range(4):
        emb[n * step : (n + 1) * step, :] = mm(sw[:, n * step : (n + 1) * step], pext[...], TN)
    chunk = 64

    def add(i, acc):
        x = emb[pl.ds(pl.multiple_of(i * chunk, chunk), chunk), :]
        return acc + jnp.sum(x.reshape(chunk // 8, 8, block), axis=0)

    total = lax.fori_loop(0, width // chunk, add, jnp.zeros((8, block), F32), unroll=2)
    mu = jnp.sum(total, axis=0, keepdims=True) * (1.0 / width)

    def add_squares(i, acc):
        x = emb[pl.ds(pl.multiple_of(i * chunk, chunk), chunk), :] - mu
        return acc + jnp.sum((x * x).reshape(chunk // 8, 8, block), axis=0)

    total = lax.fori_loop(0, width // chunk, add_squares, jnp.zeros((8, block), F32), unroll=2)
    inv = lax.rsqrt(jnp.sum(total, axis=0, keepdims=True) * (1.0 / width) + ln_eps)
    inv_out[...] = jnp.broadcast_to(inv, (8, block))

    def normalise(i, carry):
        at = pl.ds(pl.multiple_of(i * chunk, chunk), chunk)
        n = (emb[at, :] - mu) * inv
        emb[at, :] = n
        wide = lambda ref: jnp.concatenate([ref[at, :]] * (block // 128), 1)
        hid_all[at, :] = (n * wide(sc) + wide(sh)).astype(BF16)
        return carry

    lax.fori_loop(0, width // chunk, normalise, 0, unroll=2)
    for g in range(16):
        at = pl.ds(pl.multiple_of(4 * rows * g + rows * j, 16), rows)
        hid[g * rows : (g + 1) * rows, :] = hid_all[at, :]
        nrm[g * rows : (g + 1) * rows, :] = emb[at, :]

    @pl.when(first)
    def _():
        for copy in copies:
            copy.wait()
        row = lax.broadcasted_iota(jnp.int32, (8, width), 0)
        fill = jnp.zeros((8, width), F32)
        for n, part in enumerate(split2(1.0 + scale[...]) + split2(shift[...])):
            fill = jnp.where(row == n, part.astype(F32), fill)
        wv[...] = mm(fill.astype(BF16), w[...])

    proj[...] = mm(hid_all[...], w[...], TN)


def forward(ids, pext, stem, bias, scale, shift, w9, block=BLOCK):
    tokens = pext.shape[1]
    count, width, hd = w9.shape
    columns = count * hd
    share = width // 4
    whole = lambda i, ids: (0, 0)
    rows = lambda i, ids: (i, 0)
    lanes = lambda i, ids: (0, i)
    once = pl.Buffered(1)
    vec = pl.BlockSpec((1, width), whole, pipeline_mode=once)
    return pl.pallas_call(
        forward_kernel,
        grid_spec=pltpu.PrefetchScalarGridSpec(
            num_scalar_prefetch=1,
            grid=(tokens // block,),
            in_specs=[
                pl.BlockSpec((256, block), lanes),
                pl.BlockSpec(stem.shape, whole, pipeline_mode=once),
                vec,
                vec,
                vec,
                pl.BlockSpec(memory_space=pl.ANY),
            ],
            out_specs=[
                pl.BlockSpec((block, columns), rows),
                pl.BlockSpec((share, block), lanes),
                pl.BlockSpec((share, block), lanes),
                pl.BlockSpec((8, block), lanes),
                pl.BlockSpec((8, columns), whole),
                pl.BlockSpec((share, 128), whole),
            ],
            scratch_shapes=[
                pltpu.VMEM((width, block), F32),
                pltpu.VMEM((width, block), BF16),
                pltpu.VMEM((256, width), BF16),
                pltpu.VMEM((width, columns), BF16),
                pltpu.VMEM((width, 128), F32),
                pltpu.VMEM((width, 128), F32),
                pltpu.SemaphoreType.DMA((count,)),
            ],
        ),
        out_shape=[
            jax.ShapeDtypeStruct((tokens, columns), F32),
            jax.ShapeDtypeStruct((share, tokens), BF16),
            jax.ShapeDtypeStruct((share, tokens), F32),
            jax.ShapeDtypeStruct((8, tokens), F32),
            jax.ShapeDtypeStruct((8, columns), F32),
            jax.ShapeDtypeStruct((share, 128), F32),
        ],
        compiler_params=pltpu.CompilerParams(vmem_limit_bytes=60 * 2**20),
        cost_estimate=pl.CostEstimate(
            flops=2 * tokens * width * (columns + 256), bytes_accessed=24 * 2**20, transcendentals=0
        ),
        name="forward",
    )(ids, pext, stem, bias, scale, shift, w9)


def attention_kernel(
    ids, lists, pq, pk, pv, og, qg, kg, wq, wk, wv, mixed, means, q_s, k_s, v_s, o_s, iq_s, ik_s, dq_s, dk_s, dv_s, a1_s, a2_s
):
    tokens, hd = pq.shape
    score_scale = hd ** (-0.5)
    j, g = ids[0], ids[1]
    tile = TT * TS * TS
    count = tokens // tile
    frame_tile = TS * TS
    for raw, gain, keep, store in ((pq, qg, iq_s, q_s), (pk, kg, ik_s, k_s)):
        r = raw[...]
        inv = lax.rsqrt(jnp.mean(r * r, -1, keepdims=True) + ln_eps)
        keep[...] = inv
        store[...] = (r * inv * gain[...]).astype(BF16)
    v_s[...] = pv[...].astype(BF16)
    dk_s[...] = jnp.zeros_like(dk_s)
    dv_s[...] = jnp.zeros_like(dv_s)
    for half in range(2):
        for t in range(count // 2):
            for frame in range(2):
                at = ((half * (count // 2) + t) * 2 + frame) * frame_tile
                o_s[at : at + frame_tile, :] = og[jnp.bitwise_xor(j, 2 * frame + half), 0, t]

    def visit(b, carry):
        mine = pl.ds(pl.multiple_of(b * tile, tile), tile)
        q_b = q_s[mine, :]
        o_b = o_s[mine, :]
        near = [
            pl.ds(pl.multiple_of((lists[g * count + b, n] - g * count) * tile, tile), tile)
            for n in range(KNB)
        ]
        keys = jnp.concatenate([k_s[at, :] for at in near], 0)
        vals = jnp.concatenate([v_s[at, :] for at in near], 0)
        e = jnp.exp(mm(q_b, keys, NT) * score_scale)
        prob = e * (1.0 / jnp.sum(e, -1, keepdims=True))
        slope = mm(o_b, vals, NT)
        centre = jnp.sum(prob * slope, -1, keepdims=True)
        shaped = (prob * (slope - centre)).astype(BF16)
        rounded = prob.astype(BF16)
        dq_s[mine, :] = mm(shaped, keys) * score_scale
        dk = mm(shaped, q_b, TN)
        dv = mm(rounded, o_b, TN)
        for n, at in enumerate(near):
            dk_s[at, :] += dk[n * tile : (n + 1) * tile, :]
            dv_s[at, :] += dv[n * tile : (n + 1) * tile, :]
        return carry

    lax.fori_loop(0, count, visit, 0, unroll=2)

    @pl.when(pl.program_id(0) == 0)
    def _():
        a1_s[...] = jnp.zeros_like(a1_s)
        a2_s[...] = jnp.zeros_like(a2_s)

    m1 = a1_s[...]
    m2 = a2_s[...]
    for i, (raw, gain, keep, grad, factor, vec) in enumerate(
        (
            (pq, qg, iq_s, dq_s, 1.0, wq),
            (pk, kg, ik_s, dk_s, score_scale, wk),
            (pv, None, None, dv_s, 1.0, wv),
        )
    ):
        r = raw[...]
        if gain is None:
            out = grad[...]
        else:
            inv = keep[...]
            u = grad[...] * (gain[...] * factor)
            out = inv * (u - r * (inv * inv * jnp.mean(r * u, -1, keepdims=True)))
        out = out.astype(BF16)
        mixed[i] = out
        out = out.astype(F32)
        m1 = m1 + out * (vec[0:1, :] + vec[1:2, :])
        m2 = m2 + out * (r - (vec[2:3, :] + vec[3:4, :]))
    a1_s[...] = m1
    a2_s[...] = m2

    @pl.when(pl.program_id(0) == pl.num_programs(0) - 1)
    def _():
        for n, total in enumerate((m1, m2)):
            row = jnp.sum(jnp.transpose(total), axis=0, keepdims=True)
            means[n] = jnp.broadcast_to(row, (8, tokens))


def attention(ids, lists, proj, og, q_gain, k_gain, wv):
    tokens, columns = proj.shape
    hd = q_gain.shape[-1]
    heads = columns // 3 // hd
    pick = lambda i: pl.BlockSpec((tokens, hd), lambda h, *_: (0, i * heads + h))
    vec = lambda i: pl.BlockSpec((8, hd), lambda h, *_: (0, i * heads + h))
    gain = pl.BlockSpec((1, hd), lambda h, *_: (0, 0))
    return pl.pallas_call(
        attention_kernel,
        grid_spec=pltpu.PrefetchScalarGridSpec(
            num_scalar_prefetch=2,
            grid=(heads,),
            in_specs=[
                pick(0),
                pick(1),
                pick(2),
                pl.BlockSpec((4, 1) + og.shape[2:], lambda h, *_: (0, h, 0, 0, 0)),
                gain,
                gain,
                vec(0),
                vec(1),
                vec(2),
            ],
            out_specs=[
                pl.BlockSpec((3, tokens, hd), lambda h, *_: (0, 0, h)),
                pl.BlockSpec((2, 8, tokens), lambda h, *_: (0, 0, 0)),
            ],
            scratch_shapes=[pltpu.VMEM((tokens, hd), BF16)] * 4
            + [pltpu.VMEM((tokens, 1), F32)] * 2
            + [pltpu.VMEM((tokens, hd), F32)] * 5,
        ),
        out_shape=[
            jax.ShapeDtypeStruct((3, tokens, heads * hd), BF16),
            jax.ShapeDtypeStruct((2, 8, tokens), F32),
        ],
        compiler_params=pltpu.CompilerParams(vmem_limit_bytes=48 * 2**20),
        cost_estimate=pl.CostEstimate(
            flops=10 * tokens * 512 * hd * heads, bytes_accessed=10 * 2**20, transcendentals=tokens * 512 * heads
        ),
        name="attention",
    )(ids, lists, proj, proj, proj, og, q_gain, k_gain, wv, wv, wv)


def weight_kernel(ids, hid, mixed, *outs):
    rows, hd = outs[0].shape[2:]
    block = 4 * rows
    x = ids[1] // 4
    for k in range(4):
        at = pl.ds(pl.multiple_of((x + k) % 4 * block, block), block)
        mine = hid[at, :]
        for i in range(3):
            part = mm(mine, mixed[i]).astype(BF16)
            for n in range(3):
                for z in range(4):
                    outs[k][z, 3 * i + n] = part[z * rows : (z + 1) * rows, n * hd : (n + 1) * hd]


def weight_part(ids, hid, mixed, hd):
    share, tokens = hid.shape
    third = mixed.shape[2]
    out = jax.ShapeDtypeStruct((4, 3 * third // hd, share // 16, hd), BF16)
    vmem = pl.BlockSpec(memory_space=pltpu.VMEM)
    return pl.pallas_call(
        weight_kernel,
        in_specs=[pl.BlockSpec(memory_space=pltpu.SMEM), vmem, vmem],
        out_specs=[vmem] * 4,
        out_shape=[out] * 4,
        compiler_params=pltpu.CompilerParams(vmem_limit_bytes=40 * 2**20),
        cost_estimate=pl.CostEstimate(
            flops=2 * share * tokens * 3 * third, bytes_accessed=6 * 2**20, transcendentals=0
        ),
        name="weight_part",
    )(ids, hid, mixed)


def stem_kernel(ids, w9, mixed, nrm, sc, means, inv, pext, own, *others):
    third = mixed.shape[2]
    block, tokens = nrm.shape
    count, _, _, _, hd = w9.shape
    w = jnp.concatenate([w9[n, :, 0].reshape(block, hd) for n in range(count)], 1)
    fg = mm(w[:, 0:third], mixed[0], NT)
    for i in range(1, 3):
        fg = fg + mm(w[:, i * third : (i + 1) * third], mixed[i], NT)
    n = nrm[...]
    scale = 1.0 / (4 * 4 * block)
    m1 = means[0, 0:1, :] * scale
    m2 = means[1, 0:1, :] * scale
    eg = (fg * jnp.concatenate([sc[...]] * (tokens // 128), 1) - m1 - n * m2) * inv[0:1, :]
    hi, lo = split2(eg)
    grad = mm(hi, pext[...], NT) + mm(lo, pext[...], NT)
    shift_grad = jnp.sum(fg, -1, keepdims=True)
    scale_grad = jnp.sum(fg * n, -1, keepdims=True)
    lane = lax.broadcasted_iota(jnp.int32, grad.shape, 1)
    grad = jnp.where(lane == 193, shift_grad, grad)
    grad = jnp.where(lane == 194, scale_grad, grad)
    for k, out in enumerate((own,) + others):

        @pl.when(pl.program_id(0) == k)
        def _():
            out[...] = grad.astype(out.dtype)


def stem_part(ids, w9, mixed, nrm, sc, means, inv, pext):
    share, tokens = nrm.shape
    block = share // 4
    count, width, hd = w9.shape
    w9 = w9.reshape(count, 16, 4, share // 16, hd)
    rows = lambda i, ids: ((i + ids[2]) % 4, 0)
    once = pl.Buffered(1)
    shape = (block, 256)
    return pl.pallas_call(
        stem_kernel,
        grid_spec=pltpu.PrefetchScalarGridSpec(
            num_scalar_prefetch=1,
            grid=(4,),
            in_specs=[
                pl.BlockSpec((count, 4, 1, share // 16, hd), lambda i, ids: (0, (i + ids[2]) % 4, ids[0], 0, 0)),
                pl.BlockSpec(mixed.shape, lambda i, ids: (0, 0, 0), pipeline_mode=once),
                pl.BlockSpec((block, tokens), rows),
                pl.BlockSpec((block, 128), rows),
                pl.BlockSpec(means.shape, lambda i, ids: (0, 0, 0), pipeline_mode=once),
                pl.BlockSpec(inv.shape, lambda i, ids: (0, 0), pipeline_mode=once),
                pl.BlockSpec(pext.shape, lambda i, ids: (0, 0), pipeline_mode=once),
            ],
            out_specs=[pl.BlockSpec(shape, lambda i, ids: (0, 0))] * 4,
        ),
        out_shape=[jax.ShapeDtypeStruct(shape, F32)] + [jax.ShapeDtypeStruct(shape, BF16)] * 3,
        compiler_params=pltpu.CompilerParams(vmem_limit_bytes=40 * 2**20),
        cost_estimate=pl.CostEstimate(
            flops=2 * share * tokens * (count * hd + 512), bytes_accessed=10 * 2**20, transcendentals=0
        ),
        name="stem_part",
    )(ids, w9, mixed, nrm, sc, means, inv, pext)


def per_device(
    latent,
    stem_weight,
    stem_bias,
    mod_shift,
    mod_scale,
    qkv_weight,
    q_gain,
    k_gain,
    tile_lists,
    out_grad,
):
    width = qkv_weight.shape[0]
    heads, hd = qkv_weight.shape[2:]
    columns = 3 * heads * hd
    channels = latent.shape[1]
    seq = lax.axis_size("seq")
    groups = seq // 4
    rows = width // seq
    s = lax.axis_index("seq")
    h = lax.axis_index("head")
    g, j = s // 4, s % 4
    half_rows = HG // 2
    tr, tc = half_rows // TS, WG // TS
    tiles = tr * tc
    cell = TS * TS
    x, z = g // 4, g % 4

    def xor(value, mask):
        return lax.ppermute(value, "seq", [(a, a ^ mask) for a in range(seq)])

    piece = latent.reshape(channels, tr, TS, 2, tc, TS, 2)
    piece = jnp.transpose(piece, (0, 3, 6, 1, 4, 2, 5)).reshape(4 * channels, tiles * cell)
    other = xor(piece, 1)
    is_low = s % 2 == 0
    frame = jnp.concatenate([jnp.where(is_low, piece, other), jnp.where(is_low, other, piece)], 1)
    behind = lax.ppermute(frame, "seq", [(a, a + 2) for a in range(seq - 2)])
    ahead = lax.ppermute(frame, "seq", [(a, a - 2) for a in range(2, seq)])
    far_pairs = [(a, a - 4 if a % 4 < 2 else a + 4) for a in range(seq)]
    far = lax.ppermute(frame, "seq", [(a, b) for a, b in far_pairs if 0 <= b < seq])
    even = j < 2
    window = [
        jnp.where(even, behind, far),
        jnp.where(even, frame, behind),
        jnp.where(even, ahead, frame),
        jnp.where(even, far, ahead),
    ]
    fill = jnp.zeros((256 - 12 * channels, 2 * tiles * cell), BF16).at[:3].set(1)
    pext = jnp.stack(
        [
            jnp.concatenate(window[k : k + 3] + [fill], 0).reshape(256, 2 * tiles, cell)
            for k in range(2)
        ],
        2,
    ).reshape(256, 4 * tiles * cell)

    grads = jnp.transpose(out_grad, (1, 0, 2)).reshape(heads, tr, TS, tc, TS, hd)
    grads = jnp.transpose(grads, (0, 1, 3, 2, 4, 5)).reshape(heads, tiles, cell, hd)
    grads = jnp.stack([grads] + [xor(grads, mask) for mask in (1, 2, 3)])

    w9 = jnp.transpose(qkv_weight, (1, 2, 0, 3)).reshape(3 * heads, width, hd)
    ids = jnp.stack([j, g, h]).astype(jnp.int32)

    proj, hid, nrm, inv, wv, sc = forward(
        ids, pext, stem_weight, stem_bias[None], mod_scale[None], mod_shift[None], w9
    )
    mixed, means = attention(ids, tile_lists, proj, grads, q_gain[None], k_gain[None], wv)
    weight = weight_part(ids, hid, mixed, hd)
    stem = stem_part(ids, w9, mixed, nrm, sc, means, inv, pext)

    def shift(value, step, place):
        def target(a):
            ax, az, aj = a // 16, a // 4 % 4, a % 4
            if place == "x":
                ax = (ax + step) % 4
            else:
                az = (az + step) % 4
            return ax * 16 + az * 4 + aj

        return lax.ppermute(value, "seq", [(a, target(a)) for a in range(seq)])

    total = weight[0].astype(F32)
    for k in range(1, 4):
        total = total + shift(weight[k], k, "x").astype(F32)
    total = total.astype(BF16)

    def part(k):
        return lax.dynamic_index_in_dim(total, (z + k) % 4, 0, keepdims=False)

    weight_grad = part(0).astype(F32)
    for k in range(1, 4):
        weight_grad = weight_grad + shift(part(k), k, "z").astype(F32)
    weight_grad = jnp.transpose(weight_grad.reshape(3, heads, rows, hd), (2, 0, 1, 3))

    total = stem[0]
    count = lax.axis_size("head")
    for k in range(1, count):
        pairs = [(a, (a + k) % count) for a in range(count)]
        total = total + lax.ppermute(stem[k], "head", pairs).astype(F32)
    for mask in (16, 32, 4, 8):
        held = lax.reduce_precision(total, 8, 7)
        total = held + xor(held.astype(BF16), mask).astype(F32)
    full = total.astype(BF16)[None]
    for mask in (1, 2):
        other = xor(full, mask)
        low = (s // mask) % 2 == 0
        full = jnp.concatenate([jnp.where(low, full, other), jnp.where(low, other, full)])
    full = full.reshape(4, groups // 4, rows, 256)
    full = jnp.transpose(full, (1, 0, 2, 3)).reshape(width // 4, 256).T.astype(F32)
    base = 12 * channels
    stem_grad = full[:base]
    vector_grad = jnp.stack([full[base + 1], full[base + 2], full[base]])
    return (weight_grad, stem_grad, vector_grad)


def solution(mesh):
    return jax.shard_map(
        per_device,
        mesh=mesh,
        in_specs=(
            P("seq", None, None),
            P(),
            P(),
            P(),
            P(),
            P(None, None, "head", None),
            P(),
            P(),
            P(),
            P("seq", "head", None),
        ),
        out_specs=(P("seq", None, "head", None), P(None, "head"), P(None, "head")),
        check_vma=False,
    )
```

```python
import functools

import jax
import jax.numpy as jnp
from jax import lax
from jax.experimental import pallas as pl
from jax.experimental.pallas import tpu as pltpu
from jax.sharding import PartitionSpec as P

TT = 2
TS = 8
KNB = 4
HG = 32
WG = 16

ln_eps = 1e-06
LOG2E = 1.4426950408889634
F32 = jnp.float32
BF16 = jnp.bfloat16

NN = (((1,), (0,)), ((), ()))
NT = (((1,), (1,)), ((), ()))
TN = (((0,), (0,)), ((), ()))


def mm(a, b, dims=NN):
    return lax.dot_general(a, b, dims, preferred_element_type=F32)


def split2(v):
    hi = v.astype(BF16)
    return hi, (v - hi.astype(F32)).astype(BF16)


def split3(v):
    hi = v.astype(BF16)
    return (hi,) + split2(v - hi.astype(F32))


BLOCK = 512


def forward_kernel(
    ids, pext, stem, bias, scale, shift, w9, proj, hid, nrm, inv_out, wv, scale_out, emb, hid_all, sw, w, sc, sh, sems
):
    width, block = emb.shape
    share = hid.shape[0]
    rows = share // 16
    pin = stem.shape[0]
    hd = w9.shape[2]
    j = ids[0]
    first = pl.program_id(0) == 0
    copies = [
        pltpu.make_async_copy(w9.at[n], w.at[:, n * hd : (n + 1) * hd], sems.at[n]) for n in range(w9.shape[0])
    ]

    @pl.when(first)
    def _():
        for copy in copies:
            copy.start()
        row = lax.broadcasted_iota(jnp.int32, (256 - pin, width), 0)
        parts = split3(bias[...])
        fill = jnp.zeros((256 - pin, width), F32)
        for n in range(3):
            fill = jnp.where(row == n, parts[n].astype(F32), fill)
        sw[0:pin, :] = stem[...]
        sw[pin:256, :] = fill.astype(BF16)
        ones = jnp.ones((8, 128), BF16)
        row = lax.broadcasted_iota(jnp.int32, (8, width), 0)
        for value, column in ((1.0 + scale[...], sc), (shift[...], sh)):
            parts = split3(value)
            fill = jnp.zeros((8, width), F32)
            for n in range(3):
                fill = jnp.where(row == n, parts[n].astype(F32), fill)
            column[...] = mm(fill.astype(BF16), ones, TN)
        for g in range(16):
            at = pl.ds(pl.multiple_of(4 * rows * g + rows * j, 16), rows)
            scale_out[g * rows : (g + 1) * rows, :] = sc[at, :]

    step = width // 4
    for n in range(4):
        emb[n * step : (n + 1) * step, :] = mm(sw[:, n * step : (n + 1) * step], pext[...], TN)
    chunk = 64

    def add(i, acc):
        x = emb[pl.ds(pl.multiple_of(i * chunk, chunk), chunk), :]
        return acc + jnp.sum(x.reshape(chunk // 8, 8, block), axis=0)

    total = lax.fori_loop(0, width // chunk, add, jnp.zeros((8, block), F32), unroll=2)
    mu = jnp.sum(total, axis=0, keepdims=True) * (1.0 / width)

    def add_squares(i, acc):
        x = emb[pl.ds(pl.multiple_of(i * chunk, chunk), chunk), :] - mu
        return acc + jnp.sum((x * x).reshape(chunk // 8, 8, block), axis=0)

    total = lax.fori_loop(0, width // chunk, add_squares, jnp.zeros((8, block), F32), unroll=2)
    inv = lax.rsqrt(jnp.sum(total, axis=0, keepdims=True) * (1.0 / width) + ln_eps)
    inv_out[...] = jnp.broadcast_to(inv, (8, block))

    def normalise(i, carry):
        at = pl.ds(pl.multiple_of(i * chunk, chunk), chunk)
        n = (emb[at, :] - mu) * inv
        emb[at, :] = n
        wide = lambda ref: jnp.concatenate([ref[at, :]] * (block // 128), 1)
        hid_all[at, :] = (n * wide(sc) + wide(sh)).astype(BF16)
        return carry

    lax.fori_loop(0, width // chunk, normalise, 0, unroll=2)
    for g in range(16):
        at = pl.ds(pl.multiple_of(4 * rows * g + rows * j, 16), rows)
        hid[g * rows : (g + 1) * rows, :] = hid_all[at, :]
        nrm[g * rows : (g + 1) * rows, :] = emb[at, :]

    @pl.when(first)
    def _():
        for copy in copies:
            copy.wait()
        row = lax.broadcasted_iota(jnp.int32, (8, width), 0)
        fill = jnp.zeros((8, width), F32)
        for n, part in enumerate(split2(1.0 + scale[...]) + split2(shift[...])):
            fill = jnp.where(row == n, part.astype(F32), fill)
        wv[...] = mm(fill.astype(BF16), w[...])

    proj[...] = mm(hid_all[...], w[...], TN)


def forward(ids, pext, stem, bias, scale, shift, w9, block=BLOCK):
    tokens = pext.shape[1]
    count, width, hd = w9.shape
    columns = count * hd
    share = width // 4
    whole = lambda i, ids: (0, 0)
    rows = lambda i, ids: (i, 0)
    lanes = lambda i, ids: (0, i)
    once = pl.Buffered(1)
    vec = pl.BlockSpec((1, width), whole, pipeline_mode=once)
    return pl.pallas_call(
        forward_kernel,
        grid_spec=pltpu.PrefetchScalarGridSpec(
            num_scalar_prefetch=1,
            grid=(tokens // block,),
            in_specs=[
                pl.BlockSpec((256, block), lanes),
                pl.BlockSpec(stem.shape, whole, pipeline_mode=once),
                vec,
                vec,
                vec,
                pl.BlockSpec(memory_space=pl.ANY),
            ],
            out_specs=[
                pl.BlockSpec((block, columns), rows),
                pl.BlockSpec((share, block), lanes),
                pl.BlockSpec((share, block), lanes),
                pl.BlockSpec((8, block), lanes),
                pl.BlockSpec((8, columns), whole),
                pl.BlockSpec((share, 128), whole),
            ],
            scratch_shapes=[
                pltpu.VMEM((width, block), F32),
                pltpu.VMEM((width, block), BF16),
                pltpu.VMEM((256, width), BF16),
                pltpu.VMEM((width, columns), BF16),
                pltpu.VMEM((width, 128), F32),
                pltpu.VMEM((width, 128), F32),
                pltpu.SemaphoreType.DMA((count,)),
            ],
        ),
        out_shape=[
            jax.ShapeDtypeStruct((tokens, columns), F32),
            jax.ShapeDtypeStruct((share, tokens), BF16),
            jax.ShapeDtypeStruct((share, tokens), F32),
            jax.ShapeDtypeStruct((8, tokens), F32),
            jax.ShapeDtypeStruct((8, columns), F32),
            jax.ShapeDtypeStruct((share, 128), F32),
        ],
        compiler_params=pltpu.CompilerParams(vmem_limit_bytes=60 * 2**20),
        cost_estimate=pl.CostEstimate(
            flops=2 * tokens * width * (columns + 256), bytes_accessed=24 * 2**20, transcendentals=0
        ),
        name="forward",
    )(ids, pext, stem, bias, scale, shift, w9)


def attention_kernel(
    ids, lists, pq, pk, pv, og, qg, kg, wq, wk, wv, mixed, means, q_s, k_s, v_s, o_s, iq_s, ik_s, dq_s, dk_s, dv_s, a1_s, a2_s
):
    tokens, hd = pq.shape
    score_scale = hd ** (-0.5)
    j, g = ids[0], ids[1]
    tile = TT * TS * TS
    count = tokens // tile
    frame_tile = TS * TS
    for raw, gain, keep, store in ((pq, qg, iq_s, q_s), (pk, kg, ik_s, k_s)):
        r = raw[...]
        inv = lax.rsqrt(jnp.mean(r * r, -1, keepdims=True) + ln_eps)
        keep[...] = inv
        store[...] = (r * inv * gain[...]).astype(BF16)
    v_s[...] = pv[...].astype(BF16)
    dk_s[...] = jnp.zeros_like(dk_s)
    dv_s[...] = jnp.zeros_like(dv_s)
    for half in range(2):
        for t in range(count // 2):
            for frame in range(2):
                at = ((half * (count // 2) + t) * 2 + frame) * frame_tile
                o_s[at : at + frame_tile, :] = og[jnp.bitwise_xor(j, 2 * frame + half), 0, t]

    def visit(b, carry):
        mine = pl.ds(pl.multiple_of(b * tile, tile), tile)
        q_b = q_s[mine, :]
        o_b = o_s[mine, :]
        near = [
            pl.ds(pl.multiple_of((lists[g * count + b, n] - g * count) * tile, tile), tile)
            for n in range(KNB)
        ]
        keys = jnp.concatenate([k_s[at, :] for at in near], 0)
        vals = jnp.concatenate([v_s[at, :] for at in near], 0)
        e = jnp.exp2(mm(q_b, keys, NT) * (score_scale * LOG2E))
        prob = e * (1.0 / jnp.sum(e, -1, keepdims=True))
        slope = mm(o_b, vals, NT)
        centre = jnp.sum(prob * slope, -1, keepdims=True)
        shaped = (prob * (slope - centre)).astype(BF16)
        rounded = prob.astype(BF16)
        dq_s[mine, :] = mm(shaped, keys) * score_scale
        dk = mm(q_b, shaped, TN)
        dv = mm(o_b, rounded, TN)
        for n, at in enumerate(near):
            dk_s[:, at] += dk[:, n * tile : (n + 1) * tile]
            dv_s[:, at] += dv[:, n * tile : (n + 1) * tile]
        return carry

    lax.fori_loop(0, count, visit, 0, unroll=8)

    @pl.when(pl.program_id(0) == 0)
    def _():
        a1_s[...] = jnp.zeros_like(a1_s)
        a2_s[...] = jnp.zeros_like(a2_s)

    m1 = a1_s[...]
    m2 = a2_s[...]
    for i, (raw, gain, keep, grad, factor, vec) in enumerate(
        (
            (pq, qg, iq_s, dq_s[...], 1.0, wq),
            (pk, kg, ik_s, jnp.transpose(dk_s[...]), score_scale, wk),
            (pv, None, None, jnp.transpose(dv_s[...]), 1.0, wv),
        )
    ):
        r = raw[...]
        if gain is None:
            out = grad
        else:
            inv = keep[...]
            u = grad * (gain[...] * factor)
            out = inv * (u - r * (inv * inv * jnp.mean(r * u, -1, keepdims=True)))
        out = out.astype(BF16)
        mixed[i] = out
        out = out.astype(F32)
        m1 = m1 + out * (vec[0:1, :] + vec[1:2, :])
        m2 = m2 + out * (r - (vec[2:3, :] + vec[3:4, :]))
    a1_s[...] = m1
    a2_s[...] = m2

    @pl.when(pl.program_id(0) == pl.num_programs(0) - 1)
    def _():
        for n, total in enumerate((m1, m2)):
            row = jnp.sum(jnp.transpose(total), axis=0, keepdims=True)
            means[n] = jnp.broadcast_to(row, (8, tokens))


def attention(ids, lists, proj, og, q_gain, k_gain, wv):
    tokens, columns = proj.shape
    hd = q_gain.shape[-1]
    heads = columns // 3 // hd
    pick = lambda i: pl.BlockSpec((tokens, hd), lambda h, *_: (0, i * heads + h))
    vec = lambda i: pl.BlockSpec((8, hd), lambda h, *_: (0, i * heads + h))
    gain = pl.BlockSpec((1, hd), lambda h, *_: (0, 0))
    return pl.pallas_call(
        attention_kernel,
        grid_spec=pltpu.PrefetchScalarGridSpec(
            num_scalar_prefetch=2,
            grid=(heads,),
            in_specs=[
                pick(0),
                pick(1),
                pick(2),
                pl.BlockSpec((4, 1) + og.shape[2:], lambda h, *_: (0, h, 0, 0, 0)),
                gain,
                gain,
                vec(0),
                vec(1),
                vec(2),
            ],
            out_specs=[
                pl.BlockSpec((3, tokens, hd), lambda h, *_: (0, 0, h)),
                pl.BlockSpec((2, 8, tokens), lambda h, *_: (0, 0, 0)),
            ],
            scratch_shapes=[pltpu.VMEM((tokens, hd), BF16)] * 4
            + [pltpu.VMEM((tokens, 1), F32)] * 2
            + [pltpu.VMEM((tokens, hd), F32)]
            + [pltpu.VMEM((hd, tokens), F32)] * 2
            + [pltpu.VMEM((tokens, hd), F32)] * 2,
        ),
        out_shape=[
            jax.ShapeDtypeStruct((3, tokens, heads * hd), BF16),
            jax.ShapeDtypeStruct((2, 8, tokens), F32),
        ],
        compiler_params=pltpu.CompilerParams(vmem_limit_bytes=48 * 2**20),
        cost_estimate=pl.CostEstimate(
            flops=10 * tokens * 512 * hd * heads, bytes_accessed=10 * 2**20, transcendentals=tokens * 512 * heads
        ),
        name="attention",
    )(ids, lists, proj, proj, proj, og, q_gain, k_gain, wv, wv, wv)


def weight_kernel(ids, hid, mixed, *outs):
    rows, hd = outs[0].shape[2:]
    block = 4 * rows
    x = ids[1] // 4
    for k in range(4):
        at = pl.ds(pl.multiple_of((x + k) % 4 * block, block), block)
        mine = hid[at, :]
        for i in range(3):
            part = mm(mine, mixed[i]).astype(BF16)
            for n in range(3):
                for z in range(4):
                    outs[k][z, 3 * i + n] = part[z * rows : (z + 1) * rows, n * hd : (n + 1) * hd]


def weight_part(ids, hid, mixed, hd):
    share, tokens = hid.shape
    third = mixed.shape[2]
    out = jax.ShapeDtypeStruct((4, 3 * third // hd, share // 16, hd), BF16)
    vmem = pl.BlockSpec(memory_space=pltpu.VMEM)
    return pl.pallas_call(
        weight_kernel,
        in_specs=[pl.BlockSpec(memory_space=pltpu.SMEM), vmem, vmem],
        out_specs=[vmem] * 4,
        out_shape=[out] * 4,
        compiler_params=pltpu.CompilerParams(vmem_limit_bytes=40 * 2**20),
        cost_estimate=pl.CostEstimate(
            flops=2 * share * tokens * 3 * third, bytes_accessed=6 * 2**20, transcendentals=0
        ),
        name="weight_part",
    )(ids, hid, mixed)


def stem_kernel(ids, w9, mixed, nrm, sc, means, inv, pext, own, *others):
    third = mixed.shape[2]
    block, tokens = nrm.shape
    count, _, _, _, hd = w9.shape
    w = jnp.concatenate([w9[n, :, 0].reshape(block, hd) for n in range(count)], 1)
    fg = mm(w[:, 0:third], mixed[0], NT)
    for i in range(1, 3):
        fg = fg + mm(w[:, i * third : (i + 1) * third], mixed[i], NT)
    n = nrm[...]
    scale = 1.0 / (4 * 4 * block)
    m1 = means[0, 0:1, :] * scale
    m2 = means[1, 0:1, :] * scale
    eg = (fg * jnp.concatenate([sc[...]] * (tokens // 128), 1) - m1 - n * m2) * inv[0:1, :]
    hi, lo = split2(eg)
    grad = mm(hi, pext[...], NT) + mm(lo, pext[...], NT)
    shift_grad = jnp.sum(fg, -1, keepdims=True)
    scale_grad = jnp.sum(fg * n, -1, keepdims=True)
    lane = lax.broadcasted_iota(jnp.int32, grad.shape, 1)
    grad = jnp.where(lane == 193, shift_grad, grad)
    grad = jnp.where(lane == 194, scale_grad, grad)
    for k, out in enumerate((own,) + others):

        @pl.when(pl.program_id(0) == k)
        def _():
            out[...] = grad.astype(out.dtype)


def stem_part(ids, w9, mixed, nrm, sc, means, inv, pext):
    share, tokens = nrm.shape
    block = share // 4
    count, width, hd = w9.shape
    w9 = w9.reshape(count, 16, 4, share // 16, hd)
    rows = lambda i, ids: ((i + ids[2]) % 4, 0)
    once = pl.Buffered(1)
    shape = (block, 256)
    return pl.pallas_call(
        stem_kernel,
        grid_spec=pltpu.PrefetchScalarGridSpec(
            num_scalar_prefetch=1,
            grid=(4,),
            in_specs=[
                pl.BlockSpec((count, 4, 1, share // 16, hd), lambda i, ids: (0, (i + ids[2]) % 4, ids[0], 0, 0)),
                pl.BlockSpec(mixed.shape, lambda i, ids: (0, 0, 0), pipeline_mode=once),
                pl.BlockSpec((block, tokens), rows),
                pl.BlockSpec((block, 128), rows),
                pl.BlockSpec(means.shape, lambda i, ids: (0, 0, 0), pipeline_mode=once),
                pl.BlockSpec(inv.shape, lambda i, ids: (0, 0), pipeline_mode=once),
                pl.BlockSpec(pext.shape, lambda i, ids: (0, 0), pipeline_mode=once),
            ],
            out_specs=[pl.BlockSpec(shape, lambda i, ids: (0, 0))] * 4,
        ),
        out_shape=[jax.ShapeDtypeStruct(shape, F32)] + [jax.ShapeDtypeStruct(shape, BF16)] * 3,
        compiler_params=pltpu.CompilerParams(vmem_limit_bytes=40 * 2**20),
        cost_estimate=pl.CostEstimate(
            flops=1000, bytes_accessed=1000, transcendentals=0
        ),
        name="stem_part",
    )(ids, w9, mixed, nrm, sc, means, inv, pext)


def per_device(
    latent,
    stem_weight,
    stem_bias,
    mod_shift,
    mod_scale,
    qkv_weight,
    q_gain,
    k_gain,
    tile_lists,
    out_grad,
):
    width = qkv_weight.shape[0]
    heads, hd = qkv_weight.shape[2:]
    columns = 3 * heads * hd
    channels = latent.shape[1]
    seq = lax.axis_size("seq")
    groups = seq // 4
    rows = width // seq
    s = lax.axis_index("seq")
    h = lax.axis_index("head")
    g, j = s // 4, s % 4
    half_rows = HG // 2
    tr, tc = half_rows // TS, WG // TS
    tiles = tr * tc
    cell = TS * TS

    def xor(value, mask):
        return lax.ppermute(value, "seq", [(a, a ^ mask) for a in range(seq)])

    piece = latent.reshape(channels, tr, TS, 2, tc, TS, 2)
    piece = jnp.transpose(piece, (0, 3, 6, 1, 4, 2, 5)).reshape(4 * channels, tiles * cell)
    other = xor(piece, 1)
    is_low = s % 2 == 0
    frame = jnp.concatenate([jnp.where(is_low, piece, other), jnp.where(is_low, other, piece)], 1)
    behind = lax.ppermute(frame, "seq", [(a, a + 2) for a in range(seq - 2)])
    ahead = lax.ppermute(frame, "seq", [(a, a - 2) for a in range(2, seq)])
    far_pairs = [(a, a - 4 if a % 4 < 2 else a + 4) for a in range(seq)]
    far = lax.ppermute(frame, "seq", [(a, b) for a, b in far_pairs if 0 <= b < seq])
    even = j < 2
    window = [
        jnp.where(even, behind, far),
        jnp.where(even, frame, behind),
        jnp.where(even, ahead, frame),
        jnp.where(even, far, ahead),
    ]
    fill = jnp.zeros((256 - 12 * channels, 2 * tiles * cell), BF16).at[:3].set(1)
    pext = jnp.stack(
        [
            jnp.concatenate(window[k : k + 3] + [fill], 0).reshape(256, 2 * tiles, cell)
            for k in range(2)
        ],
        2,
    ).reshape(256, 4 * tiles * cell)

    grads = jnp.transpose(out_grad, (1, 0, 2)).reshape(heads, tr, TS, tc, TS, hd)
    grads = jnp.transpose(grads, (0, 1, 3, 2, 4, 5)).reshape(heads, tiles, cell, hd)
    grads = jnp.stack([grads] + [xor(grads, mask) for mask in (1, 2, 3)])

    w9 = jnp.transpose(qkv_weight, (1, 2, 0, 3)).reshape(3 * heads, width, hd)
    ids = jnp.stack([j, g, h]).astype(jnp.int32)

    proj, hid, nrm, inv, wv, sc = forward(
        ids, pext, stem_weight, stem_bias[None], mod_scale[None], mod_shift[None], w9
    )
    mixed, means = attention(ids, tile_lists, proj, grads, q_gain[None], k_gain[None], wv)
    weight = weight_part(ids, hid, mixed, hd)
    mixed, *weight = lax.optimization_barrier((mixed, *weight))
    stem = stem_part(ids, w9, mixed, nrm, sc, means, inv, pext)

    weight_total = weight[0].astype(F32)
    for k in range(1, 4):
        pairs = [(a, (a + 16 * k) % seq) for a in range(seq)]
        weight_total = weight_total + lax.ppermute(weight[k], "seq", pairs).astype(F32)

    total = stem[0]
    count = lax.axis_size("head")
    for k in range(1, count):
        pairs = [(a, (a + k) % count) for a in range(count)]
        total = total + lax.ppermute(stem[k], "head", pairs).astype(F32)

    def pair_sum(value, mask):
        held = lax.reduce_precision(value, 8, 7)
        return held + xor(held.astype(BF16), mask).astype(F32)

    def half_sum(value, mask):
        side = s // mask % 2
        half = value.shape[0] // 2
        kept = lax.dynamic_slice_in_dim(value, side * half, half, 0)
        sent = lax.dynamic_slice_in_dim(value, (1 - side) * half, half, 0)
        return kept + xor(sent.astype(BF16), mask).astype(F32)

    total, weight_total = lax.optimization_barrier((total, weight_total))
    weight_grad = half_sum(half_sum(weight_total, 8), 4)[0]
    weight_grad = jnp.transpose(weight_grad.reshape(3, heads, rows, hd), (2, 0, 1, 3))
    for mask in (4, 8, 16, 32):
        total = pair_sum(total, mask)
    full = total.astype(BF16)[None]
    for mask in (1, 2):
        other = xor(full, mask)
        low = (s // mask) % 2 == 0
        full = jnp.concatenate([jnp.where(low, full, other), jnp.where(low, other, full)])
    full = full.reshape(4, groups // 4, rows, 256)
    full = jnp.transpose(full, (1, 0, 2, 3)).reshape(width // 4, 256).T.astype(F32)
    base = 12 * channels
    stem_grad = full[:base]
    vector_grad = jnp.stack([full[base + 1], full[base + 2], full[base]])
    return (weight_grad, stem_grad, vector_grad)


def solution(mesh):
    return jax.shard_map(
        per_device,
        mesh=mesh,
        in_specs=(
            P("seq", None, None),
            P(),
            P(),
            P(),
            P(),
            P(None, None, "head", None),
            P(),
            P(),
            P(),
            P("seq", "head", None),
        ),
        out_specs=(P("seq", None, "head", None), P(None, "head"), P(None, "head")),
        check_vma=False,
    )
```

```python
import functools

import jax
import jax.numpy as jnp
from jax import lax
from jax.experimental import pallas as pl
from jax.experimental.pallas import tpu as pltpu
from jax.sharding import PartitionSpec as P

TT = 2
TS = 8
KNB = 4
HG = 32
WG = 16

ln_eps = 1e-06
LOG2E = 1.4426950408889634
F32 = jnp.float32
BF16 = jnp.bfloat16

NN = (((1,), (0,)), ((), ()))
NT = (((1,), (1,)), ((), ()))
TN = (((0,), (0,)), ((), ()))


def mm(a, b, dims=NN):
    return lax.dot_general(a, b, dims, preferred_element_type=F32)


def split2(v):
    hi = v.astype(BF16)
    return hi, (v - hi.astype(F32)).astype(BF16)


def split3(v):
    hi = v.astype(BF16)
    return (hi,) + split2(v - hi.astype(F32))


BLOCK = 512


def forward_kernel(
    ids, pext, stem, bias, scale, shift, w9, proj, hid, nrm, inv_out, wv, scale_out, emb, hid_all, sw, w, sc, sh, sems
):
    width, block = emb.shape
    share = hid.shape[0]
    rows = share // 16
    pin = stem.shape[0]
    hd = w9.shape[2]
    j = ids[0]
    first = pl.program_id(0) == 0
    copies = [
        pltpu.make_async_copy(w9.at[n], w.at[:, n * hd : (n + 1) * hd], sems.at[n]) for n in range(w9.shape[0])
    ]

    @pl.when(first)
    def _():
        for copy in copies:
            copy.start()
        row = lax.broadcasted_iota(jnp.int32, (256 - pin, width), 0)
        parts = split3(bias[...])
        fill = jnp.zeros((256 - pin, width), F32)
        for n in range(3):
            fill = jnp.where(row == n, parts[n].astype(F32), fill)
        sw[0:pin, :] = stem[...]
        sw[pin:256, :] = fill.astype(BF16)
        ones = jnp.ones((8, 128), BF16)
        row = lax.broadcasted_iota(jnp.int32, (8, width), 0)
        for value, column in ((1.0 + scale[...], sc), (shift[...], sh)):
            parts = split3(value)
            fill = jnp.zeros((8, width), F32)
            for n in range(3):
                fill = jnp.where(row == n, parts[n].astype(F32), fill)
            column[...] = mm(fill.astype(BF16), ones, TN)
        for g in range(16):
            at = pl.ds(pl.multiple_of(4 * rows * g + rows * j, 16), rows)
            scale_out[g * rows : (g + 1) * rows, :] = sc[at, :]

    step = width // 4
    for n in range(4):
        emb[n * step : (n + 1) * step, :] = mm(sw[:, n * step : (n + 1) * step], pext[...], TN)
    chunk = 64

    def add(i, acc):
        x = emb[pl.ds(pl.multiple_of(i * chunk, chunk), chunk), :]
        return acc + jnp.sum(x.reshape(chunk // 8, 8, block), axis=0)

    total = lax.fori_loop(0, width // chunk, add, jnp.zeros((8, block), F32), unroll=2)
    mu = jnp.sum(total, axis=0, keepdims=True) * (1.0 / width)

    def add_squares(i, acc):
        x = emb[pl.ds(pl.multiple_of(i * chunk, chunk), chunk), :] - mu
        return acc + jnp.sum((x * x).reshape(chunk // 8, 8, block), axis=0)

    total = lax.fori_loop(0, width // chunk, add_squares, jnp.zeros((8, block), F32), unroll=2)
    inv = lax.rsqrt(jnp.sum(total, axis=0, keepdims=True) * (1.0 / width) + ln_eps)
    inv_out[...] = jnp.broadcast_to(inv, (8, block))

    def normalise(i, carry):
        at = pl.ds(pl.multiple_of(i * chunk, chunk), chunk)
        n = (emb[at, :] - mu) * inv
        emb[at, :] = n
        wide = lambda ref: jnp.concatenate([ref[at, :]] * (block // 128), 1)
        hid_all[at, :] = (n * wide(sc) + wide(sh)).astype(BF16)
        return carry

    lax.fori_loop(0, width // chunk, normalise, 0, unroll=2)
    for g in range(16):
        at = pl.ds(pl.multiple_of(4 * rows * g + rows * j, 16), rows)
        hid[g * rows : (g + 1) * rows, :] = hid_all[at, :]
        nrm[g * rows : (g + 1) * rows, :] = emb[at, :].astype(BF16)

    @pl.when(first)
    def _():
        for copy in copies:
            copy.wait()
        row = lax.broadcasted_iota(jnp.int32, (8, width), 0)
        fill = jnp.zeros((8, width), F32)
        for n, part in enumerate(split2(1.0 + scale[...]) + split2(shift[...])):
            fill = jnp.where(row == n, part.astype(F32), fill)
        wv[...] = mm(fill.astype(BF16), w[...])

    proj[...] = mm(hid_all[...], w[...], TN)


def forward(ids, pext, stem, bias, scale, shift, w9, block=BLOCK):
    tokens = pext.shape[1]
    count, width, hd = w9.shape
    columns = count * hd
    share = width // 4
    whole = lambda i, ids: (0, 0)
    rows = lambda i, ids: (i, 0)
    lanes = lambda i, ids: (0, i)
    once = pl.Buffered(1)
    vec = pl.BlockSpec((1, width), whole, pipeline_mode=once)
    return pl.pallas_call(
        forward_kernel,
        grid_spec=pltpu.PrefetchScalarGridSpec(
            num_scalar_prefetch=1,
            grid=(tokens // block,),
            in_specs=[
                pl.BlockSpec((256, block), lanes),
                pl.BlockSpec(stem.shape, whole, pipeline_mode=once),
                vec,
                vec,
                vec,
                pl.BlockSpec(memory_space=pl.ANY),
            ],
            out_specs=[
                pl.BlockSpec((block, columns), rows),
                pl.BlockSpec((share, block), lanes),
                pl.BlockSpec((share, block), lanes),
                pl.BlockSpec((8, block), lanes),
                pl.BlockSpec((8, columns), whole),
                pl.BlockSpec((share, 128), whole),
            ],
            scratch_shapes=[
                pltpu.VMEM((width, block), F32),
                pltpu.VMEM((width, block), BF16),
                pltpu.VMEM((256, width), BF16),
                pltpu.VMEM((width, columns), BF16),
                pltpu.VMEM((width, 128), F32),
                pltpu.VMEM((width, 128), F32),
                pltpu.SemaphoreType.DMA((count,)),
            ],
        ),
        out_shape=[
            jax.ShapeDtypeStruct((tokens, columns), F32),
            jax.ShapeDtypeStruct((share, tokens), BF16),
            jax.ShapeDtypeStruct((share, tokens), BF16),
            jax.ShapeDtypeStruct((8, tokens), F32),
            jax.ShapeDtypeStruct((8, columns), F32),
            jax.ShapeDtypeStruct((share, 128), F32),
        ],
        compiler_params=pltpu.CompilerParams(vmem_limit_bytes=60 * 2**20),
        cost_estimate=pl.CostEstimate(
            flops=2 * tokens * width * (columns + 256), bytes_accessed=24 * 2**20, transcendentals=0
        ),
        name="forward",
    )(ids, pext, stem, bias, scale, shift, w9)


def attention_kernel(
    ids,
    lists,
    pq,
    pk,
    pv,
    og,
    qg,
    kg,
    wq,
    wk,
    wv,
    mixed,
    means,
    q_s,
    k_s,
    v_s,
    o_s,
    kt_s,
    iq_s,
    ik_s,
    dq_s,
    dk_s,
    dv_s,
    a1_s,
    a2_s,
):
    tokens, hd = pq.shape
    score_scale = hd ** (-0.5)
    j, g = ids[0], ids[1]
    tile = TT * TS * TS
    count = tokens // tile
    frame_tile = TS * TS
    first = pl.program_id(0) == 0
    last = pl.program_id(0) == pl.num_programs(0) - 1

    def rows(b):
        return pl.ds(pl.multiple_of(b * tile, tile), tile)

    def prepare(b, carry):
        at = rows(b)
        for raw, gain, keep, store in ((pq, qg, iq_s, q_s), (pk, kg, ik_s, k_s)):
            r = raw[at, :]
            inv = lax.rsqrt(jnp.mean(r * r, -1, keepdims=True) + ln_eps)
            keep[at, :] = inv
            value = r * inv * gain[...]
            store[at, :] = value.astype(BF16)
        kt_s[:, at] = jnp.transpose(value).astype(BF16)
        v_s[at, :] = pv[at, :].astype(BF16)
        half, t = b // (count // 2), b % (count // 2)
        for frame in range(2):
            to = pl.ds(pl.multiple_of(b * tile + frame * frame_tile, frame_tile), frame_tile)
            o_s[to, :] = og[jnp.bitwise_xor(j, 2 * frame + half), 0, t]
        dk_s[at, :] = jnp.zeros((tile, hd), F32)
        dv_s[at, :] = jnp.zeros((tile, hd), F32)
        return carry

    lax.fori_loop(0, count, prepare, 0, unroll=8)

    def visit(b, carry):
        mine = rows(b)
        q_b = q_s[mine, :]
        o_b = o_s[mine, :]
        near = [rows(lists[g * count + b, n] - g * count) for n in range(KNB)]
        keys = jnp.concatenate([k_s[at, :] for at in near], 0)
        keys_t = jnp.concatenate([kt_s[:, at] for at in near], 1)
        vals = jnp.concatenate([v_s[at, :] for at in near], 0)
        e = jnp.exp2(mm(keys, q_b, NT) * (score_scale * LOG2E))
        prob = e * (1.0 / jnp.sum(e, 0, keepdims=True))
        slope = mm(vals, o_b, NT)
        centre = jnp.sum(prob * slope, 0, keepdims=True)
        shaped = (prob * (slope - centre)).astype(BF16)
        rounded = prob.astype(BF16)
        dq_s[:, mine] = mm(keys_t, shaped)
        dk = mm(shaped, q_b)
        dv = mm(rounded, o_b)
        for n, at in enumerate(near):
            dk_s[at, :] += dk[n * tile : (n + 1) * tile, :]
            dv_s[at, :] += dv[n * tile : (n + 1) * tile, :]
        return carry

    lax.fori_loop(0, count, visit, 0, unroll=8)

    @pl.when(first)
    def _():
        a1_s[...] = jnp.zeros_like(a1_s)
        a2_s[...] = jnp.zeros_like(a2_s)

    def finish(b, carry):
        at = rows(b)
        m1 = a1_s[at, :]
        m2 = a2_s[at, :]
        for i, (raw, gain, keep, grad, vec) in enumerate(
            (
                (pq, qg, iq_s, jnp.transpose(dq_s[:, at]), wq),
                (pk, kg, ik_s, dk_s[at, :], wk),
                (pv, None, None, dv_s[at, :], wv),
            )
        ):
            r = raw[at, :]
            out = grad
            if gain is not None:
                inv = keep[at, :]
                u = grad * (gain[...] * score_scale)
                out = inv * (u - r * (inv * inv * jnp.mean(r * u, -1, keepdims=True)))
            out = out.astype(BF16)
            mixed[i, at, :] = out
            out = out.astype(F32)
            m1 = m1 + out * (vec[0:1, :] + vec[1:2, :])
            m2 = m2 + out * (r - (vec[2:3, :] + vec[3:4, :]))
        a1_s[at, :] = m1
        a2_s[at, :] = m2
        return carry

    lax.fori_loop(0, count, finish, 0, unroll=8)

    @pl.when(last)
    def _():
        for n, total in enumerate((a1_s, a2_s)):
            for b in range(count):
                at = slice(b * tile, (b + 1) * tile)
                row = jnp.sum(jnp.transpose(total[at, :]), axis=0, keepdims=True)
                means[n, :, at] = jnp.broadcast_to(row, (8, tile))


def attention(ids, lists, proj, og, q_gain, k_gain, wv):
    tokens, columns = proj.shape
    hd = q_gain.shape[-1]
    heads = columns // 3 // hd
    pick = lambda i: pl.BlockSpec((tokens, hd), lambda h, *_: (0, i * heads + h))
    vec = lambda i: pl.BlockSpec((8, hd), lambda h, *_: (0, i * heads + h))
    gain = pl.BlockSpec((1, hd), lambda h, *_: (0, 0))
    return pl.pallas_call(
        attention_kernel,
        grid_spec=pltpu.PrefetchScalarGridSpec(
            num_scalar_prefetch=2,
            grid=(heads,),
            in_specs=[
                pick(0),
                pick(1),
                pick(2),
                pl.BlockSpec((4, 1) + og.shape[2:], lambda h, *_: (0, h, 0, 0, 0)),
                gain,
                gain,
                vec(0),
                vec(1),
                vec(2),
            ],
            out_specs=[
                pl.BlockSpec((3, tokens, hd), lambda h, *_: (0, 0, h)),
                pl.BlockSpec((2, 8, tokens), lambda h, *_: (0, 0, 0)),
            ],
            scratch_shapes=[pltpu.VMEM((tokens, hd), BF16)] * 4
            + [pltpu.VMEM((hd, tokens), BF16)]
            + [pltpu.VMEM((tokens, 1), F32)] * 2
            + [pltpu.VMEM((hd, tokens), F32)]
            + [pltpu.VMEM((tokens, hd), F32)] * 4,
        ),
        out_shape=[
            jax.ShapeDtypeStruct((3, tokens, heads * hd), BF16),
            jax.ShapeDtypeStruct((2, 8, tokens), F32),
        ],
        compiler_params=pltpu.CompilerParams(vmem_limit_bytes=48 * 2**20),
        cost_estimate=pl.CostEstimate(
            flops=10 * tokens * 512 * hd * heads, bytes_accessed=10 * 2**20, transcendentals=tokens * 512 * heads
        ),
        name="attention",
    )(ids, lists, proj, proj, proj, og, q_gain, k_gain, wv, wv, wv)


def weight_kernel(ids, hid, mixed, *outs):
    rows, hd = outs[0].shape[2:]
    block = 4 * rows
    x = ids[1] // 4
    for k in range(4):
        at = pl.ds(pl.multiple_of((x + k) % 4 * block, block), block)
        mine = hid[at, :]
        for i in range(3):
            part = mm(mine, mixed[i]).astype(BF16)
            for n in range(3):
                for z in range(4):
                    outs[k][z, 3 * i + n] = part[z * rows : (z + 1) * rows, n * hd : (n + 1) * hd]


def weight_part(ids, hid, mixed, hd):
    share, tokens = hid.shape
    third = mixed.shape[2]
    out = jax.ShapeDtypeStruct((4, 3 * third // hd, share // 16, hd), BF16)
    vmem = pl.BlockSpec(memory_space=pltpu.VMEM)
    return pl.pallas_call(
        weight_kernel,
        in_specs=[pl.BlockSpec(memory_space=pltpu.SMEM), vmem, vmem],
        out_specs=[vmem] * 4,
        out_shape=[out] * 4,
        compiler_params=pltpu.CompilerParams(vmem_limit_bytes=40 * 2**20),
        cost_estimate=pl.CostEstimate(
            flops=2 * share * tokens * 3 * third, bytes_accessed=6 * 2**20, transcendentals=0
        ),
        name="weight_part",
    )(ids, hid, mixed)


def stem_kernel(ids, w9, mixed, nrm, sc, means, inv, pext, own, *rest):
    others, (mixed_t,) = rest[:3], rest[3:]
    third = mixed.shape[2]
    block, tokens = nrm.shape
    count, _, _, _, hd = w9.shape
    w = jnp.concatenate([w9[n, :, 0].reshape(block, hd) for n in range(count)], 1)

    @pl.when(pl.program_id(0) == 0)
    def _():
        for i in range(3):
            mixed_t[i * third : (i + 1) * third, :] = jnp.transpose(mixed[i])

    fg = mm(w, mixed_t[...])
    n = nrm[...].astype(F32)
    scale = 1.0 / (4 * 4 * block)
    m1 = means[0, 0:1, :] * scale
    m2 = means[1, 0:1, :] * scale
    eg = (fg * jnp.concatenate([sc[...]] * (tokens // 128), 1) - m1 - n * m2) * inv[0:1, :]
    hi, lo = split2(eg)
    grad = mm(hi, pext[...], NT) + mm(lo, pext[...], NT)
    shift_grad = jnp.sum(fg, -1, keepdims=True)
    scale_grad = jnp.sum(fg * n, -1, keepdims=True)
    lane = lax.broadcasted_iota(jnp.int32, grad.shape, 1)
    grad = jnp.where(lane == 193, shift_grad, grad)
    grad = jnp.where(lane == 194, scale_grad, grad)
    for k, out in enumerate((own,) + others):

        @pl.when(pl.program_id(0) == k)
        def _():
            out[...] = grad.astype(out.dtype)


def stem_part(ids, w9, mixed, nrm, sc, means, inv, pext):
    share, tokens = nrm.shape
    block = share // 4
    count, width, hd = w9.shape
    w9 = w9.reshape(count, 16, 4, share // 16, hd)
    rows = lambda i, ids: ((i + ids[2]) % 4, 0)
    once = pl.Buffered(1)
    shape = (block, 256)
    return pl.pallas_call(
        stem_kernel,
        grid_spec=pltpu.PrefetchScalarGridSpec(
            num_scalar_prefetch=1,
            grid=(4,),
            in_specs=[
                pl.BlockSpec((count, 4, 1, share // 16, hd), lambda i, ids: (0, (i + ids[2]) % 4, ids[0], 0, 0)),
                pl.BlockSpec(mixed.shape, lambda i, ids: (0, 0, 0), pipeline_mode=once),
                pl.BlockSpec((block, tokens), rows),
                pl.BlockSpec((block, 128), rows),
                pl.BlockSpec(means.shape, lambda i, ids: (0, 0, 0), pipeline_mode=once),
                pl.BlockSpec(inv.shape, lambda i, ids: (0, 0), pipeline_mode=once),
                pl.BlockSpec(pext.shape, lambda i, ids: (0, 0), pipeline_mode=once),
            ],
            out_specs=[pl.BlockSpec(shape, lambda i, ids: (0, 0))] * 4,
            scratch_shapes=[pltpu.VMEM((count * hd, tokens), BF16)],
        ),
        out_shape=[jax.ShapeDtypeStruct(shape, F32)] + [jax.ShapeDtypeStruct(shape, BF16)] * 3,
        compiler_params=pltpu.CompilerParams(vmem_limit_bytes=40 * 2**20),
        cost_estimate=pl.CostEstimate(
            flops=1000, bytes_accessed=1000, transcendentals=0
        ),
        name="stem_part",
    )(ids, w9, mixed, nrm, sc, means, inv, pext)


def per_device(
    latent,
    stem_weight,
    stem_bias,
    mod_shift,
    mod_scale,
    qkv_weight,
    q_gain,
    k_gain,
    tile_lists,
    out_grad,
):
    width = qkv_weight.shape[0]
    heads, hd = qkv_weight.shape[2:]
    columns = 3 * heads * hd
    channels = latent.shape[1]
    seq = lax.axis_size("seq")
    groups = seq // 4
    rows = width // seq
    s = lax.axis_index("seq")
    h = lax.axis_index("head")
    g, j = s // 4, s % 4
    half_rows = HG // 2
    tr, tc = half_rows // TS, WG // TS
    tiles = tr * tc
    cell = TS * TS

    def xor(value, mask):
        return lax.ppermute(value, "seq", [(a, a ^ mask) for a in range(seq)])

    is_low = s % 2 == 0
    even = j < 2
    piece = latent.reshape(channels, tr, TS, 2, tc, TS, 2)
    piece = jnp.transpose(piece, (0, 3, 6, 1, 4, 2, 5)).reshape(4 * channels, tiles * cell)
    border = [(a, a - 2 if a % 4 < 2 else a + 2) for a in range(seq)]
    outer = lax.ppermute(piece, "seq", [(a, b) for a, b in border if 0 <= b < seq])
    pair = jnp.stack([outer, piece])
    facing = xor(pair, 2)
    window = jnp.stack(
        [
            jnp.where(even, outer, facing[0]),
            jnp.where(even, piece, facing[1]),
            jnp.where(even, facing[1], piece),
            jnp.where(even, facing[0], outer),
        ]
    )
    grads = jnp.transpose(out_grad, (1, 0, 2)).reshape(heads, tr, TS, tc, TS, hd)
    grads = jnp.transpose(grads, (0, 1, 3, 2, 4, 5)).reshape(heads, tiles, cell, hd)
    grads = jnp.stack([grads, xor(grads, 1)])
    other = xor(window, 1)
    other, grads = lax.optimization_barrier((other, grads))
    grads = jnp.concatenate([grads, xor(grads, 2)])
    window = jnp.concatenate([jnp.where(is_low, window, other), jnp.where(is_low, other, window)], 2)
    fill = jnp.zeros((256 - 12 * channels, 2 * tiles * cell), BF16).at[:3].set(1)
    pext = jnp.stack(
        [
            jnp.concatenate([window[k], window[k + 1], window[k + 2], fill], 0).reshape(
                256, 2 * tiles, cell
            )
            for k in range(2)
        ],
        2,
    ).reshape(256, 4 * tiles * cell)

    w9 = jnp.transpose(qkv_weight, (1, 2, 0, 3)).reshape(3 * heads, width, hd)
    ids = jnp.stack([j, g, h]).astype(jnp.int32)

    proj, hid, nrm, inv, wv, sc = forward(
        ids, pext, stem_weight, stem_bias[None], mod_scale[None], mod_shift[None], w9
    )
    mixed, means = attention(ids, tile_lists, proj, grads, q_gain[None], k_gain[None], wv)
    weight = weight_part(ids, hid, mixed, hd)
    mixed, *weight = lax.optimization_barrier((mixed, *weight))
    stem = stem_part(ids, w9, mixed, nrm, sc, means, inv, pext)

    weight_total = weight[0].astype(F32)
    for k in range(1, 4):
        pairs = [(a, (a + 16 * k) % seq) for a in range(seq)]
        weight_total = weight_total + lax.ppermute(weight[k], "seq", pairs).astype(F32)

    total = stem[0]
    count = lax.axis_size("head")
    for k in range(1, count):
        pairs = [(a, (a + k) % count) for a in range(count)]
        total = total + lax.ppermute(stem[k], "head", pairs).astype(F32)

    def pair_sum(value, mask):
        held = lax.reduce_precision(value, 8, 7)
        return held + xor(held.astype(BF16), mask).astype(F32)

    def half_sum(value, mask):
        side = s // mask % 2
        half = value.shape[0] // 2
        kept = lax.dynamic_slice_in_dim(value, side * half, half, 0)
        sent = lax.dynamic_slice_in_dim(value, (1 - side) * half, half, 0)
        return kept + xor(sent.astype(BF16), mask).astype(F32)

    total, weight_total = lax.optimization_barrier((total, weight_total))
    weight_grad = half_sum(half_sum(weight_total, 8), 4)[0]
    weight_grad = jnp.transpose(weight_grad.reshape(3, heads, rows, hd), (2, 0, 1, 3))
    for mask in (4, 8, 16, 32):
        total = pair_sum(total, mask)
    full = total.astype(BF16)[None]
    for mask in (1, 2):
        other = xor(full, mask)
        low = (s // mask) % 2 == 0
        full = jnp.concatenate([jnp.where(low, full, other), jnp.where(low, other, full)])
    full = full.reshape(4, groups // 4, rows, 256)
    full = jnp.transpose(full, (1, 0, 2, 3)).reshape(width // 4, 256).T.astype(F32)
    base = 12 * channels
    stem_grad = full[:base]
    vector_grad = jnp.stack([full[base + 1], full[base + 2], full[base]])
    return (weight_grad, stem_grad, vector_grad)


def solution(mesh):
    return jax.shard_map(
        per_device,
        mesh=mesh,
        in_specs=(
            P("seq", None, None),
            P(),
            P(),
            P(),
            P(),
            P(None, None, "head", None),
            P(),
            P(),
            P(),
            P("seq", "head", None),
        ),
        out_specs=(P("seq", None, "head", None), P(None, "head"), P(None, "head")),
        check_vma=False,
    )
```

```python
import functools

import jax
import jax.numpy as jnp
from jax import lax
from jax.experimental import pallas as pl
from jax.experimental.pallas import tpu as pltpu
from jax.sharding import PartitionSpec as P

TT = 2
TS = 8
KNB = 4
HG = 32
WG = 16

ln_eps = 1e-06
LOG2E = 1.4426950408889634
F32 = jnp.float32
BF16 = jnp.bfloat16

NN = (((1,), (0,)), ((), ()))
NT = (((1,), (1,)), ((), ()))
TN = (((0,), (0,)), ((), ()))


def mm(a, b, dims=NN):
    return lax.dot_general(a, b, dims, preferred_element_type=F32)


def split2(v):
    hi = v.astype(BF16)
    return hi, (v - hi.astype(F32)).astype(BF16)


def split3(v):
    hi = v.astype(BF16)
    return (hi,) + split2(v - hi.astype(F32))


BLOCK = 512


def forward_kernel(
    ids, pext, stem, bias, scale, shift, w9, proj, hid, nrm, inv_out, wv, scale_out, emb, hid_all, sw, w, sc, sh, sems
):
    width, block = emb.shape
    share = hid.shape[0]
    rows = share // 16
    pin = stem.shape[0]
    hd = w9.shape[2]
    j = ids[0]
    first = pl.program_id(0) == 0
    copies = [
        pltpu.make_async_copy(w9.at[n], w.at[:, n * hd : (n + 1) * hd], sems.at[n]) for n in range(w9.shape[0])
    ]

    @pl.when(first)
    def _():
        for copy in copies:
            copy.start()
        row = lax.broadcasted_iota(jnp.int32, (256 - pin, width), 0)
        parts = split3(bias[...])
        fill = jnp.zeros((256 - pin, width), F32)
        for n in range(3):
            fill = jnp.where(row == n, parts[n].astype(F32), fill)
        sw[0:pin, :] = stem[...]
        sw[pin:256, :] = fill.astype(BF16)
        ones = jnp.ones((8, 128), BF16)
        row = lax.broadcasted_iota(jnp.int32, (8, width), 0)
        for value, column in ((1.0 + scale[...], sc), (shift[...], sh)):
            parts = split3(value)
            fill = jnp.zeros((8, width), F32)
            for n in range(3):
                fill = jnp.where(row == n, parts[n].astype(F32), fill)
            column[...] = mm(fill.astype(BF16), ones, TN)
        for g in range(16):
            at = pl.ds(pl.multiple_of(4 * rows * g + rows * j, 16), rows)
            scale_out[g * rows : (g + 1) * rows, :] = sc[at, :]

    step = width // 4
    for n in range(4):
        emb[n * step : (n + 1) * step, :] = mm(sw[:, n * step : (n + 1) * step], pext[...], TN)
    chunk = 64

    def add(i, acc):
        x = emb[pl.ds(pl.multiple_of(i * chunk, chunk), chunk), :]
        return acc + jnp.sum(x.reshape(chunk // 8, 8, block), axis=0)

    total = lax.fori_loop(0, width // chunk, add, jnp.zeros((8, block), F32), unroll=2)
    mu = jnp.sum(total, axis=0, keepdims=True) * (1.0 / width)

    def add_squares(i, acc):
        x = emb[pl.ds(pl.multiple_of(i * chunk, chunk), chunk), :] - mu
        return acc + jnp.sum((x * x).reshape(chunk // 8, 8, block), axis=0)

    total = lax.fori_loop(0, width // chunk, add_squares, jnp.zeros((8, block), F32), unroll=2)
    inv = lax.rsqrt(jnp.sum(total, axis=0, keepdims=True) * (1.0 / width) + ln_eps)
    inv_out[...] = jnp.broadcast_to(inv, (8, block))

    def normalise(i, carry):
        at = pl.ds(pl.multiple_of(i * chunk, chunk), chunk)
        n = (emb[at, :] - mu) * inv
        emb[at, :] = n
        wide = lambda ref: jnp.concatenate([ref[at, :]] * (block // 128), 1)
        hid_all[at, :] = (n * wide(sc) + wide(sh)).astype(BF16)
        return carry

    lax.fori_loop(0, width // chunk, normalise, 0, unroll=2)
    for g in range(16):
        at = pl.ds(pl.multiple_of(4 * rows * g + rows * j, 16), rows)
        hid[g * rows : (g + 1) * rows, :] = hid_all[at, :]
        nrm[g * rows : (g + 1) * rows, :] = emb[at, :].astype(BF16)

    @pl.when(first)
    def _():
        for copy in copies:
            copy.wait()
        row = lax.broadcasted_iota(jnp.int32, (8, width), 0)
        fill = jnp.zeros((8, width), F32)
        for n, part in enumerate(split2(1.0 + scale[...]) + split2(shift[...])):
            fill = jnp.where(row == n, part.astype(F32), fill)
        wv[...] = mm(fill.astype(BF16), w[...])

    proj[...] = mm(hid_all[...], w[...], TN)


def forward(ids, pext, stem, bias, scale, shift, w9, block=BLOCK):
    tokens = pext.shape[1]
    count, width, hd = w9.shape
    columns = count * hd
    share = width // 4
    whole = lambda i, ids: (0, 0)
    rows = lambda i, ids: (i, 0)
    lanes = lambda i, ids: (0, i)
    once = pl.Buffered(1)
    vec = pl.BlockSpec((1, width), whole, pipeline_mode=once)
    return pl.pallas_call(
        forward_kernel,
        grid_spec=pltpu.PrefetchScalarGridSpec(
            num_scalar_prefetch=1,
            grid=(tokens // block,),
            in_specs=[
                pl.BlockSpec((256, block), lanes),
                pl.BlockSpec(stem.shape, whole, pipeline_mode=once),
                vec,
                vec,
                vec,
                pl.BlockSpec(memory_space=pl.ANY),
            ],
            out_specs=[
                pl.BlockSpec((block, columns), rows),
                pl.BlockSpec((share, block), lanes),
                pl.BlockSpec((share, block), lanes),
                pl.BlockSpec((8, block), lanes),
                pl.BlockSpec((8, columns), whole),
                pl.BlockSpec((share, 128), whole),
            ],
            scratch_shapes=[
                pltpu.VMEM((width, block), F32),
                pltpu.VMEM((width, block), BF16),
                pltpu.VMEM((256, width), BF16),
                pltpu.VMEM((width, columns), BF16),
                pltpu.VMEM((width, 128), F32),
                pltpu.VMEM((width, 128), F32),
                pltpu.SemaphoreType.DMA((count,)),
            ],
        ),
        out_shape=[
            jax.ShapeDtypeStruct((tokens, columns), F32),
            jax.ShapeDtypeStruct((share, tokens), BF16),
            jax.ShapeDtypeStruct((share, tokens), BF16),
            jax.ShapeDtypeStruct((8, tokens), F32),
            jax.ShapeDtypeStruct((8, columns), F32),
            jax.ShapeDtypeStruct((share, 128), F32),
        ],
        compiler_params=pltpu.CompilerParams(vmem_limit_bytes=60 * 2**20),
        cost_estimate=pl.CostEstimate(
            flops=2 * tokens * width * (columns + 256), bytes_accessed=24 * 2**20, transcendentals=0
        ),
        name="forward",
    )(ids, pext, stem, bias, scale, shift, w9)


def attention_kernel(
    ids,
    lists,
    pq,
    pk,
    pv,
    og,
    qg,
    kg,
    wq,
    wk,
    wv,
    mixed,
    means,
    q_s,
    k_s,
    v_s,
    o_s,
    kt_s,
    iq_s,
    ik_s,
    dq_s,
    dk_s,
    dv_s,
    a1_s,
    a2_s,
):
    tokens, hd = pq.shape
    score_scale = hd ** (-0.5)
    j, g = ids[0], ids[1]
    tile = TT * TS * TS
    count = tokens // tile
    frame_tile = TS * TS
    first = pl.program_id(0) == 0
    last = pl.program_id(0) == pl.num_programs(0) - 1

    def rows(b):
        return pl.ds(pl.multiple_of(b * tile, tile), tile)

    def prepare(b, carry):
        at = rows(b)
        for raw, gain, keep, store in ((pq, qg, iq_s, q_s), (pk, kg, ik_s, k_s)):
            r = raw[at, :]
            inv = lax.rsqrt(jnp.mean(r * r, -1, keepdims=True) + ln_eps)
            keep[at, :] = inv
            value = r * inv * gain[...]
            store[at, :] = value.astype(BF16)
        kt_s[:, at] = jnp.transpose(value).astype(BF16)
        v_s[at, :] = pv[at, :].astype(BF16)
        half, t = b // (count // 2), b % (count // 2)
        for frame in range(2):
            to = pl.ds(pl.multiple_of(b * tile + frame * frame_tile, frame_tile), frame_tile)
            o_s[to, :] = og[jnp.bitwise_xor(j, 2 * frame + half), 0, t]
        dk_s[at, :] = jnp.zeros((tile, hd), F32)
        dv_s[at, :] = jnp.zeros((tile, hd), F32)
        return carry

    lax.fori_loop(0, count, prepare, 0, unroll=8)

    def visit(b, carry):
        mine = rows(b)
        q_b = q_s[mine, :]
        o_b = o_s[mine, :]
        near = [rows(lists[g * count + b, n] - g * count) for n in range(KNB)]
        keys = jnp.concatenate([k_s[at, :] for at in near], 0)
        keys_t = jnp.concatenate([kt_s[:, at] for at in near], 1)
        vals = jnp.concatenate([v_s[at, :] for at in near], 0)
        e = jnp.exp2(mm(keys, q_b, NT) * (score_scale * LOG2E))
        prob = e * (1.0 / jnp.sum(e, 0, keepdims=True))
        slope = mm(vals, o_b, NT)
        centre = jnp.sum(prob * slope, 0, keepdims=True)
        shaped = (prob * (slope - centre)).astype(BF16)
        rounded = prob.astype(BF16)
        dq_s[:, mine] = mm(keys_t, shaped)
        dk = mm(shaped, q_b)
        dv = mm(rounded, o_b)
        for n, at in enumerate(near):
            dk_s[at, :] += dk[n * tile : (n + 1) * tile, :]
            dv_s[at, :] += dv[n * tile : (n + 1) * tile, :]
        return carry

    lax.fori_loop(0, count, visit, 0, unroll=8)

    @pl.when(first)
    def _():
        a1_s[...] = jnp.zeros_like(a1_s)
        a2_s[...] = jnp.zeros_like(a2_s)

    def finish(b, carry):
        at = rows(b)
        m1 = a1_s[at, :]
        m2 = a2_s[at, :]
        for i, (raw, gain, keep, grad, vec) in enumerate(
            (
                (pq, qg, iq_s, jnp.transpose(dq_s[:, at]), wq),
                (pk, kg, ik_s, dk_s[at, :], wk),
                (pv, None, None, dv_s[at, :], wv),
            )
        ):
            r = raw[at, :]
            out = grad
            if gain is not None:
                inv = keep[at, :]
                u = grad * (gain[...] * score_scale)
                out = inv * (u - r * (inv * inv * jnp.mean(r * u, -1, keepdims=True)))
            out = out.astype(BF16)
            mixed[i, at, :] = out
            out = out.astype(F32)
            m1 = m1 + out * (vec[0:1, :] + vec[1:2, :])
            m2 = m2 + out * (r - (vec[2:3, :] + vec[3:4, :]))
        a1_s[at, :] = m1
        a2_s[at, :] = m2
        return carry

    lax.fori_loop(0, count, finish, 0, unroll=8)

    @pl.when(last)
    def _():
        for n, total in enumerate((a1_s, a2_s)):
            for b in range(count):
                at = slice(b * tile, (b + 1) * tile)
                row = jnp.sum(jnp.transpose(total[at, :]), axis=0, keepdims=True)
                means[n, :, at] = jnp.broadcast_to(row, (8, tile))


def attention(ids, lists, proj, og, q_gain, k_gain, wv):
    tokens, columns = proj.shape
    hd = q_gain.shape[-1]
    heads = columns // 3 // hd
    pick = lambda i: pl.BlockSpec((tokens, hd), lambda h, *_: (0, i * heads + h))
    vec = lambda i: pl.BlockSpec((8, hd), lambda h, *_: (0, i * heads + h))
    gain = pl.BlockSpec((1, hd), lambda h, *_: (0, 0))
    return pl.pallas_call(
        attention_kernel,
        grid_spec=pltpu.PrefetchScalarGridSpec(
            num_scalar_prefetch=2,
            grid=(heads,),
            in_specs=[
                pick(0),
                pick(1),
                pick(2),
                pl.BlockSpec((4, 1) + og.shape[2:], lambda h, *_: (0, h, 0, 0, 0)),
                gain,
                gain,
                vec(0),
                vec(1),
                vec(2),
            ],
            out_specs=[
                pl.BlockSpec((3, tokens, hd), lambda h, *_: (0, 0, h)),
                pl.BlockSpec((2, 8, tokens), lambda h, *_: (0, 0, 0)),
            ],
            scratch_shapes=[pltpu.VMEM((tokens, hd), BF16)] * 4
            + [pltpu.VMEM((hd, tokens), BF16)]
            + [pltpu.VMEM((tokens, 1), F32)] * 2
            + [pltpu.VMEM((hd, tokens), F32)]
            + [pltpu.VMEM((tokens, hd), F32)] * 4,
        ),
        out_shape=[
            jax.ShapeDtypeStruct((3, tokens, heads * hd), BF16),
            jax.ShapeDtypeStruct((2, 8, tokens), F32),
        ],
        compiler_params=pltpu.CompilerParams(vmem_limit_bytes=48 * 2**20),
        cost_estimate=pl.CostEstimate(
            flops=10 * tokens * 512 * hd * heads, bytes_accessed=10 * 2**20, transcendentals=tokens * 512 * heads
        ),
        name="attention",
    )(ids, lists, proj, proj, proj, og, q_gain, k_gain, wv, wv, wv)


def weight_kernel(ids, hid, mixed, *outs):
    rows, hd = outs[0].shape[2:]
    block = 4 * rows
    x = ids[1] // 4
    for k in range(4):
        at = pl.ds(pl.multiple_of((x + k) % 4 * block, block), block)
        mine = hid[at, :]
        for i in range(3):
            part = mm(mine, mixed[i]).astype(BF16)
            for n in range(3):
                for z in range(4):
                    outs[k][z, 3 * i + n] = part[z * rows : (z + 1) * rows, n * hd : (n + 1) * hd]


def weight_part(ids, hid, mixed, hd):
    share, tokens = hid.shape
    third = mixed.shape[2]
    out = jax.ShapeDtypeStruct((4, 3 * third // hd, share // 16, hd), BF16)
    vmem = pl.BlockSpec(memory_space=pltpu.VMEM)
    return pl.pallas_call(
        weight_kernel,
        in_specs=[pl.BlockSpec(memory_space=pltpu.SMEM), vmem, vmem],
        out_specs=[vmem] * 4,
        out_shape=[out] * 4,
        compiler_params=pltpu.CompilerParams(vmem_limit_bytes=40 * 2**20),
        cost_estimate=pl.CostEstimate(
            flops=2 * share * tokens * 3 * third, bytes_accessed=6 * 2**20, transcendentals=0
        ),
        name="weight_part",
    )(ids, hid, mixed)


def stem_kernel(ids, w9, mixed, nrm, sc, means, inv, pext, own, *rest):
    others, (mixed_t,) = rest[:3], rest[3:]
    third = mixed.shape[2]
    block, tokens = nrm.shape
    count, _, _, _, hd = w9.shape
    w = jnp.concatenate([w9[n, :, 0].reshape(block, hd) for n in range(count)], 1)

    @pl.when(pl.program_id(0) == 0)
    def _():
        for i in range(3):
            mixed_t[i * third : (i + 1) * third, :] = jnp.transpose(mixed[i])

    fg = mm(w, mixed_t[...])
    n = nrm[...].astype(F32)
    scale = 1.0 / (4 * 4 * block)
    m1 = means[0, 0:1, :] * scale
    m2 = means[1, 0:1, :] * scale
    eg = (fg * jnp.concatenate([sc[...]] * (tokens // 128), 1) - m1 - n * m2) * inv[0:1, :]
    hi, lo = split2(eg)
    grad = mm(hi, pext[...], NT) + mm(lo, pext[...], NT)
    shift_grad = jnp.sum(fg, -1, keepdims=True)
    scale_grad = jnp.sum(fg * n, -1, keepdims=True)
    lane = lax.broadcasted_iota(jnp.int32, grad.shape, 1)
    grad = jnp.where(lane == 193, shift_grad, grad)
    grad = jnp.where(lane == 194, scale_grad, grad)
    for k, out in enumerate((own,) + others):

        @pl.when(pl.program_id(0) == k)
        def _():
            out[...] = grad.astype(out.dtype)


def stem_part(ids, w9, mixed, nrm, sc, means, inv, pext):
    share, tokens = nrm.shape
    block = share // 4
    count, width, hd = w9.shape
    w9 = w9.reshape(count, 16, 4, share // 16, hd)
    rows = lambda i, ids: ((i + ids[2]) % 4, 0)
    once = pl.Buffered(1)
    shape = (block, 256)
    return pl.pallas_call(
        stem_kernel,
        grid_spec=pltpu.PrefetchScalarGridSpec(
            num_scalar_prefetch=1,
            grid=(4,),
            in_specs=[
                pl.BlockSpec((count, 4, 1, share // 16, hd), lambda i, ids: (0, (i + ids[2]) % 4, ids[0], 0, 0)),
                pl.BlockSpec(mixed.shape, lambda i, ids: (0, 0, 0), pipeline_mode=once),
                pl.BlockSpec((block, tokens), rows),
                pl.BlockSpec((block, 128), rows),
                pl.BlockSpec(means.shape, lambda i, ids: (0, 0, 0), pipeline_mode=once),
                pl.BlockSpec(inv.shape, lambda i, ids: (0, 0), pipeline_mode=once),
                pl.BlockSpec(pext.shape, lambda i, ids: (0, 0), pipeline_mode=once),
            ],
            out_specs=[pl.BlockSpec(shape, lambda i, ids: (0, 0))] * 4,
            scratch_shapes=[pltpu.VMEM((count * hd, tokens), BF16)],
        ),
        out_shape=[jax.ShapeDtypeStruct(shape, F32)] + [jax.ShapeDtypeStruct(shape, BF16)] * 3,
        compiler_params=pltpu.CompilerParams(vmem_limit_bytes=40 * 2**20),
        cost_estimate=pl.CostEstimate(
            flops=1000, bytes_accessed=1000, transcendentals=0
        ),
        name="stem_part",
    )(ids, w9, mixed, nrm, sc, means, inv, pext)


def per_device(
    latent,
    stem_weight,
    stem_bias,
    mod_shift,
    mod_scale,
    qkv_weight,
    q_gain,
    k_gain,
    tile_lists,
    out_grad,
):
    width = qkv_weight.shape[0]
    heads, hd = qkv_weight.shape[2:]
    columns = 3 * heads * hd
    channels = latent.shape[1]
    seq = lax.axis_size("seq")
    groups = seq // 4
    rows = width // seq
    s = lax.axis_index("seq")
    h = lax.axis_index("head")
    g, j = s // 4, s % 4
    half_rows = HG // 2
    tr, tc = half_rows // TS, WG // TS
    tiles = tr * tc
    cell = TS * TS

    def xor(value, mask):
        return lax.ppermute(value, "seq", [(a, a ^ mask) for a in range(seq)])

    is_low = s % 2 == 0
    even = j < 2
    piece = latent.reshape(channels, tr, TS, 2, tc, TS, 2)
    piece = jnp.transpose(piece, (0, 3, 6, 1, 4, 2, 5)).reshape(4 * channels, tiles * cell)
    border = [(a, a - 2 if a % 4 < 2 else a + 2) for a in range(seq)]
    outer = lax.ppermute(piece, "seq", [(a, b) for a, b in border if 0 <= b < seq])
    pair = jnp.stack([outer, piece])
    facing = xor(pair, 2)
    window = jnp.stack(
        [
            jnp.where(even, outer, facing[0]),
            jnp.where(even, piece, facing[1]),
            jnp.where(even, facing[1], piece),
            jnp.where(even, facing[0], outer),
        ]
    )
    grads = jnp.transpose(out_grad, (1, 0, 2)).reshape(heads, tr, TS, tc, TS, hd)
    grads = jnp.transpose(grads, (0, 1, 3, 2, 4, 5)).reshape(heads, tiles, cell, hd)
    grads = jnp.stack([grads, xor(grads, 1)])
    other = xor(window, 1)
    other, grads = lax.optimization_barrier((other, grads))
    grads = jnp.concatenate([grads, xor(grads, 2)])
    window = jnp.concatenate([jnp.where(is_low, window, other), jnp.where(is_low, other, window)], 2)
    fill = jnp.zeros((256 - 12 * channels, 2 * tiles * cell), BF16).at[:3].set(1)
    pext = jnp.stack(
        [
            jnp.concatenate([window[k], window[k + 1], window[k + 2], fill], 0).reshape(
                256, 2 * tiles, cell
            )
            for k in range(2)
        ],
        2,
    ).reshape(256, 4 * tiles * cell)

    w9 = jnp.transpose(qkv_weight, (1, 2, 0, 3)).reshape(3 * heads, width, hd)
    ids = jnp.stack([j, g, h]).astype(jnp.int32)

    proj, hid, nrm, inv, wv, sc = forward(
        ids, pext, stem_weight, stem_bias[None], mod_scale[None], mod_shift[None], w9
    )
    mixed, means = attention(ids, tile_lists, proj, grads, q_gain[None], k_gain[None], wv)
    weight = list(weight_part(ids, hid, mixed, hd))
    stem = stem_part(ids, w9, mixed, nrm, sc, means, inv, pext)

    for k in range(1, 4):
        pairs = [(a, (a + 16 * k) % seq) for a in range(seq)]
        weight[k] = lax.ppermute(weight[k], "seq", pairs)

    total = stem[0]
    count = lax.axis_size("head")
    for k in range(1, count):
        pairs = [(a, (a + k) % count) for a in range(count)]
        total = total + lax.ppermute(stem[k], "head", pairs).astype(F32)

    def pair_sum(value, mask):
        held = lax.reduce_precision(value, 8, 7)
        return held + xor(held.astype(BF16), mask).astype(F32)

    def half_sum(value, mask):
        side = s // mask % 2
        half = value.shape[0] // 2
        kept = lax.dynamic_slice_in_dim(value, side * half, half, 0)
        sent = lax.dynamic_slice_in_dim(value, (1 - side) * half, half, 0)
        return kept + xor(sent.astype(BF16), mask).astype(F32)

    total, weight[1], weight[2] = lax.optimization_barrier((total, weight[1], weight[2]))
    total = pair_sum(pair_sum(total, 4), 8)
    total, weight[3] = lax.optimization_barrier((total, weight[3]))
    weight_total = sum(part.astype(F32) for part in weight)
    weight_grad = half_sum(half_sum(weight_total, 8), 4)[0]
    weight_grad = jnp.transpose(weight_grad.reshape(3, heads, rows, hd), (2, 0, 1, 3))
    for mask in (16, 32):
        total = pair_sum(total, mask)
    full = total.astype(BF16)[None]
    for mask in (1, 2):
        other = xor(full, mask)
        low = (s // mask) % 2 == 0
        full = jnp.concatenate([jnp.where(low, full, other), jnp.where(low, other, full)])
    full = full.reshape(4, groups // 4, rows, 256)
    full = jnp.transpose(full, (1, 0, 2, 3)).reshape(width // 4, 256).T.astype(F32)
    base = 12 * channels
    stem_grad = full[:base]
    vector_grad = jnp.stack([full[base + 1], full[base + 2], full[base]])
    return (weight_grad, stem_grad, vector_grad)


def solution(mesh):
    return jax.shard_map(
        per_device,
        mesh=mesh,
        in_specs=(
            P("seq", None, None),
            P(),
            P(),
            P(),
            P(),
            P(None, None, "head", None),
            P(),
            P(),
            P(),
            P("seq", "head", None),
        ),
        out_specs=(P("seq", None, "head", None), P(None, "head"), P(None, "head")),
        check_vma=False,
    )
```

```python
import functools

import jax
import jax.numpy as jnp
from jax import lax
from jax.experimental import pallas as pl
from jax.experimental.pallas import tpu as pltpu
from jax.sharding import PartitionSpec as P

TT = 2
TS = 8
KNB = 4
HG = 32
WG = 16

ln_eps = 1e-06
LOG2E = 1.4426950408889634
F32 = jnp.float32
BF16 = jnp.bfloat16

NN = (((1,), (0,)), ((), ()))
NT = (((1,), (1,)), ((), ()))
TN = (((0,), (0,)), ((), ()))


def mm(a, b, dims=NN):
    return lax.dot_general(a, b, dims, preferred_element_type=F32)


def split2(v):
    hi = v.astype(BF16)
    return hi, (v - hi.astype(F32)).astype(BF16)


def split3(v):
    hi = v.astype(BF16)
    return (hi,) + split2(v - hi.astype(F32))


BLOCK = 512


def forward_kernel(
    ids, pext, stem, bias, scale, shift, w9, proj, hid, nrm, inv_out, wv, scale_out, emb, hid_all, sw, w, sc, sh, sems
):
    width, block = emb.shape
    share = hid.shape[0]
    rows = share // 16
    pin = stem.shape[0]
    hd = w9.shape[2]
    j = ids[0]
    first = pl.program_id(0) == 0
    copies = [
        pltpu.make_async_copy(w9.at[n], w.at[:, n * hd : (n + 1) * hd], sems.at[n]) for n in range(w9.shape[0])
    ]

    @pl.when(first)
    def _():
        for copy in copies:
            copy.start()
        row = lax.broadcasted_iota(jnp.int32, (256 - pin, width), 0)
        parts = split3(bias[...])
        fill = jnp.zeros((256 - pin, width), F32)
        for n in range(3):
            fill = jnp.where(row == n, parts[n].astype(F32), fill)
        sw[0:pin, :] = stem[...]
        sw[pin:256, :] = fill.astype(BF16)
        ones = jnp.ones((8, 128), BF16)
        row = lax.broadcasted_iota(jnp.int32, (8, width), 0)
        for value, column in ((1.0 + scale[...], sc), (shift[...], sh)):
            parts = split3(value)
            fill = jnp.zeros((8, width), F32)
            for n in range(3):
                fill = jnp.where(row == n, parts[n].astype(F32), fill)
            column[...] = mm(fill.astype(BF16), ones, TN)
        for g in range(16):
            at = pl.ds(pl.multiple_of(4 * rows * g + rows * j, 16), rows)
            scale_out[g * rows : (g + 1) * rows, :] = sc[at, :]

    step = width // 4
    for n in range(4):
        emb[n * step : (n + 1) * step, :] = mm(sw[:, n * step : (n + 1) * step], pext[...], TN)
    chunk = 64

    def add(i, acc):
        x = emb[pl.ds(pl.multiple_of(i * chunk, chunk), chunk), :]
        return acc + jnp.sum(x.reshape(chunk // 8, 8, block), axis=0)

    total = lax.fori_loop(0, width // chunk, add, jnp.zeros((8, block), F32), unroll=2)
    mu = jnp.sum(total, axis=0, keepdims=True) * (1.0 / width)

    def add_squares(i, acc):
        x = emb[pl.ds(pl.multiple_of(i * chunk, chunk), chunk), :] - mu
        return acc + jnp.sum((x * x).reshape(chunk // 8, 8, block), axis=0)

    total = lax.fori_loop(0, width // chunk, add_squares, jnp.zeros((8, block), F32), unroll=2)
    inv = lax.rsqrt(jnp.sum(total, axis=0, keepdims=True) * (1.0 / width) + ln_eps)
    inv_out[...] = jnp.broadcast_to(inv, (8, block))

    def normalise(i, carry):
        at = pl.ds(pl.multiple_of(i * chunk, chunk), chunk)
        n = (emb[at, :] - mu) * inv
        emb[at, :] = n
        wide = lambda ref: jnp.concatenate([ref[at, :]] * (block // 128), 1)
        hid_all[at, :] = (n * wide(sc) + wide(sh)).astype(BF16)
        return carry

    lax.fori_loop(0, width // chunk, normalise, 0, unroll=2)
    for g in range(16):
        at = pl.ds(pl.multiple_of(4 * rows * g + rows * j, 16), rows)
        hid[g * rows : (g + 1) * rows, :] = hid_all[at, :]
        nrm[g * rows : (g + 1) * rows, :] = emb[at, :].astype(BF16)

    @pl.when(first)
    def _():
        for copy in copies:
            copy.wait()
        row = lax.broadcasted_iota(jnp.int32, (8, width), 0)
        fill = jnp.zeros((8, width), F32)
        for n, part in enumerate(split2(1.0 + scale[...]) + split2(shift[...])):
            fill = jnp.where(row == n, part.astype(F32), fill)
        wv[...] = mm(fill.astype(BF16), w[...])

    proj[...] = mm(hid_all[...], w[...], TN)


def forward(ids, pext, stem, bias, scale, shift, w9, block=BLOCK):
    tokens = pext.shape[1]
    count, width, hd = w9.shape
    columns = count * hd
    share = width // 4
    whole = lambda i, ids: (0, 0)
    rows = lambda i, ids: (i, 0)
    lanes = lambda i, ids: (0, i)
    once = pl.Buffered(1)
    vec = pl.BlockSpec((1, width), whole, pipeline_mode=once)
    return pl.pallas_call(
        forward_kernel,
        grid_spec=pltpu.PrefetchScalarGridSpec(
            num_scalar_prefetch=1,
            grid=(tokens // block,),
            in_specs=[
                pl.BlockSpec((256, block), lanes),
                pl.BlockSpec(stem.shape, whole, pipeline_mode=once),
                vec,
                vec,
                vec,
                pl.BlockSpec(memory_space=pl.ANY),
            ],
            out_specs=[
                pl.BlockSpec((block, columns), rows),
                pl.BlockSpec((share, block), lanes),
                pl.BlockSpec((share, block), lanes),
                pl.BlockSpec((8, block), lanes),
                pl.BlockSpec((8, columns), whole),
                pl.BlockSpec((share, 128), whole),
            ],
            scratch_shapes=[
                pltpu.VMEM((width, block), F32),
                pltpu.VMEM((width, block), BF16),
                pltpu.VMEM((256, width), BF16),
                pltpu.VMEM((width, columns), BF16),
                pltpu.VMEM((width, 128), F32),
                pltpu.VMEM((width, 128), F32),
                pltpu.SemaphoreType.DMA((count,)),
            ],
        ),
        out_shape=[
            jax.ShapeDtypeStruct((tokens, columns), F32),
            jax.ShapeDtypeStruct((share, tokens), BF16),
            jax.ShapeDtypeStruct((share, tokens), BF16),
            jax.ShapeDtypeStruct((8, tokens), F32),
            jax.ShapeDtypeStruct((8, columns), F32),
            jax.ShapeDtypeStruct((share, 128), F32),
        ],
        compiler_params=pltpu.CompilerParams(vmem_limit_bytes=60 * 2**20),
        cost_estimate=pl.CostEstimate(
            flops=2 * tokens * width * (columns + 256), bytes_accessed=24 * 2**20, transcendentals=0
        ),
        name="forward",
    )(ids, pext, stem, bias, scale, shift, w9)


def attention_kernel(
    ids,
    lists,
    pq,
    pk,
    pv,
    og,
    qg,
    kg,
    wq,
    wk,
    wv,
    mixed,
    means,
    q_s,
    k_s,
    v_s,
    o_s,
    kt_s,
    iq_s,
    ik_s,
    dq_s,
    dk_s,
    dv_s,
    a1_s,
    a2_s,
):
    tokens, hd = pq.shape
    score_scale = hd ** (-0.5)
    j, g = ids[0], ids[1]
    tile = TT * TS * TS
    count = tokens // tile
    frame_tile = TS * TS
    first = pl.program_id(0) == 0
    last = pl.program_id(0) == pl.num_programs(0) - 1

    def rows(b):
        return pl.ds(pl.multiple_of(b * tile, tile), tile)

    def prepare(b, carry):
        at = rows(b)
        for raw, gain, keep, store in ((pq, qg, iq_s, q_s), (pk, kg, ik_s, k_s)):
            r = raw[at, :]
            inv = lax.rsqrt(jnp.mean(r * r, -1, keepdims=True) + ln_eps)
            keep[at, :] = inv
            value = r * inv * gain[...]
            store[at, :] = value.astype(BF16)
        kt_s[:, at] = jnp.transpose(value).astype(BF16)
        v_s[at, :] = pv[at, :].astype(BF16)
        half, t = b // (count // 2), b % (count // 2)
        for frame in range(2):
            to = pl.ds(pl.multiple_of(b * tile + frame * frame_tile, frame_tile), frame_tile)
            o_s[to, :] = og[jnp.bitwise_xor(j, 2 * frame + half), 0, t]
        dk_s[at, :] = jnp.zeros((tile, hd), F32)
        dv_s[at, :] = jnp.zeros((tile, hd), F32)
        return carry

    lax.fori_loop(0, count, prepare, 0, unroll=8)

    def visit(b, carry):
        mine = rows(b)
        q_b = q_s[mine, :]
        o_b = o_s[mine, :]
        near = [rows(lists[g * count + b, n] - g * count) for n in range(KNB)]
        keys = jnp.concatenate([k_s[at, :] for at in near], 0)
        keys_t = jnp.concatenate([kt_s[:, at] for at in near], 1)
        vals = jnp.concatenate([v_s[at, :] for at in near], 0)
        e = jnp.exp2(mm(keys, q_b, NT) * (score_scale * LOG2E))
        prob = e * (1.0 / jnp.sum(e, 0, keepdims=True))
        slope = mm(vals, o_b, NT)
        centre = jnp.sum(prob * slope, 0, keepdims=True)
        shaped = (prob * (slope - centre)).astype(BF16)
        rounded = prob.astype(BF16)
        dq_s[:, mine] = mm(keys_t, shaped)
        dk = mm(shaped, q_b)
        dv = mm(rounded, o_b)
        for n, at in enumerate(near):
            dk_s[at, :] += dk[n * tile : (n + 1) * tile, :]
            dv_s[at, :] += dv[n * tile : (n + 1) * tile, :]
        return carry

    lax.fori_loop(0, count, visit, 0, unroll=8)

    @pl.when(first)
    def _():
        a1_s[...] = jnp.zeros_like(a1_s)
        a2_s[...] = jnp.zeros_like(a2_s)

    def finish(b, carry):
        at = rows(b)
        m1 = a1_s[at, :]
        m2 = a2_s[at, :]
        for i, (raw, gain, keep, grad, vec) in enumerate(
            (
                (pq, qg, iq_s, jnp.transpose(dq_s[:, at]), wq),
                (pk, kg, ik_s, dk_s[at, :], wk),
                (pv, None, None, dv_s[at, :], wv),
            )
        ):
            r = raw[at, :]
            out = grad
            if gain is not None:
                inv = keep[at, :]
                u = grad * (gain[...] * score_scale)
                out = inv * (u - r * (inv * inv * jnp.mean(r * u, -1, keepdims=True)))
            out = out.astype(BF16)
            mixed[i, at, :] = out
            out = out.astype(F32)
            m1 = m1 + out * (vec[0:1, :] + vec[1:2, :])
            m2 = m2 + out * (r - (vec[2:3, :] + vec[3:4, :]))
        a1_s[at, :] = m1
        a2_s[at, :] = m2
        return carry

    lax.fori_loop(0, count, finish, 0, unroll=8)

    @pl.when(last)
    def _():
        for n, total in enumerate((a1_s, a2_s)):
            for b in range(count):
                at = slice(b * tile, (b + 1) * tile)
                row = jnp.sum(jnp.transpose(total[at, :]), axis=0, keepdims=True)
                means[n, :, at] = jnp.broadcast_to(row, (8, tile))


def attention(ids, lists, proj, og, q_gain, k_gain, wv):
    tokens, columns = proj.shape
    hd = q_gain.shape[-1]
    heads = columns // 3 // hd
    pick = lambda i: pl.BlockSpec((tokens, hd), lambda h, *_: (0, i * heads + h))
    vec = lambda i: pl.BlockSpec((8, hd), lambda h, *_: (0, i * heads + h))
    gain = pl.BlockSpec((1, hd), lambda h, *_: (0, 0))
    return pl.pallas_call(
        attention_kernel,
        grid_spec=pltpu.PrefetchScalarGridSpec(
            num_scalar_prefetch=2,
            grid=(heads,),
            in_specs=[
                pick(0),
                pick(1),
                pick(2),
                pl.BlockSpec((4, 1) + og.shape[2:], lambda h, *_: (0, h, 0, 0, 0)),
                gain,
                gain,
                vec(0),
                vec(1),
                vec(2),
            ],
            out_specs=[
                pl.BlockSpec((3, tokens, hd), lambda h, *_: (0, 0, h)),
                pl.BlockSpec((2, 8, tokens), lambda h, *_: (0, 0, 0)),
            ],
            scratch_shapes=[pltpu.VMEM((tokens, hd), BF16)] * 4
            + [pltpu.VMEM((hd, tokens), BF16)]
            + [pltpu.VMEM((tokens, 1), F32)] * 2
            + [pltpu.VMEM((hd, tokens), F32)]
            + [pltpu.VMEM((tokens, hd), F32)] * 4,
        ),
        out_shape=[
            jax.ShapeDtypeStruct((3, tokens, heads * hd), BF16),
            jax.ShapeDtypeStruct((2, 8, tokens), F32),
        ],
        compiler_params=pltpu.CompilerParams(vmem_limit_bytes=48 * 2**20),
        cost_estimate=pl.CostEstimate(
            flops=10 * tokens * 512 * hd * heads, bytes_accessed=10 * 2**20, transcendentals=tokens * 512 * heads
        ),
        name="attention",
    )(ids, lists, proj, proj, proj, og, q_gain, k_gain, wv, wv, wv)


def weight_kernel(ids, hid, mixed, *outs):
    rows, hd = outs[0].shape[2:]
    block = 4 * rows
    x = ids[1] // 4
    for k in range(4):
        at = pl.ds(pl.multiple_of((x + k) % 4 * block, block), block)
        mine = hid[at, :]
        for i in range(3):
            part = mm(mine, mixed[i]).astype(BF16)
            for n in range(3):
                for z in range(4):
                    outs[k][z, 3 * i + n] = part[z * rows : (z + 1) * rows, n * hd : (n + 1) * hd]


def weight_part(ids, hid, mixed, hd):
    share, tokens = hid.shape
    third = mixed.shape[2]
    out = jax.ShapeDtypeStruct((4, 3 * third // hd, share // 16, hd), BF16)
    vmem = pl.BlockSpec(memory_space=pltpu.VMEM)
    return pl.pallas_call(
        weight_kernel,
        in_specs=[pl.BlockSpec(memory_space=pltpu.SMEM), vmem, vmem],
        out_specs=[vmem] * 4,
        out_shape=[out] * 4,
        compiler_params=pltpu.CompilerParams(vmem_limit_bytes=40 * 2**20),
        cost_estimate=pl.CostEstimate(
            flops=2 * share * tokens * 3 * third, bytes_accessed=6 * 2**20, transcendentals=0
        ),
        name="weight_part",
    )(ids, hid, mixed)


def stem_kernel(ids, w9, mixed, nrm, sc, means, inv, pext, own, *rest):
    others, (mixed_t,) = rest[:3], rest[3:]
    third = mixed.shape[2]
    block, tokens = nrm.shape
    count, _, _, _, hd = w9.shape
    w = jnp.concatenate([w9[n, :, 0].reshape(block, hd) for n in range(count)], 1)

    @pl.when(pl.program_id(0) == 0)
    def _():
        for i in range(3):
            mixed_t[i * third : (i + 1) * third, :] = jnp.transpose(mixed[i])

    fg = mm(w, mixed_t[...])
    n = nrm[...].astype(F32)
    scale = 1.0 / (4 * 4 * block)
    m1 = means[0, 0:1, :] * scale
    m2 = means[1, 0:1, :] * scale
    eg = (fg * jnp.concatenate([sc[...]] * (tokens // 128), 1) - m1 - n * m2) * inv[0:1, :]
    hi, lo = split2(eg)
    grad = mm(hi, pext[...], NT) + mm(lo, pext[...], NT)
    shift_grad = jnp.sum(fg, -1, keepdims=True)
    scale_grad = jnp.sum(fg * n, -1, keepdims=True)
    lane = lax.broadcasted_iota(jnp.int32, grad.shape, 1)
    grad = jnp.where(lane == 193, shift_grad, grad)
    grad = jnp.where(lane == 194, scale_grad, grad)
    for k, out in enumerate((own,) + others):

        @pl.when(pl.program_id(0) == k)
        def _():
            out[...] = grad.astype(out.dtype)


def stem_part(ids, w9, mixed, nrm, sc, means, inv, pext):
    share, tokens = nrm.shape
    block = share // 4
    count, width, hd = w9.shape
    w9 = w9.reshape(count, 16, 4, share // 16, hd)
    rows = lambda i, ids: ((i + ids[2]) % 4, 0)
    once = pl.Buffered(1)
    shape = (block, 256)
    return pl.pallas_call(
        stem_kernel,
        grid_spec=pltpu.PrefetchScalarGridSpec(
            num_scalar_prefetch=1,
            grid=(4,),
            in_specs=[
                pl.BlockSpec((count, 4, 1, share // 16, hd), lambda i, ids: (0, (i + ids[2]) % 4, ids[0], 0, 0)),
                pl.BlockSpec(mixed.shape, lambda i, ids: (0, 0, 0), pipeline_mode=once),
                pl.BlockSpec((block, tokens), rows),
                pl.BlockSpec((block, 128), rows),
                pl.BlockSpec(means.shape, lambda i, ids: (0, 0, 0), pipeline_mode=once),
                pl.BlockSpec(inv.shape, lambda i, ids: (0, 0), pipeline_mode=once),
                pl.BlockSpec(pext.shape, lambda i, ids: (0, 0), pipeline_mode=once),
            ],
            out_specs=[pl.BlockSpec(shape, lambda i, ids: (0, 0))] * 4,
            scratch_shapes=[pltpu.VMEM((count * hd, tokens), BF16)],
        ),
        out_shape=[jax.ShapeDtypeStruct(shape, F32)] + [jax.ShapeDtypeStruct(shape, BF16)] * 3,
        compiler_params=pltpu.CompilerParams(vmem_limit_bytes=40 * 2**20),
        cost_estimate=pl.CostEstimate(
            flops=1000, bytes_accessed=1000, transcendentals=0
        ),
        name="stem_part",
    )(ids, w9, mixed, nrm, sc, means, inv, pext)


def per_device(
    latent,
    stem_weight,
    stem_bias,
    mod_shift,
    mod_scale,
    qkv_weight,
    q_gain,
    k_gain,
    tile_lists,
    out_grad,
):
    width = qkv_weight.shape[0]
    heads, hd = qkv_weight.shape[2:]
    columns = 3 * heads * hd
    channels = latent.shape[1]
    seq = lax.axis_size("seq")
    groups = seq // 4
    rows = width // seq
    s = lax.axis_index("seq")
    h = lax.axis_index("head")
    g, j = s // 4, s % 4
    half_rows = HG // 2
    tr, tc = half_rows // TS, WG // TS
    tiles = tr * tc
    cell = TS * TS

    def xor(value, mask):
        return lax.ppermute(value, "seq", [(a, a ^ mask) for a in range(seq)])

    is_low = s % 2 == 0
    even = j < 2
    piece = latent.reshape(channels, tr, TS, 2, tc, TS, 2)
    piece = jnp.transpose(piece, (0, 3, 6, 1, 4, 2, 5)).reshape(4 * channels, tiles * cell)
    border = [(a, a - 2 if a % 4 < 2 else a + 2) for a in range(seq)]
    outer = lax.ppermute(piece, "seq", [(a, b) for a, b in border if 0 <= b < seq])
    pair = jnp.stack([outer, piece])
    facing = xor(pair, 2)
    window = jnp.stack(
        [
            jnp.where(even, outer, facing[0]),
            jnp.where(even, piece, facing[1]),
            jnp.where(even, facing[1], piece),
            jnp.where(even, facing[0], outer),
        ]
    )
    grads = jnp.transpose(out_grad, (1, 0, 2)).reshape(heads, tr, TS, tc, TS, hd)
    grads = jnp.transpose(grads, (0, 1, 3, 2, 4, 5)).reshape(heads, tiles, cell, hd)
    grads = jnp.stack([grads, xor(grads, 1)])
    other = xor(window, 1)
    other, grads = lax.optimization_barrier((other, grads))
    grads = jnp.concatenate([grads, xor(grads, 2)])
    window = jnp.concatenate([jnp.where(is_low, window, other), jnp.where(is_low, other, window)], 2)
    fill = jnp.zeros((256 - 12 * channels, 2 * tiles * cell), BF16).at[:3].set(1)
    pext = jnp.stack(
        [
            jnp.concatenate([window[k], window[k + 1], window[k + 2], fill], 0).reshape(
                256, 2 * tiles, cell
            )
            for k in range(2)
        ],
        2,
    ).reshape(256, 4 * tiles * cell)

    w9 = jnp.transpose(qkv_weight, (1, 2, 0, 3)).reshape(3 * heads, width, hd)
    ids = jnp.stack([j, g, h]).astype(jnp.int32)

    proj, hid, nrm, inv, wv, sc = forward(
        ids, pext, stem_weight, stem_bias[None], mod_scale[None], mod_shift[None], w9
    )
    mixed, means = attention(ids, tile_lists, proj, grads, q_gain[None], k_gain[None], wv)
    weight = list(weight_part(ids, hid, mixed, hd))
    stem = stem_part(ids, w9, mixed, nrm, sc, means, inv, pext)

    for k in range(1, 4):
        pairs = [(a, (a + 16 * k) % seq) for a in range(seq)]
        weight[k] = lax.ppermute(weight[k], "seq", pairs)

    total = stem[0]
    count = lax.axis_size("head")
    for k in range(1, count):
        pairs = [(a, (a + k) % count) for a in range(count)]
        total = total + lax.ppermute(stem[k], "head", pairs).astype(F32)

    def quad_sum(value, low, high):
        held = lax.reduce_precision(value, 8, 7)
        sent = held.astype(BF16)
        near, far, both = (xor(sent, mask).astype(F32) for mask in (low, high, low + high))
        return (held + near) + (far + both)

    total, weight[1], weight[2] = lax.optimization_barrier((total, weight[1], weight[2]))
    total = quad_sum(total, 4, 8)
    total, weight[3] = lax.optimization_barrier((total, weight[3]))
    weight_total = sum(part.astype(F32) for part in weight)

    zhi = g % 4
    parts = []
    for k in range(4):
        part = lax.dynamic_index_in_dim(weight_total, (zhi + k) % 4, 0, keepdims=False)
        if k > 0:
            pairs = [(a, a - a % 16 + (a + 4 * k) % 16) for a in range(seq)]
            part = lax.ppermute(part.astype(BF16), "seq", pairs)
        parts.append(part)
    total = quad_sum(total, 16, 32)
    total, parts[1], parts[2] = lax.optimization_barrier((total, parts[1], parts[2]))
    weight_grad = sum(part.astype(F32) for part in parts)
    weight_grad = jnp.transpose(weight_grad.reshape(3, heads, rows, hd), (2, 0, 1, 3))

    held = total.astype(BF16)
    found = [held] + [xor(held, mask) for mask in (1, 2, 3)]
    low, high = j % 2 == 0, j < 2
    swapped = [jnp.where(low, found[m], found[m ^ 1]) for m in range(4)]
    full = jnp.stack([jnp.where(high, swapped[m], swapped[m ^ 2]) for m in range(4)])
    full = full.reshape(4, groups // 4, rows, 256)
    full = jnp.transpose(full, (1, 0, 2, 3)).reshape(width // 4, 256).T.astype(F32)
    base = 12 * channels
    stem_grad = full[:base]
    vector_grad = jnp.stack([full[base + 1], full[base + 2], full[base]])
    return (weight_grad, stem_grad, vector_grad)


def solution(mesh):
    return jax.shard_map(
        per_device,
        mesh=mesh,
        in_specs=(
            P("seq", None, None),
            P(),
            P(),
            P(),
            P(),
            P(None, None, "head", None),
            P(),
            P(),
            P(),
            P("seq", "head", None),
        ),
        out_specs=(P("seq", None, "head", None), P(None, "head"), P(None, "head")),
        check_vma=False,
    )
```

```python
import functools

import jax
import jax.numpy as jnp
from jax import lax
from jax.experimental import pallas as pl
from jax.experimental.pallas import tpu as pltpu
from jax.sharding import PartitionSpec as P

TT = 2
TS = 8
KNB = 4
HG = 32
WG = 16

ln_eps = 1e-06
LOG2E = 1.4426950408889634
F32 = jnp.float32
BF16 = jnp.bfloat16

NN = (((1,), (0,)), ((), ()))
NT = (((1,), (1,)), ((), ()))
TN = (((0,), (0,)), ((), ()))


def mm(a, b, dims=NN):
    return lax.dot_general(a, b, dims, preferred_element_type=F32)


def split2(v):
    hi = v.astype(BF16)
    return hi, (v - hi.astype(F32)).astype(BF16)


def split3(v):
    hi = v.astype(BF16)
    return (hi,) + split2(v - hi.astype(F32))


BLOCK = 512


def forward_kernel(
    ids, pext, stem, bias, scale, shift, w9, proj, hid, nrm, inv_out, wv, scale_out, emb, hid_all, sw, w, sc, sh, px, sums, sems
):
    width, block = emb.shape
    share = hid.shape[0]
    rows = share // 16
    pin = stem.shape[0]
    hd = w9.shape[2]
    j = ids[0]
    first = pl.program_id(0) == 0
    copies = [
        pltpu.make_async_copy(w9.at[n], w.at[:, n * hd : (n + 1) * hd], sems.at[n]) for n in range(w9.shape[0])
    ]

    @pl.when(first)
    def _():
        for copy in copies:
            copy.start()
        row = lax.broadcasted_iota(jnp.int32, (256 - pin, width), 0)
        parts = split3(bias[...])
        fill = jnp.zeros((256 - pin, width), F32)
        for n in range(3):
            fill = jnp.where(row == n, parts[n].astype(F32), fill)
        fill = jnp.where((row >= 8) & (row < 11), 1.0, fill)
        sw[0:pin, :] = stem[...]
        sw[pin:256, :] = fill.astype(BF16)
        total = mm(jnp.ones((8, width), BF16), sw[...], NT) * (-1.0 / width)
        row = lax.broadcasted_iota(jnp.int32, (8, 256), 0)
        lane = lax.broadcasted_iota(jnp.int32, (8, 256), 1)
        fill = jnp.zeros((8, 256), F32)
        for n, part in enumerate(split3(total)):
            fill = jnp.where(row == n, part.astype(F32), fill)
        sums[...] = jnp.where(lane < pin + 3, fill, 0.0).astype(BF16)
        ones = jnp.ones((8, 128), BF16)
        row = lax.broadcasted_iota(jnp.int32, (8, width), 0)
        for value, column in ((1.0 + scale[...], sc), (shift[...], sh)):
            parts = split3(value)
            fill = jnp.zeros((8, width), F32)
            for n in range(3):
                fill = jnp.where(row == n, parts[n].astype(F32), fill)
            column[...] = mm(fill.astype(BF16), ones, TN)
        for g in range(16):
            at = pl.ds(pl.multiple_of(4 * rows * g + rows * j, 16), rows)
            scale_out[g * rows : (g + 1) * rows, :] = sc[at, :]

    shift_row = jnp.sum(mm(sums[...], pext[...]), axis=0, keepdims=True)
    row = lax.broadcasted_iota(jnp.int32, (256 - pin, block), 0)
    tail = pext[pin:256, :].astype(F32)
    for n, part in enumerate(split3(shift_row)):
        tail = jnp.where(row == 8 + n, part.astype(F32), tail)
    px[0:pin, :] = pext[0:pin, :]
    px[pin:256, :] = tail.astype(BF16)
    step = width // 24
    total = jnp.zeros((8, block), F32)
    for n in range(24):
        x = mm(sw[:, n * step : (n + 1) * step], px[...], TN)
        emb[n * step : (n + 1) * step, :] = x
        total = total + jnp.sum((x * x).reshape(step // 8, 8, block), axis=0)
    inv = lax.rsqrt(jnp.sum(total, axis=0, keepdims=True) * (1.0 / width) + ln_eps)
    inv_out[...] = jnp.broadcast_to(inv, (8, block))
    chunk = 64

    def normalise(i, carry):
        at = pl.ds(pl.multiple_of(i * chunk, chunk), chunk)
        wide = lambda ref: jnp.concatenate([ref[at, :]] * (block // 128), 1)
        hid_all[at, :] = (emb[at, :] * inv * wide(sc) + wide(sh)).astype(BF16)
        return carry

    lax.fori_loop(0, width // chunk, normalise, 0, unroll=4)
    for g in range(16):
        at = pl.ds(pl.multiple_of(4 * rows * g + rows * j, 16), rows)
        hid[g * rows : (g + 1) * rows, :] = hid_all[at, :]
        nrm[g * rows : (g + 1) * rows, :] = (emb[at, :] * inv).astype(BF16)

    @pl.when(first)
    def _():
        for copy in copies:
            copy.wait()
        row = lax.broadcasted_iota(jnp.int32, (8, width), 0)
        fill = jnp.zeros((8, width), F32)
        for n, part in enumerate(split2(1.0 + scale[...]) + split2(shift[...])):
            fill = jnp.where(row == n, part.astype(F32), fill)
        wv[...] = mm(fill.astype(BF16), w[...])

    proj[...] = mm(hid_all[...], w[...], TN)


def forward(ids, pext, stem, bias, scale, shift, w9, block=BLOCK):
    tokens = pext.shape[1]
    count, width, hd = w9.shape
    columns = count * hd
    share = width // 4
    whole = lambda i, ids: (0, 0)
    rows = lambda i, ids: (i, 0)
    lanes = lambda i, ids: (0, i)
    once = pl.Buffered(1)
    vec = pl.BlockSpec((1, width), whole, pipeline_mode=once)
    return pl.pallas_call(
        forward_kernel,
        grid_spec=pltpu.PrefetchScalarGridSpec(
            num_scalar_prefetch=1,
            grid=(tokens // block,),
            in_specs=[
                pl.BlockSpec((256, block), lanes),
                pl.BlockSpec(stem.shape, whole, pipeline_mode=once),
                vec,
                vec,
                vec,
                pl.BlockSpec(memory_space=pl.ANY),
            ],
            out_specs=[
                pl.BlockSpec((block, columns), rows),
                pl.BlockSpec((share, block), lanes),
                pl.BlockSpec((share, block), lanes),
                pl.BlockSpec((8, block), lanes),
                pl.BlockSpec((8, columns), whole),
                pl.BlockSpec((share, 128), whole),
            ],
            scratch_shapes=[
                pltpu.VMEM((width, block), F32),
                pltpu.VMEM((width, block), BF16),
                pltpu.VMEM((256, width), BF16),
                pltpu.VMEM((width, columns), BF16),
                pltpu.VMEM((width, 128), F32),
                pltpu.VMEM((width, 128), F32),
                pltpu.VMEM((256, block), BF16),
                pltpu.VMEM((8, 256), BF16),
                pltpu.SemaphoreType.DMA((count,)),
            ],
        ),
        out_shape=[
            jax.ShapeDtypeStruct((tokens, columns), F32),
            jax.ShapeDtypeStruct((share, tokens), BF16),
            jax.ShapeDtypeStruct((share, tokens), BF16),
            jax.ShapeDtypeStruct((8, tokens), F32),
            jax.ShapeDtypeStruct((8, columns), F32),
            jax.ShapeDtypeStruct((share, 128), F32),
        ],
        compiler_params=pltpu.CompilerParams(vmem_limit_bytes=60 * 2**20),
        cost_estimate=pl.CostEstimate(
            flops=2 * tokens * width * (columns + 256), bytes_accessed=24 * 2**20, transcendentals=0
        ),
        name="forward",
    )(ids, pext, stem, bias, scale, shift, w9)


def attention_kernel(
    ids,
    lists,
    pq,
    pk,
    pv,
    og,
    qg,
    kg,
    wq,
    wk,
    wv,
    mixed,
    means,
    q_s,
    k_s,
    v_s,
    o_s,
    kt_s,
    iq_s,
    ik_s,
    dq_s,
    dk_s,
    dv_s,
    a1_s,
    a2_s,
):
    tokens, hd = pq.shape
    score_scale = hd ** (-0.5)
    j, g = ids[0], ids[1]
    tile = TT * TS * TS
    count = tokens // tile
    frame_tile = TS * TS
    first = pl.program_id(0) == 0
    last = pl.program_id(0) == pl.num_programs(0) - 1

    def rows(b):
        return pl.ds(pl.multiple_of(b * tile, tile), tile)

    def prepare(b, carry):
        at = rows(b)
        for raw, gain, keep, store in ((pq, qg, iq_s, q_s), (pk, kg, ik_s, k_s)):
            r = raw[at, :]
            inv = lax.rsqrt(jnp.mean(r * r, -1, keepdims=True) + ln_eps)
            keep[at, :] = inv
            value = r * inv * gain[...]
            store[at, :] = value.astype(BF16)
        kt_s[:, at] = jnp.transpose(value).astype(BF16)
        v_s[at, :] = pv[at, :].astype(BF16)
        half, t = b // (count // 2), b % (count // 2)
        for frame in range(2):
            to = pl.ds(pl.multiple_of(b * tile + frame * frame_tile, frame_tile), frame_tile)
            o_s[to, :] = og[jnp.bitwise_xor(j, 2 * frame + half), 0, t]
        dk_s[at, :] = jnp.zeros((tile, hd), F32)
        dv_s[at, :] = jnp.zeros((tile, hd), F32)
        return carry

    lax.fori_loop(0, count, prepare, 0, unroll=8)

    def visit(b, carry):
        mine = rows(b)
        q_b = q_s[mine, :]
        o_b = o_s[mine, :]
        near = [rows(lists[g * count + b, n] - g * count) for n in range(KNB)]
        keys = jnp.concatenate([k_s[at, :] for at in near], 0)
        keys_t = jnp.concatenate([kt_s[:, at] for at in near], 1)
        vals = jnp.concatenate([v_s[at, :] for at in near], 0)
        e = jnp.exp2(mm(keys, q_b, NT) * (score_scale * LOG2E))
        prob = e * (1.0 / jnp.sum(e, 0, keepdims=True))
        slope = mm(vals, o_b, NT)
        centre = jnp.sum(prob * slope, 0, keepdims=True)
        shaped = (prob * (slope - centre)).astype(BF16)
        rounded = prob.astype(BF16)
        dq_s[:, mine] = mm(keys_t, shaped)
        dk = mm(shaped, q_b)
        dv = mm(rounded, o_b)
        for n, at in enumerate(near):
            dk_s[at, :] += dk[n * tile : (n + 1) * tile, :]
            dv_s[at, :] += dv[n * tile : (n + 1) * tile, :]
        return carry

    lax.fori_loop(0, count, visit, 0, unroll=8)

    @pl.when(first)
    def _():
        a1_s[...] = jnp.zeros_like(a1_s)
        a2_s[...] = jnp.zeros_like(a2_s)

    def finish(b, carry):
        at = rows(b)
        m1 = a1_s[at, :]
        m2 = a2_s[at, :]
        for i, (raw, gain, keep, grad, vec) in enumerate(
            (
                (pq, qg, iq_s, jnp.transpose(dq_s[:, at]), wq),
                (pk, kg, ik_s, dk_s[at, :], wk),
                (pv, None, None, dv_s[at, :], wv),
            )
        ):
            r = raw[at, :]
            out = grad
            if gain is not None:
                inv = keep[at, :]
                u = grad * (gain[...] * score_scale)
                out = inv * (u - r * (inv * inv * jnp.mean(r * u, -1, keepdims=True)))
            out = out.astype(BF16)
            mixed[i, at, :] = out
            out = out.astype(F32)
            m1 = m1 + out * (vec[0:1, :] + vec[1:2, :])
            m2 = m2 + out * (r - (vec[2:3, :] + vec[3:4, :]))
        a1_s[at, :] = m1
        a2_s[at, :] = m2
        return carry

    lax.fori_loop(0, count, finish, 0, unroll=8)

    @pl.when(last)
    def _():
        for n, total in enumerate((a1_s, a2_s)):
            for b in range(count):
                at = slice(b * tile, (b + 1) * tile)
                row = jnp.sum(jnp.transpose(total[at, :]), axis=0, keepdims=True)
                means[n, :, at] = jnp.broadcast_to(row, (8, tile))


def attention(ids, lists, proj, og, q_gain, k_gain, wv):
    tokens, columns = proj.shape
    hd = q_gain.shape[-1]
    heads = columns // 3 // hd
    pick = lambda i: pl.BlockSpec((tokens, hd), lambda h, *_: (0, i * heads + h))
    vec = lambda i: pl.BlockSpec((8, hd), lambda h, *_: (0, i * heads + h))
    gain = pl.BlockSpec((1, hd), lambda h, *_: (0, 0))
    return pl.pallas_call(
        attention_kernel,
        grid_spec=pltpu.PrefetchScalarGridSpec(
            num_scalar_prefetch=2,
            grid=(heads,),
            in_specs=[
                pick(0),
                pick(1),
                pick(2),
                pl.BlockSpec((4, 1) + og.shape[2:], lambda h, *_: (0, h, 0, 0, 0)),
                gain,
                gain,
                vec(0),
                vec(1),
                vec(2),
            ],
            out_specs=[
                pl.BlockSpec((3, tokens, hd), lambda h, *_: (0, 0, h)),
                pl.BlockSpec((2, 8, tokens), lambda h, *_: (0, 0, 0)),
            ],
            scratch_shapes=[pltpu.VMEM((tokens, hd), BF16)] * 4
            + [pltpu.VMEM((hd, tokens), BF16)]
            + [pltpu.VMEM((tokens, 1), F32)] * 2
            + [pltpu.VMEM((hd, tokens), F32)]
            + [pltpu.VMEM((tokens, hd), F32)] * 4,
        ),
        out_shape=[
            jax.ShapeDtypeStruct((3, tokens, heads * hd), BF16),
            jax.ShapeDtypeStruct((2, 8, tokens), F32),
        ],
        compiler_params=pltpu.CompilerParams(vmem_limit_bytes=48 * 2**20),
        cost_estimate=pl.CostEstimate(
            flops=10 * tokens * 512 * hd * heads, bytes_accessed=10 * 2**20, transcendentals=tokens * 512 * heads
        ),
        name="attention",
    )(ids, lists, proj, proj, proj, og, q_gain, k_gain, wv, wv, wv)


def weight_kernel(ids, hid, mixed, *outs):
    rows, hd = outs[0].shape[2:]
    block = 4 * rows
    x = ids[1] // 4
    for k in range(4):
        at = pl.ds(pl.multiple_of((x + k) % 4 * block, block), block)
        mine = hid[at, :]
        for i in range(3):
            part = mm(mine, mixed[i]).astype(BF16)
            for n in range(3):
                for z in range(4):
                    outs[k][z, 3 * i + n] = part[z * rows : (z + 1) * rows, n * hd : (n + 1) * hd]


def weight_part(ids, hid, mixed, hd):
    share, tokens = hid.shape
    third = mixed.shape[2]
    out = jax.ShapeDtypeStruct((4, 3 * third // hd, share // 16, hd), BF16)
    vmem = pl.BlockSpec(memory_space=pltpu.VMEM)
    return pl.pallas_call(
        weight_kernel,
        in_specs=[pl.BlockSpec(memory_space=pltpu.SMEM), vmem, vmem],
        out_specs=[vmem] * 4,
        out_shape=[out] * 4,
        compiler_params=pltpu.CompilerParams(vmem_limit_bytes=40 * 2**20),
        cost_estimate=pl.CostEstimate(
            flops=2 * share * tokens * 3 * third, bytes_accessed=6 * 2**20, transcendentals=0
        ),
        name="weight_part",
    )(ids, hid, mixed)


def stem_kernel(ids, w9, mixed, nrm, sc, means, inv, pext, own, *rest):
    others, (mixed_t,) = rest[:3], rest[3:]
    third = mixed.shape[2]
    block, tokens = nrm.shape
    count, _, _, _, hd = w9.shape
    w = jnp.concatenate([w9[n, :, 0].reshape(block, hd) for n in range(count)], 1)

    @pl.when(pl.program_id(0) == 0)
    def _():
        for i in range(3):
            mixed_t[i * third : (i + 1) * third, :] = jnp.transpose(mixed[i])

    fg = mm(w, mixed_t[...])
    n = nrm[...].astype(F32)
    scale = 1.0 / (4 * 4 * block)
    m1 = means[0, 0:1, :] * scale
    m2 = means[1, 0:1, :] * scale
    eg = (fg * jnp.concatenate([sc[...]] * (tokens // 128), 1) - m1 - n * m2) * inv[0:1, :]
    hi, lo = split2(eg)
    grad = mm(hi, pext[...], NT) + mm(lo, pext[...], NT)
    shift_grad = jnp.sum(fg, -1, keepdims=True)
    scale_grad = jnp.sum(fg * n, -1, keepdims=True)
    lane = lax.broadcasted_iota(jnp.int32, grad.shape, 1)
    grad = jnp.where(lane == 193, shift_grad, grad)
    grad = jnp.where(lane == 194, scale_grad, grad)
    for k, out in enumerate((own,) + others):

        @pl.when(pl.program_id(0) == k)
        def _():
            out[...] = grad.astype(out.dtype)


def stem_part(ids, w9, mixed, nrm, sc, means, inv, pext):
    share, tokens = nrm.shape
    block = share // 4
    count, width, hd = w9.shape
    w9 = w9.reshape(count, 16, 4, share // 16, hd)
    rows = lambda i, ids: ((i + ids[2]) % 4, 0)
    once = pl.Buffered(1)
    shape = (block, 256)
    return pl.pallas_call(
        stem_kernel,
        grid_spec=pltpu.PrefetchScalarGridSpec(
            num_scalar_prefetch=1,
            grid=(4,),
            in_specs=[
                pl.BlockSpec((count, 4, 1, share // 16, hd), lambda i, ids: (0, (i + ids[2]) % 4, ids[0], 0, 0)),
                pl.BlockSpec(mixed.shape, lambda i, ids: (0, 0, 0), pipeline_mode=once),
                pl.BlockSpec((block, tokens), rows),
                pl.BlockSpec((block, 128), rows),
                pl.BlockSpec(means.shape, lambda i, ids: (0, 0, 0), pipeline_mode=once),
                pl.BlockSpec(inv.shape, lambda i, ids: (0, 0), pipeline_mode=once),
                pl.BlockSpec(pext.shape, lambda i, ids: (0, 0), pipeline_mode=once),
            ],
            out_specs=[pl.BlockSpec(shape, lambda i, ids: (0, 0))] * 4,
            scratch_shapes=[pltpu.VMEM((count * hd, tokens), BF16)],
        ),
        out_shape=[jax.ShapeDtypeStruct(shape, F32)] + [jax.ShapeDtypeStruct(shape, BF16)] * 3,
        compiler_params=pltpu.CompilerParams(vmem_limit_bytes=40 * 2**20),
        cost_estimate=pl.CostEstimate(
            flops=1000, bytes_accessed=1000, transcendentals=0
        ),
        name="stem_part",
    )(ids, w9, mixed, nrm, sc, means, inv, pext)


def per_device(
    latent,
    stem_weight,
    stem_bias,
    mod_shift,
    mod_scale,
    qkv_weight,
    q_gain,
    k_gain,
    tile_lists,
    out_grad,
):
    width = qkv_weight.shape[0]
    heads, hd = qkv_weight.shape[2:]
    columns = 3 * heads * hd
    channels = latent.shape[1]
    seq = lax.axis_size("seq")
    groups = seq // 4
    rows = width // seq
    s = lax.axis_index("seq")
    h = lax.axis_index("head")
    g, j = s // 4, s % 4
    half_rows = HG // 2
    tr, tc = half_rows // TS, WG // TS
    tiles = tr * tc
    cell = TS * TS

    def xor(value, mask):
        return lax.ppermute(value, "seq", [(a, a ^ mask) for a in range(seq)])

    is_low = s % 2 == 0
    even = j < 2
    piece = latent.reshape(channels, tr, TS, 2, tc, TS, 2)
    piece = jnp.transpose(piece, (0, 3, 6, 1, 4, 2, 5)).reshape(4 * channels, tiles * cell)
    border = [(a, a - 2 if a % 4 < 2 else a + 2) for a in range(seq)]
    outer = lax.ppermute(piece, "seq", [(a, b) for a, b in border if 0 <= b < seq])
    pair = jnp.stack([outer, piece])
    facing = xor(pair, 2)
    window = jnp.stack(
        [
            jnp.where(even, outer, facing[0]),
            jnp.where(even, piece, facing[1]),
            jnp.where(even, facing[1], piece),
            jnp.where(even, facing[0], outer),
        ]
    )
    grads = jnp.transpose(out_grad, (1, 0, 2)).reshape(heads, tr, TS, tc, TS, hd)
    grads = jnp.transpose(grads, (0, 1, 3, 2, 4, 5)).reshape(heads, tiles, cell, hd)
    grads = jnp.stack([grads, xor(grads, 1)])
    other = xor(window, 1)
    other, grads = lax.optimization_barrier((other, grads))
    grads = jnp.concatenate([grads, xor(grads, 2)])
    window = jnp.concatenate([jnp.where(is_low, window, other), jnp.where(is_low, other, window)], 2)
    fill = jnp.zeros((256 - 12 * channels, 2 * tiles * cell), BF16).at[:3].set(1)
    pext = jnp.stack(
        [
            jnp.concatenate([window[k], window[k + 1], window[k + 2], fill], 0).reshape(
                256, 2 * tiles, cell
            )
            for k in range(2)
        ],
        2,
    ).reshape(256, 4 * tiles * cell)

    w9 = jnp.transpose(qkv_weight, (1, 2, 0, 3)).reshape(3 * heads, width, hd)
    ids = jnp.stack([j, g, h]).astype(jnp.int32)

    proj, hid, nrm, inv, wv, sc = forward(
        ids, pext, stem_weight, stem_bias[None], mod_scale[None], mod_shift[None], w9
    )
    mixed, means = attention(ids, tile_lists, proj, grads, q_gain[None], k_gain[None], wv)
    weight = list(weight_part(ids, hid, mixed, hd))
    stem = stem_part(ids, w9, mixed, nrm, sc, means, inv, pext)

    for k in range(1, 4):
        pairs = [(a, (a + 16 * k) % seq) for a in range(seq)]
        weight[k] = lax.ppermute(weight[k], "seq", pairs)

    total = stem[0]
    count = lax.axis_size("head")
    for k in range(1, count):
        pairs = [(a, (a + k) % count) for a in range(count)]
        total = total + lax.ppermute(stem[k], "head", pairs).astype(F32)

    def quad_sum(value, low, high):
        held = lax.reduce_precision(value, 8, 7)
        sent = held.astype(BF16)
        near, far, both = (xor(sent, mask).astype(F32) for mask in (low, high, low + high))
        return (held + near) + (far + both)

    total, weight[1], weight[2] = lax.optimization_barrier((total, weight[1], weight[2]))
    total = quad_sum(total, 4, 8)
    total, weight[3] = lax.optimization_barrier((total, weight[3]))
    weight_total = sum(part.astype(F32) for part in weight)

    zhi = g % 4
    parts = []
    for k in range(4):
        part = lax.dynamic_index_in_dim(weight_total, (zhi + k) % 4, 0, keepdims=False)
        if k > 0:
            pairs = [(a, a - a % 16 + (a + 4 * k) % 16) for a in range(seq)]
            part = lax.ppermute(part.astype(BF16), "seq", pairs)
        parts.append(part)
    total = quad_sum(total, 16, 32)
    total, parts[1], parts[2] = lax.optimization_barrier((total, parts[1], parts[2]))
    weight_grad = sum(part.astype(F32) for part in parts)
    weight_grad = jnp.transpose(weight_grad.reshape(3, heads, rows, hd), (2, 0, 1, 3))

    held = total.astype(BF16)
    found = [held] + [xor(held, mask) for mask in (1, 2, 3)]
    low, high = j % 2 == 0, j < 2
    swapped = [jnp.where(low, found[m], found[m ^ 1]) for m in range(4)]
    full = jnp.stack([jnp.where(high, swapped[m], swapped[m ^ 2]) for m in range(4)])
    full = full.reshape(4, groups // 4, rows, 256)
    full = jnp.transpose(full, (1, 0, 2, 3)).reshape(width // 4, 256).T.astype(F32)
    base = 12 * channels
    stem_grad = full[:base]
    vector_grad = jnp.stack([full[base + 1], full[base + 2], full[base]])
    return (weight_grad, stem_grad, vector_grad)


def solution(mesh):
    return jax.shard_map(
        per_device,
        mesh=mesh,
        in_specs=(
            P("seq", None, None),
            P(),
            P(),
            P(),
            P(),
            P(None, None, "head", None),
            P(),
            P(),
            P(),
            P("seq", "head", None),
        ),
        out_specs=(P("seq", None, "head", None), P(None, "head"), P(None, "head")),
        check_vma=False,
    )
```

```python
import functools

import jax
import jax.numpy as jnp
from jax import lax
from jax.experimental import pallas as pl
from jax.experimental.pallas import tpu as pltpu
from jax.sharding import PartitionSpec as P

TT = 2
TS = 8
KNB = 4
HG = 32
WG = 16

ln_eps = 1e-06
LOG2E = 1.4426950408889634
F32 = jnp.float32
BF16 = jnp.bfloat16

NN = (((1,), (0,)), ((), ()))
NT = (((1,), (1,)), ((), ()))
TN = (((0,), (0,)), ((), ()))


def mm(a, b, dims=NN):
    return lax.dot_general(a, b, dims, preferred_element_type=F32)


def split2(v):
    hi = v.astype(BF16)
    return hi, (v - hi.astype(F32)).astype(BF16)


def split3(v):
    hi = v.astype(BF16)
    return (hi,) + split2(v - hi.astype(F32))


BLOCK = 512


def forward_kernel(
    ids, pext, stem, bias, scale, shift, w9, proj, hid, nrm, inv_out, wv, scale_out, emb, hid_all, sw, w, sc, sh, px, sums, sems
):
    width, block = emb.shape
    share = hid.shape[0]
    rows = share // 16
    pin = stem.shape[0]
    hd = w9.shape[2]
    j = ids[0]
    first = pl.program_id(0) == 0
    copies = [
        pltpu.make_async_copy(w9.at[n], w.at[:, n * hd : (n + 1) * hd], sems.at[n]) for n in range(w9.shape[0])
    ]

    @pl.when(first)
    def _():
        for copy in copies:
            copy.start()
        row = lax.broadcasted_iota(jnp.int32, (256 - pin, width), 0)
        parts = split3(bias[...])
        fill = jnp.zeros((256 - pin, width), F32)
        for n in range(3):
            fill = jnp.where(row == n, parts[n].astype(F32), fill)
        fill = jnp.where((row >= 8) & (row < 11), 1.0, fill)
        sw[0:pin, :] = stem[...]
        sw[pin:256, :] = fill.astype(BF16)
        total = mm(jnp.ones((8, width), BF16), sw[...], NT) * (-1.0 / width)
        row = lax.broadcasted_iota(jnp.int32, (8, 256), 0)
        lane = lax.broadcasted_iota(jnp.int32, (8, 256), 1)
        fill = jnp.zeros((8, 256), F32)
        for n, part in enumerate(split3(total)):
            fill = jnp.where(row == n, part.astype(F32), fill)
        sums[...] = jnp.where(lane < pin + 3, fill, 0.0).astype(BF16)
        ones = jnp.ones((8, 128), BF16)
        row = lax.broadcasted_iota(jnp.int32, (8, width), 0)
        for value, column in ((1.0 + scale[...], sc), (shift[...], sh)):
            parts = split3(value)
            fill = jnp.zeros((8, width), F32)
            for n in range(3):
                fill = jnp.where(row == n, parts[n].astype(F32), fill)
            column[...] = mm(fill.astype(BF16), ones, TN)
        for g in range(16):
            at = pl.ds(pl.multiple_of(4 * rows * g + rows * j, 16), rows)
            scale_out[g * rows : (g + 1) * rows, :] = sc[at, :]

    shift_row = jnp.sum(mm(sums[...], pext[...]), axis=0, keepdims=True)
    row = lax.broadcasted_iota(jnp.int32, (256 - pin, block), 0)
    tail = pext[pin:256, :].astype(F32)
    for n, part in enumerate(split3(shift_row)):
        tail = jnp.where(row == 8 + n, part.astype(F32), tail)
    px[0:pin, :] = pext[0:pin, :]
    px[pin:256, :] = tail.astype(BF16)
    step = width // 24
    total = jnp.zeros((8, block), F32)
    for n in range(24):
        x = mm(sw[:, n * step : (n + 1) * step], px[...], TN)
        emb[n * step : (n + 1) * step, :] = x
        total = total + jnp.sum((x * x).reshape(step // 8, 8, block), axis=0)
    inv = lax.rsqrt(jnp.sum(total, axis=0, keepdims=True) * (1.0 / width) + ln_eps)
    inv_out[...] = jnp.broadcast_to(inv, (8, block))
    chunk = 64

    def normalise(i, carry):
        at = pl.ds(pl.multiple_of(i * chunk, chunk), chunk)
        wide = lambda ref: jnp.concatenate([ref[at, :]] * (block // 128), 1)
        hid_all[at, :] = (emb[at, :] * inv * wide(sc) + wide(sh)).astype(BF16)
        return carry

    lax.fori_loop(0, width // chunk, normalise, 0, unroll=4)
    for g in range(16):
        at = pl.ds(pl.multiple_of(4 * rows * g + rows * j, 16), rows)
        hid[g * rows : (g + 1) * rows, :] = hid_all[at, :]
        nrm[g * rows : (g + 1) * rows, :] = (emb[at, :] * inv).astype(BF16)

    @pl.when(first)
    def _():
        for copy in copies:
            copy.wait()
        row = lax.broadcasted_iota(jnp.int32, (8, width), 0)
        fill = jnp.zeros((8, width), F32)
        for n, part in enumerate(split2(1.0 + scale[...]) + split2(shift[...])):
            fill = jnp.where(row == n, part.astype(F32), fill)
        wv[...] = mm(fill.astype(BF16), w[...])

    proj[...] = mm(hid_all[...], w[...], TN)


def forward(ids, pext, stem, bias, scale, shift, w9, block=BLOCK):
    tokens = pext.shape[1]
    count, width, hd = w9.shape
    columns = count * hd
    share = width // 4
    whole = lambda i, ids: (0, 0)
    rows = lambda i, ids: (i, 0)
    lanes = lambda i, ids: (0, i)
    once = pl.Buffered(1)
    vec = pl.BlockSpec((1, width), whole, pipeline_mode=once)
    return pl.pallas_call(
        forward_kernel,
        grid_spec=pltpu.PrefetchScalarGridSpec(
            num_scalar_prefetch=1,
            grid=(tokens // block,),
            in_specs=[
                pl.BlockSpec((256, block), lanes),
                pl.BlockSpec(stem.shape, whole, pipeline_mode=once),
                vec,
                vec,
                vec,
                pl.BlockSpec(memory_space=pl.ANY),
            ],
            out_specs=[
                pl.BlockSpec((block, columns), rows),
                pl.BlockSpec((share, block), lanes),
                pl.BlockSpec((share, block), lanes),
                pl.BlockSpec((8, block), lanes),
                pl.BlockSpec((8, columns), whole),
                pl.BlockSpec((share, 128), whole),
            ],
            scratch_shapes=[
                pltpu.VMEM((width, block), F32),
                pltpu.VMEM((width, block), BF16),
                pltpu.VMEM((256, width), BF16),
                pltpu.VMEM((width, columns), BF16),
                pltpu.VMEM((width, 128), F32),
                pltpu.VMEM((width, 128), F32),
                pltpu.VMEM((256, block), BF16),
                pltpu.VMEM((8, 256), BF16),
                pltpu.SemaphoreType.DMA((count,)),
            ],
        ),
        out_shape=[
            jax.ShapeDtypeStruct((tokens, columns), F32),
            jax.ShapeDtypeStruct((share, tokens), BF16),
            jax.ShapeDtypeStruct((share, tokens), BF16),
            jax.ShapeDtypeStruct((8, tokens), F32),
            jax.ShapeDtypeStruct((8, columns), F32),
            jax.ShapeDtypeStruct((share, 128), F32),
        ],
        compiler_params=pltpu.CompilerParams(vmem_limit_bytes=60 * 2**20),
        cost_estimate=pl.CostEstimate(
            flops=2 * tokens * width * (columns + 256), bytes_accessed=24 * 2**20, transcendentals=0
        ),
        name="forward",
    )(ids, pext, stem, bias, scale, shift, w9)


def attention_kernel(
    ids,
    lists,
    pq,
    pk,
    pv,
    og,
    qg,
    kg,
    wq,
    wk,
    wv,
    mixed,
    means,
    q_s,
    k_s,
    v_s,
    o_s,
    kt_s,
    iq_s,
    ik_s,
    dq_s,
    dk_s,
    dv_s,
    a1_s,
    a2_s,
):
    tokens, hd = pq.shape
    score_scale = hd ** (-0.5)
    j, g = ids[0], ids[1]
    tile = TT * TS * TS
    count = tokens // tile
    frame_tile = TS * TS
    first = pl.program_id(0) == 0
    last = pl.program_id(0) == pl.num_programs(0) - 1

    def rows(b):
        return pl.ds(pl.multiple_of(b * tile, tile), tile)

    def prepare(b, carry):
        at = rows(b)
        for raw, gain, keep, store in ((pq, qg, iq_s, q_s), (pk, kg, ik_s, k_s)):
            r = raw[at, :]
            inv = lax.rsqrt(jnp.mean(r * r, -1, keepdims=True) + ln_eps)
            keep[at, :] = inv
            value = r * inv * gain[...]
            store[at, :] = value.astype(BF16)
        kt_s[:, at] = jnp.transpose(value).astype(BF16)
        v_s[at, :] = pv[at, :].astype(BF16)
        half, t = b // (count // 2), b % (count // 2)
        for frame in range(2):
            to = pl.ds(pl.multiple_of(b * tile + frame * frame_tile, frame_tile), frame_tile)
            o_s[to, :] = og[jnp.bitwise_xor(j, 2 * frame + half), 0, t]
        dk_s[at, :] = jnp.zeros((tile, hd), F32)
        dv_s[at, :] = jnp.zeros((tile, hd), F32)
        return carry

    lax.fori_loop(0, count, prepare, 0, unroll=8)

    def visit(b, carry):
        mine = rows(b)
        q_b = q_s[mine, :]
        o_b = o_s[mine, :]
        near = [rows(lists[g * count + b, n] - g * count) for n in range(KNB)]
        keys = jnp.concatenate([k_s[at, :] for at in near], 0)
        keys_t = jnp.concatenate([kt_s[:, at] for at in near], 1)
        vals = jnp.concatenate([v_s[at, :] for at in near], 0)
        e = jnp.exp2(mm(keys, q_b, NT) * (score_scale * LOG2E))
        prob = e * (1.0 / jnp.sum(e, 0, keepdims=True))
        slope = mm(vals, o_b, NT)
        centre = jnp.sum(prob * slope, 0, keepdims=True)
        shaped = (prob * (slope - centre)).astype(BF16)
        rounded = prob.astype(BF16)
        dq_s[:, mine] = mm(keys_t, shaped)
        dk = mm(shaped, q_b)
        dv = mm(rounded, o_b)
        for n, at in enumerate(near):
            dk_s[at, :] += dk[n * tile : (n + 1) * tile, :]
            dv_s[at, :] += dv[n * tile : (n + 1) * tile, :]
        return carry

    lax.fori_loop(0, count, visit, 0, unroll=8)

    @pl.when(first)
    def _():
        a1_s[...] = jnp.zeros_like(a1_s)
        a2_s[...] = jnp.zeros_like(a2_s)

    def finish(b, carry):
        at = rows(b)
        m1 = a1_s[at, :]
        m2 = a2_s[at, :]
        for i, (raw, gain, keep, grad, vec) in enumerate(
            (
                (pq, qg, iq_s, jnp.transpose(dq_s[:, at]), wq),
                (pk, kg, ik_s, dk_s[at, :], wk),
                (pv, None, None, dv_s[at, :], wv),
            )
        ):
            r = raw[at, :]
            out = grad
            if gain is not None:
                inv = keep[at, :]
                u = grad * (gain[...] * score_scale)
                out = inv * (u - r * (inv * inv * jnp.mean(r * u, -1, keepdims=True)))
            out = out.astype(BF16)
            mixed[i, at, :] = out
            out = out.astype(F32)
            m1 = m1 + out * (vec[0:1, :] + vec[1:2, :])
            m2 = m2 + out * (r - (vec[2:3, :] + vec[3:4, :]))
        a1_s[at, :] = m1
        a2_s[at, :] = m2
        return carry

    lax.fori_loop(0, count, finish, 0, unroll=8)

    @pl.when(last)
    def _():
        for n, total in enumerate((a1_s, a2_s)):
            for b in range(count):
                at = slice(b * tile, (b + 1) * tile)
                row = jnp.sum(jnp.transpose(total[at, :]), axis=0, keepdims=True)
                means[n, :, at] = jnp.broadcast_to(row, (8, tile))


def attention(ids, lists, proj, og, q_gain, k_gain, wv):
    tokens, columns = proj.shape
    hd = q_gain.shape[-1]
    heads = columns // 3 // hd
    pick = lambda i: pl.BlockSpec((tokens, hd), lambda h, *_: (0, i * heads + h))
    vec = lambda i: pl.BlockSpec((8, hd), lambda h, *_: (0, i * heads + h))
    gain = pl.BlockSpec((1, hd), lambda h, *_: (0, 0))
    return pl.pallas_call(
        attention_kernel,
        grid_spec=pltpu.PrefetchScalarGridSpec(
            num_scalar_prefetch=2,
            grid=(heads,),
            in_specs=[
                pick(0),
                pick(1),
                pick(2),
                pl.BlockSpec((4, 1) + og.shape[2:], lambda h, *_: (0, h, 0, 0, 0)),
                gain,
                gain,
                vec(0),
                vec(1),
                vec(2),
            ],
            out_specs=[
                pl.BlockSpec((3, tokens, hd), lambda h, *_: (0, 0, h)),
                pl.BlockSpec((2, 8, tokens), lambda h, *_: (0, 0, 0)),
            ],
            scratch_shapes=[pltpu.VMEM((tokens, hd), BF16)] * 4
            + [pltpu.VMEM((hd, tokens), BF16)]
            + [pltpu.VMEM((tokens, 1), F32)] * 2
            + [pltpu.VMEM((hd, tokens), F32)]
            + [pltpu.VMEM((tokens, hd), F32)] * 4,
        ),
        out_shape=[
            jax.ShapeDtypeStruct((3, tokens, heads * hd), BF16),
            jax.ShapeDtypeStruct((2, 8, tokens), F32),
        ],
        compiler_params=pltpu.CompilerParams(vmem_limit_bytes=48 * 2**20),
        cost_estimate=pl.CostEstimate(
            flops=10 * tokens * 512 * hd * heads, bytes_accessed=10 * 2**20, transcendentals=tokens * 512 * heads
        ),
        name="attention",
    )(ids, lists, proj, proj, proj, og, q_gain, k_gain, wv, wv, wv)


def weight_kernel(ids, hid, mixed, *outs):
    rows, hd = outs[0].shape[2:]
    block = 4 * rows
    x = ids[1] // 4
    for k in range(4):
        at = pl.ds(pl.multiple_of((x + k) % 4 * block, block), block)
        mine = hid[at, :]
        for i in range(3):
            part = mm(mine, mixed[i]).astype(BF16)
            for n in range(3):
                for z in range(4):
                    outs[k][z, 3 * i + n] = part[z * rows : (z + 1) * rows, n * hd : (n + 1) * hd]


def weight_part(ids, hid, mixed, hd):
    share, tokens = hid.shape
    third = mixed.shape[2]
    out = jax.ShapeDtypeStruct((4, 3 * third // hd, share // 16, hd), BF16)
    vmem = pl.BlockSpec(memory_space=pltpu.VMEM)
    return pl.pallas_call(
        weight_kernel,
        in_specs=[pl.BlockSpec(memory_space=pltpu.SMEM), vmem, vmem],
        out_specs=[vmem] * 4,
        out_shape=[out] * 4,
        compiler_params=pltpu.CompilerParams(vmem_limit_bytes=40 * 2**20),
        cost_estimate=pl.CostEstimate(
            flops=2 * share * tokens * 3 * third, bytes_accessed=6 * 2**20, transcendentals=0
        ),
        name="weight_part",
    )(ids, hid, mixed)


def stem_kernel(ids, w9, mixed, nrm, sc, means, inv, pext, own, *rest):
    others, (mixed_t,) = rest[:3], rest[3:]
    third = mixed.shape[2]
    block, tokens = nrm.shape
    count, _, _, _, hd = w9.shape
    w = jnp.concatenate([w9[n, :, 0].reshape(block, hd) for n in range(count)], 1)

    @pl.when(pl.program_id(0) == 0)
    def _():
        for i in range(3):
            mixed_t[i * third : (i + 1) * third, :] = jnp.transpose(mixed[i])

    fg = mm(w, mixed_t[...])
    n = nrm[...].astype(F32)
    scale = 1.0 / (4 * 4 * block)
    m1 = means[0, 0:1, :] * scale
    m2 = means[1, 0:1, :] * scale
    eg = (fg * jnp.concatenate([sc[...]] * (tokens // 128), 1) - m1 - n * m2) * inv[0:1, :]
    hi, lo = split2(eg)
    grad = mm(hi, pext[...], NT) + mm(lo, pext[...], NT)
    shift_grad = jnp.sum(fg, -1, keepdims=True)
    scale_grad = jnp.sum(fg * n, -1, keepdims=True)
    lane = lax.broadcasted_iota(jnp.int32, grad.shape, 1)
    grad = jnp.where(lane == 193, shift_grad, grad)
    grad = jnp.where(lane == 194, scale_grad, grad)
    for k, out in enumerate((own,) + others):

        @pl.when(pl.program_id(0) == k)
        def _():
            out[...] = grad.astype(out.dtype)


def stem_part(ids, w9, mixed, nrm, sc, means, inv, pext):
    share, tokens = nrm.shape
    block = share // 4
    count, width, hd = w9.shape
    w9 = w9.reshape(count, 16, 4, share // 16, hd)
    rows = lambda i, ids: ((i + ids[2]) % 4, 0)
    once = pl.Buffered(1)
    shape = (block, 256)
    return pl.pallas_call(
        stem_kernel,
        grid_spec=pltpu.PrefetchScalarGridSpec(
            num_scalar_prefetch=1,
            grid=(4,),
            in_specs=[
                pl.BlockSpec((count, 4, 1, share // 16, hd), lambda i, ids: (0, (i + ids[2]) % 4, ids[0], 0, 0)),
                pl.BlockSpec(mixed.shape, lambda i, ids: (0, 0, 0), pipeline_mode=once),
                pl.BlockSpec((block, tokens), rows),
                pl.BlockSpec((block, 128), rows),
                pl.BlockSpec(means.shape, lambda i, ids: (0, 0, 0), pipeline_mode=once),
                pl.BlockSpec(inv.shape, lambda i, ids: (0, 0), pipeline_mode=once),
                pl.BlockSpec(pext.shape, lambda i, ids: (0, 0), pipeline_mode=once),
            ],
            out_specs=[pl.BlockSpec(shape, lambda i, ids: (0, 0))] * 4,
            scratch_shapes=[pltpu.VMEM((count * hd, tokens), BF16)],
        ),
        out_shape=[jax.ShapeDtypeStruct(shape, F32)] + [jax.ShapeDtypeStruct(shape, BF16)] * 3,
        compiler_params=pltpu.CompilerParams(vmem_limit_bytes=40 * 2**20),
        cost_estimate=pl.CostEstimate(
            flops=1000, bytes_accessed=1000, transcendentals=0
        ),
        name="stem_part",
    )(ids, w9, mixed, nrm, sc, means, inv, pext)


def per_device(
    latent,
    stem_weight,
    stem_bias,
    mod_shift,
    mod_scale,
    qkv_weight,
    q_gain,
    k_gain,
    tile_lists,
    out_grad,
):
    width = qkv_weight.shape[0]
    heads, hd = qkv_weight.shape[2:]
    columns = 3 * heads * hd
    channels = latent.shape[1]
    seq = lax.axis_size("seq")
    groups = seq // 4
    rows = width // seq
    s = lax.axis_index("seq")
    h = lax.axis_index("head")
    g, j = s // 4, s % 4
    half_rows = HG // 2
    tr, tc = half_rows // TS, WG // TS
    tiles = tr * tc
    cell = TS * TS

    def xor(value, mask):
        return lax.ppermute(value, "seq", [(a, a ^ mask) for a in range(seq)])

    is_low = s % 2 == 0
    even = j < 2
    piece = latent.reshape(channels, tr, TS, 2, tc, TS, 2)
    piece = jnp.transpose(piece, (0, 3, 6, 1, 4, 2, 5)).reshape(4 * channels, tiles * cell)
    border = [(a, a - 2 if a % 4 < 2 else a + 2) for a in range(seq)]
    outer = lax.ppermute(piece, "seq", [(a, b) for a, b in border if 0 <= b < seq])
    pair = jnp.stack([outer, piece])
    facing = xor(pair, 2)
    window = jnp.stack(
        [
            jnp.where(even, outer, facing[0]),
            jnp.where(even, piece, facing[1]),
            jnp.where(even, facing[1], piece),
            jnp.where(even, facing[0], outer),
        ]
    )
    grads = jnp.transpose(out_grad, (1, 0, 2)).reshape(heads, tr, TS, tc, TS, hd)
    grads = jnp.transpose(grads, (0, 1, 3, 2, 4, 5)).reshape(heads, tiles, cell, hd)
    grads = jnp.stack([grads, xor(grads, 1)])
    other = xor(window, 1)
    other, grads = lax.optimization_barrier((other, grads))
    grads = jnp.concatenate([grads, xor(grads, 2)])
    window = jnp.concatenate([jnp.where(is_low, window, other), jnp.where(is_low, other, window)], 2)
    fill = jnp.zeros((256 - 12 * channels, 2 * tiles * cell), BF16).at[:3].set(1)
    pext = jnp.stack(
        [
            jnp.concatenate([window[k], window[k + 1], window[k + 2], fill], 0).reshape(
                256, 2 * tiles, cell
            )
            for k in range(2)
        ],
        2,
    ).reshape(256, 4 * tiles * cell)

    w9 = jnp.transpose(qkv_weight, (1, 2, 0, 3)).reshape(3 * heads, width, hd)
    ids = jnp.stack([j, g, h]).astype(jnp.int32)

    proj, hid, nrm, inv, wv, sc = forward(
        ids, pext, stem_weight, stem_bias[None], mod_scale[None], mod_shift[None], w9
    )
    wv = pltpu.with_memory_space_constraint(wv, pltpu.HBM)
    mixed, means = attention(ids, tile_lists, proj, grads, q_gain[None], k_gain[None], wv)
    weight = list(weight_part(ids, hid, mixed, hd))
    stem = stem_part(ids, w9, mixed, nrm, sc, means, inv, pext)

    for k in range(1, 4):
        pairs = [(a, (a + 16 * k) % seq) for a in range(seq)]
        weight[k] = lax.ppermute(weight[k], "seq", pairs)

    total = stem[0]
    count = lax.axis_size("head")
    for k in range(1, count):
        pairs = [(a, (a + k) % count) for a in range(count)]
        total = total + lax.ppermute(stem[k], "head", pairs).astype(F32)

    def quad_sum(value, low, high):
        held = lax.reduce_precision(value, 8, 7)
        sent = held.astype(BF16)
        near, far, both = (xor(sent, mask).astype(F32) for mask in (low, high, low + high))
        return (held + near) + (far + both)

    total, weight[1], weight[3] = lax.optimization_barrier((total, weight[1], weight[3]))
    total = quad_sum(total, 4, 8)
    total, weight[2] = lax.optimization_barrier((total, weight[2]))
    weight_total = sum(part.astype(F32) for part in weight)

    zhi = g % 4
    parts = []
    for k in range(4):
        part = lax.dynamic_index_in_dim(weight_total, (zhi + k) % 4, 0, keepdims=False)
        if k > 0:
            pairs = [(a, a - a % 16 + (a + 4 * k) % 16) for a in range(seq)]
            part = lax.ppermute(part.astype(BF16), "seq", pairs)
        parts.append(part)
    total = quad_sum(total, 16, 32)
    total, parts[1], parts[2] = lax.optimization_barrier((total, parts[1], parts[2]))
    weight_grad = sum(part.astype(F32) for part in parts)
    weight_grad = jnp.transpose(weight_grad.reshape(3, heads, rows, hd), (2, 0, 1, 3))

    held = total.astype(BF16)
    found = [held] + [xor(held, mask) for mask in (1, 2, 3)]
    low, high = j % 2 == 0, j < 2
    swapped = [jnp.where(low, found[m], found[m ^ 1]) for m in range(4)]
    full = jnp.stack([jnp.where(high, swapped[m], swapped[m ^ 2]) for m in range(4)])
    full = full.reshape(4, groups // 4, rows, 256)
    full = jnp.transpose(full, (1, 0, 2, 3)).reshape(width // 4, 256).T.astype(F32)
    base = 12 * channels
    stem_grad = full[:base]
    vector_grad = jnp.stack([full[base + 1], full[base + 2], full[base]])
    return (weight_grad, stem_grad, vector_grad)


def solution(mesh):
    return jax.shard_map(
        per_device,
        mesh=mesh,
        in_specs=(
            P("seq", None, None),
            P(),
            P(),
            P(),
            P(),
            P(None, None, "head", None),
            P(),
            P(),
            P(),
            P("seq", "head", None),
        ),
        out_specs=(P("seq", None, "head", None), P(None, "head"), P(None, "head")),
        check_vma=False,
    )
```

```python
import functools

import jax
import jax.numpy as jnp
from jax import lax
from jax.experimental import pallas as pl
from jax.experimental.pallas import tpu as pltpu
from jax.sharding import PartitionSpec as P

TT = 2
TS = 8
KNB = 4
HG = 32
WG = 16

ln_eps = 1e-06
LOG2E = 1.4426950408889634
F32 = jnp.float32
BF16 = jnp.bfloat16

NN = (((1,), (0,)), ((), ()))
NT = (((1,), (1,)), ((), ()))
TN = (((0,), (0,)), ((), ()))


def mm(a, b, dims=NN):
    return lax.dot_general(a, b, dims, preferred_element_type=F32)


def split2(v):
    hi = v.astype(BF16)
    return hi, (v - hi.astype(F32)).astype(BF16)


def split3(v):
    hi = v.astype(BF16)
    return (hi,) + split2(v - hi.astype(F32))


BLOCK = 512


def forward_kernel(
    ids, pext, stem, bias, scale, shift, w9, proj, hid, nrm, inv_out, wv, scale_out, emb, hid_all, sw, w, sc, sh, px, sums, sems
):
    width, block = emb.shape
    share = hid.shape[0]
    rows = share // 16
    pin = stem.shape[0]
    hd = w9.shape[2]
    j = ids[0]
    first = pl.program_id(0) == 0
    copies = [
        pltpu.make_async_copy(w9.at[n], w.at[:, n * hd : (n + 1) * hd], sems.at[n]) for n in range(w9.shape[0])
    ]

    @pl.when(first)
    def _():
        for copy in copies:
            copy.start()
        row = lax.broadcasted_iota(jnp.int32, (256 - pin, width), 0)
        parts = split3(bias[...])
        fill = jnp.zeros((256 - pin, width), F32)
        for n in range(3):
            fill = jnp.where(row == n, parts[n].astype(F32), fill)
        fill = jnp.where((row >= 8) & (row < 11), 1.0, fill)
        sw[0:pin, :] = stem[...]
        sw[pin:256, :] = fill.astype(BF16)
        total = mm(jnp.ones((8, width), BF16), sw[...], NT) * (-1.0 / width)
        row = lax.broadcasted_iota(jnp.int32, (8, 256), 0)
        lane = lax.broadcasted_iota(jnp.int32, (8, 256), 1)
        fill = jnp.zeros((8, 256), F32)
        for n, part in enumerate(split3(total)):
            fill = jnp.where(row == n, part.astype(F32), fill)
        sums[...] = jnp.where(lane < pin + 3, fill, 0.0).astype(BF16)
        ones = jnp.ones((8, 128), BF16)
        row = lax.broadcasted_iota(jnp.int32, (8, width), 0)
        for value, column in ((1.0 + scale[...], sc), (shift[...], sh)):
            parts = split3(value)
            fill = jnp.zeros((8, width), F32)
            for n in range(3):
                fill = jnp.where(row == n, parts[n].astype(F32), fill)
            column[...] = mm(fill.astype(BF16), ones, TN)
        for g in range(16):
            at = pl.ds(pl.multiple_of(4 * rows * g + rows * j, 16), rows)
            scale_out[g * rows : (g + 1) * rows, :] = sc[at, :]

    shift_row = jnp.sum(mm(sums[...], pext[...]), axis=0, keepdims=True)
    row = lax.broadcasted_iota(jnp.int32, (256 - pin, block), 0)
    tail = pext[pin:256, :].astype(F32)
    for n, part in enumerate(split3(shift_row)):
        tail = jnp.where(row == 8 + n, part.astype(F32), tail)
    px[0:pin, :] = pext[0:pin, :]
    px[pin:256, :] = tail.astype(BF16)
    step = width // 24
    total = jnp.zeros((8, block), F32)
    for n in range(24):
        x = mm(sw[:, n * step : (n + 1) * step], px[...], TN)
        emb[n * step : (n + 1) * step, :] = x
        total = total + jnp.sum((x * x).reshape(step // 8, 8, block), axis=0)
    inv = lax.rsqrt(jnp.sum(total, axis=0, keepdims=True) * (1.0 / width) + ln_eps)
    inv_out[...] = jnp.broadcast_to(inv, (8, block))
    chunk = 64

    def normalise(i, carry):
        at = pl.ds(pl.multiple_of(i * chunk, chunk), chunk)
        wide = lambda ref: jnp.concatenate([ref[at, :]] * (block // 128), 1)
        hid_all[at, :] = (emb[at, :] * inv * wide(sc) + wide(sh)).astype(BF16)
        return carry

    lax.fori_loop(0, width // chunk, normalise, 0, unroll=4)
    for g in range(16):
        at = pl.ds(pl.multiple_of(4 * rows * g + rows * j, 16), rows)
        hid[g * rows : (g + 1) * rows, :] = hid_all[at, :]
        nrm[g * rows : (g + 1) * rows, :] = (emb[at, :] * inv).astype(BF16)

    @pl.when(first)
    def _():
        for copy in copies:
            copy.wait()
        row = lax.broadcasted_iota(jnp.int32, (8, width), 0)
        fill = jnp.zeros((8, width), F32)
        for n, part in enumerate(split2(1.0 + scale[...]) + split2(shift[...])):
            fill = jnp.where(row == n, part.astype(F32), fill)
        wv[...] = mm(fill.astype(BF16), w[...])

    proj[...] = mm(hid_all[...], w[...], TN)


def forward(ids, pext, stem, bias, scale, shift, w9, block=BLOCK):
    tokens = pext.shape[1]
    count, width, hd = w9.shape
    columns = count * hd
    share = width // 4
    whole = lambda i, ids: (0, 0)
    rows = lambda i, ids: (i, 0)
    lanes = lambda i, ids: (0, i)
    once = pl.Buffered(1)
    vec = pl.BlockSpec((1, width), whole, pipeline_mode=once)
    return pl.pallas_call(
        forward_kernel,
        grid_spec=pltpu.PrefetchScalarGridSpec(
            num_scalar_prefetch=1,
            grid=(tokens // block,),
            in_specs=[
                pl.BlockSpec((256, block), lanes),
                pl.BlockSpec(stem.shape, whole, pipeline_mode=once),
                vec,
                vec,
                vec,
                pl.BlockSpec(memory_space=pl.ANY),
            ],
            out_specs=[
                pl.BlockSpec((block, columns), rows),
                pl.BlockSpec((share, block), lanes),
                pl.BlockSpec((share, block), lanes),
                pl.BlockSpec((8, block), lanes),
                pl.BlockSpec((8, columns), whole),
                pl.BlockSpec((share, 128), whole),
            ],
            scratch_shapes=[
                pltpu.VMEM((width, block), F32),
                pltpu.VMEM((width, block), BF16),
                pltpu.VMEM((256, width), BF16),
                pltpu.VMEM((width, columns), BF16),
                pltpu.VMEM((width, 128), F32),
                pltpu.VMEM((width, 128), F32),
                pltpu.VMEM((256, block), BF16),
                pltpu.VMEM((8, 256), BF16),
                pltpu.SemaphoreType.DMA((count,)),
            ],
        ),
        out_shape=[
            jax.ShapeDtypeStruct((tokens, columns), F32),
            jax.ShapeDtypeStruct((share, tokens), BF16),
            jax.ShapeDtypeStruct((share, tokens), BF16),
            jax.ShapeDtypeStruct((8, tokens), F32),
            jax.ShapeDtypeStruct((8, columns), F32),
            jax.ShapeDtypeStruct((share, 128), F32),
        ],
        compiler_params=pltpu.CompilerParams(vmem_limit_bytes=60 * 2**20),
        cost_estimate=pl.CostEstimate(
            flops=2 * tokens * width * (columns + 256), bytes_accessed=24 * 2**20, transcendentals=0
        ),
        name="forward",
    )(ids, pext, stem, bias, scale, shift, w9)


def attention_kernel(
    ids,
    lists,
    pq,
    pk,
    pv,
    og,
    qg,
    kg,
    wq,
    wk,
    wv,
    mixed,
    means,
    q_s,
    k_s,
    v_s,
    o_s,
    kt_s,
    iq_s,
    ik_s,
    dq_s,
    dk_s,
    dv_s,
    a1_s,
    a2_s,
):
    tokens, hd = pq.shape
    score_scale = hd ** (-0.5)
    j, g = ids[0], ids[1]
    tile = TT * TS * TS
    count = tokens // tile
    frame_tile = TS * TS
    first = pl.program_id(0) == 0
    last = pl.program_id(0) == pl.num_programs(0) - 1

    def rows(b):
        return pl.ds(pl.multiple_of(b * tile, tile), tile)

    def prepare(b, carry):
        at = rows(b)
        for raw, gain, keep, store in ((pq, qg, iq_s, q_s), (pk, kg, ik_s, k_s)):
            r = raw[at, :]
            inv = lax.rsqrt(jnp.mean(r * r, -1, keepdims=True) + ln_eps)
            keep[at, :] = inv
            value = r * inv * gain[...]
            store[at, :] = value.astype(BF16)
        kt_s[:, at] = jnp.transpose(value).astype(BF16)
        v_s[at, :] = pv[at, :].astype(BF16)
        half, t = b // (count // 2), b % (count // 2)
        for frame in range(2):
            to = pl.ds(pl.multiple_of(b * tile + frame * frame_tile, frame_tile), frame_tile)
            o_s[to, :] = og[jnp.bitwise_xor(j, 2 * frame + half), 0, t]
        dk_s[at, :] = jnp.zeros((tile, hd), F32)
        dv_s[at, :] = jnp.zeros((tile, hd), F32)
        return carry

    lax.fori_loop(0, count, prepare, 0, unroll=8)

    def visit(b, carry):
        mine = rows(b)
        q_b = q_s[mine, :]
        o_b = o_s[mine, :]
        near = [rows(lists[g * count + b, n] - g * count) for n in range(KNB)]
        keys = jnp.concatenate([k_s[at, :] for at in near], 0)
        keys_t = jnp.concatenate([kt_s[:, at] for at in near], 1)
        vals = jnp.concatenate([v_s[at, :] for at in near], 0)
        e = jnp.exp2(mm(keys, q_b, NT) * (score_scale * LOG2E))
        prob = e * (1.0 / jnp.sum(e, 0, keepdims=True))
        slope = mm(vals, o_b, NT)
        centre = jnp.sum(prob * slope, 0, keepdims=True)
        shaped = (prob * (slope - centre)).astype(BF16)
        rounded = prob.astype(BF16)
        dq_s[:, mine] = mm(keys_t, shaped)
        dk = mm(shaped, q_b)
        dv = mm(rounded, o_b)
        for n, at in enumerate(near):
            dk_s[at, :] += dk[n * tile : (n + 1) * tile, :]
            dv_s[at, :] += dv[n * tile : (n + 1) * tile, :]
        return carry

    lax.fori_loop(0, count, visit, 0, unroll=8)

    @pl.when(first)
    def _():
        a1_s[...] = jnp.zeros_like(a1_s)
        a2_s[...] = jnp.zeros_like(a2_s)

    def finish(b, carry):
        at = rows(b)
        m1 = a1_s[at, :]
        m2 = a2_s[at, :]
        for i, (raw, gain, keep, grad, vec) in enumerate(
            (
                (pq, qg, iq_s, jnp.transpose(dq_s[:, at]), wq),
                (pk, kg, ik_s, dk_s[at, :], wk),
                (pv, None, None, dv_s[at, :], wv),
            )
        ):
            r = raw[at, :]
            out = grad
            if gain is not None:
                inv = keep[at, :]
                u = grad * (gain[...] * score_scale)
                out = inv * (u - r * (inv * inv * jnp.mean(r * u, -1, keepdims=True)))
            out = out.astype(BF16)
            mixed[i, at, :] = out
            out = out.astype(F32)
            m1 = m1 + out * (vec[0:1, :] + vec[1:2, :])
            m2 = m2 + out * (r - (vec[2:3, :] + vec[3:4, :]))
        a1_s[at, :] = m1
        a2_s[at, :] = m2
        return carry

    lax.fori_loop(0, count, finish, 0, unroll=8)

    @pl.when(last)
    def _():
        for n, total in enumerate((a1_s, a2_s)):
            for b in range(count):
                at = slice(b * tile, (b + 1) * tile)
                row = jnp.sum(jnp.transpose(total[at, :]), axis=0, keepdims=True)
                means[n, :, at] = jnp.broadcast_to(row, (8, tile))


def attention(ids, lists, proj, og, q_gain, k_gain, wv):
    tokens, columns = proj.shape
    hd = q_gain.shape[-1]
    heads = columns // 3 // hd
    pick = lambda i: pl.BlockSpec((tokens, hd), lambda h, *_: (0, i * heads + h))
    vec = lambda i: pl.BlockSpec((8, hd), lambda h, *_: (0, i * heads + h))
    gain = pl.BlockSpec((1, hd), lambda h, *_: (0, 0))
    return pl.pallas_call(
        attention_kernel,
        grid_spec=pltpu.PrefetchScalarGridSpec(
            num_scalar_prefetch=2,
            grid=(heads,),
            in_specs=[
                pick(0),
                pick(1),
                pick(2),
                pl.BlockSpec((4, 1) + og.shape[2:], lambda h, *_: (0, h, 0, 0, 0)),
                gain,
                gain,
                vec(0),
                vec(1),
                vec(2),
            ],
            out_specs=[
                pl.BlockSpec((3, tokens, hd), lambda h, *_: (0, 0, h)),
                pl.BlockSpec((2, 8, tokens), lambda h, *_: (0, 0, 0)),
            ],
            scratch_shapes=[pltpu.VMEM((tokens, hd), BF16)] * 4
            + [pltpu.VMEM((hd, tokens), BF16)]
            + [pltpu.VMEM((tokens, 1), F32)] * 2
            + [pltpu.VMEM((hd, tokens), F32)]
            + [pltpu.VMEM((tokens, hd), F32)] * 4,
        ),
        out_shape=[
            jax.ShapeDtypeStruct((3, tokens, heads * hd), BF16),
            jax.ShapeDtypeStruct((2, 8, tokens), F32),
        ],
        compiler_params=pltpu.CompilerParams(vmem_limit_bytes=48 * 2**20),
        cost_estimate=pl.CostEstimate(
            flops=10 * tokens * 512 * hd * heads, bytes_accessed=10 * 2**20, transcendentals=tokens * 512 * heads
        ),
        name="attention",
    )(ids, lists, proj, proj, proj, og, q_gain, k_gain, wv, wv, wv)


def weight_kernel(ids, hid, mixed, *outs):
    rows, hd = outs[0].shape[2:]
    block = 4 * rows
    x = ids[1] // 4
    for k in range(4):
        at = pl.ds(pl.multiple_of((x + k) % 4 * block, block), block)
        mine = hid[at, :]
        for i in range(3):
            part = mm(mine, mixed[i]).astype(BF16)
            for n in range(3):
                for z in range(4):
                    outs[k][z, 3 * i + n] = part[z * rows : (z + 1) * rows, n * hd : (n + 1) * hd]


def weight_part(ids, hid, mixed, hd):
    share, tokens = hid.shape
    third = mixed.shape[2]
    out = jax.ShapeDtypeStruct((4, 3 * third // hd, share // 16, hd), BF16)
    vmem = pl.BlockSpec(memory_space=pltpu.VMEM)
    return pl.pallas_call(
        weight_kernel,
        in_specs=[pl.BlockSpec(memory_space=pltpu.SMEM), vmem, vmem],
        out_specs=[vmem] * 4,
        out_shape=[out] * 4,
        compiler_params=pltpu.CompilerParams(vmem_limit_bytes=40 * 2**20),
        cost_estimate=pl.CostEstimate(
            flops=2 * share * tokens * 3 * third, bytes_accessed=6 * 2**20, transcendentals=0
        ),
        name="weight_part",
    )(ids, hid, mixed)


def stem_kernel(ids, w9, mixed, nrm, sc, means, inv, pext, own, *rest):
    others, (mixed_t,) = rest[:3], rest[3:]
    third = mixed.shape[2]
    block, tokens = nrm.shape
    count, _, _, _, hd = w9.shape
    w = jnp.concatenate([w9[n, :, 0].reshape(block, hd) for n in range(count)], 1)

    @pl.when(pl.program_id(0) == 0)
    def _():
        for i in range(3):
            mixed_t[i * third : (i + 1) * third, :] = jnp.transpose(mixed[i])

    fg = mm(w, mixed_t[...])
    n = nrm[...].astype(F32)
    scale = 1.0 / (4 * 4 * block)
    m1 = means[0, 0:1, :] * scale
    m2 = means[1, 0:1, :] * scale
    eg = (fg * jnp.concatenate([sc[...]] * (tokens // 128), 1) - m1 - n * m2) * inv[0:1, :]
    hi, lo = split2(eg)
    grad = mm(hi, pext[...], NT) + mm(lo, pext[...], NT)
    shift_grad = jnp.sum(fg, -1, keepdims=True)
    scale_grad = jnp.sum(fg * n, -1, keepdims=True)
    lane = lax.broadcasted_iota(jnp.int32, grad.shape, 1)
    grad = jnp.where(lane == 193, shift_grad, grad)
    grad = jnp.where(lane == 194, scale_grad, grad)
    for k, out in enumerate((own,) + others):

        @pl.when(pl.program_id(0) == k)
        def _():
            out[...] = grad.astype(out.dtype)


def stem_part(ids, w9, mixed, nrm, sc, means, inv, pext):
    share, tokens = nrm.shape
    block = share // 4
    count, width, hd = w9.shape
    w9 = w9.reshape(count, 16, 4, share // 16, hd)
    rows = lambda i, ids: ((i + ids[2]) % 4, 0)
    once = pl.Buffered(1)
    shape = (block, 256)
    return pl.pallas_call(
        stem_kernel,
        grid_spec=pltpu.PrefetchScalarGridSpec(
            num_scalar_prefetch=1,
            grid=(4,),
            in_specs=[
                pl.BlockSpec((count, 4, 1, share // 16, hd), lambda i, ids: (0, (i + ids[2]) % 4, ids[0], 0, 0)),
                pl.BlockSpec(mixed.shape, lambda i, ids: (0, 0, 0), pipeline_mode=once),
                pl.BlockSpec((block, tokens), rows),
                pl.BlockSpec((block, 128), rows),
                pl.BlockSpec(means.shape, lambda i, ids: (0, 0, 0), pipeline_mode=once),
                pl.BlockSpec(inv.shape, lambda i, ids: (0, 0), pipeline_mode=once),
                pl.BlockSpec(pext.shape, lambda i, ids: (0, 0), pipeline_mode=once),
            ],
            out_specs=[pl.BlockSpec(shape, lambda i, ids: (0, 0))] * 4,
            scratch_shapes=[pltpu.VMEM((count * hd, tokens), BF16)],
        ),
        out_shape=[jax.ShapeDtypeStruct(shape, F32)] + [jax.ShapeDtypeStruct(shape, BF16)] * 3,
        compiler_params=pltpu.CompilerParams(vmem_limit_bytes=40 * 2**20),
        cost_estimate=pl.CostEstimate(
            flops=1000, bytes_accessed=1000, transcendentals=0
        ),
        name="stem_part",
    )(ids, w9, mixed, nrm, sc, means, inv, pext)


def per_device(
    latent,
    stem_weight,
    stem_bias,
    mod_shift,
    mod_scale,
    qkv_weight,
    q_gain,
    k_gain,
    tile_lists,
    out_grad,
):
    width = qkv_weight.shape[0]
    heads, hd = qkv_weight.shape[2:]
    columns = 3 * heads * hd
    channels = latent.shape[1]
    seq = lax.axis_size("seq")
    groups = seq // 4
    rows = width // seq
    s = lax.axis_index("seq")
    h = lax.axis_index("head")
    g, j = s // 4, s % 4
    half_rows = HG // 2
    tr, tc = half_rows // TS, WG // TS
    tiles = tr * tc
    cell = TS * TS

    def xor(value, mask):
        return lax.ppermute(value, "seq", [(a, a ^ mask) for a in range(seq)])

    is_low = s % 2 == 0
    even = j < 2
    piece = latent.reshape(channels, tr, TS, 2, tc, TS, 2)
    piece = jnp.transpose(piece, (0, 3, 6, 1, 4, 2, 5)).reshape(4 * channels, tiles * cell)
    border = [(a, a - 2 if a % 4 < 2 else a + 2) for a in range(seq)]
    outer = lax.ppermute(piece, "seq", [(a, b) for a, b in border if 0 <= b < seq])
    pair = jnp.stack([outer, piece])
    facing = xor(pair, 2)
    window = jnp.stack(
        [
            jnp.where(even, outer, facing[0]),
            jnp.where(even, piece, facing[1]),
            jnp.where(even, facing[1], piece),
            jnp.where(even, facing[0], outer),
        ]
    )
    grads = jnp.transpose(out_grad, (1, 0, 2)).reshape(heads, tr, TS, tc, TS, hd)
    grads = jnp.transpose(grads, (0, 1, 3, 2, 4, 5)).reshape(heads, tiles, cell, hd)
    grads = jnp.stack([grads, xor(grads, 1)])
    other = xor(window, 1)
    other, grads = lax.optimization_barrier((other, grads))
    grads = jnp.concatenate([grads, xor(grads, 2)])
    window = jnp.concatenate([jnp.where(is_low, window, other), jnp.where(is_low, other, window)], 2)
    fill = jnp.zeros((256 - 12 * channels, 2 * tiles * cell), BF16).at[:3].set(1)
    pext = jnp.stack(
        [
            jnp.concatenate([window[k], window[k + 1], window[k + 2], fill], 0).reshape(
                256, 2 * tiles, cell
            )
            for k in range(2)
        ],
        2,
    ).reshape(256, 4 * tiles * cell)

    w9 = jnp.transpose(qkv_weight, (1, 2, 0, 3)).reshape(3 * heads, width, hd)
    ids = jnp.stack([j, g, h]).astype(jnp.int32)

    proj, hid, nrm, inv, wv, sc = forward(
        ids, pext, stem_weight, stem_bias[None], mod_scale[None], mod_shift[None], w9
    )
    wv = pltpu.with_memory_space_constraint(wv, pltpu.HBM)
    mixed, means = attention(ids, tile_lists, proj, grads, q_gain[None], k_gain[None], wv)
    weight = list(weight_part(ids, hid, mixed, hd))
    stem = stem_part(ids, w9, mixed, nrm, sc, means, inv, pext)

    for k in range(1, 4):
        pairs = [(a, (a + 16 * k) % seq) for a in range(seq)]
        weight[k] = lax.ppermute(weight[k], "seq", pairs)

    total = stem[0]
    count = lax.axis_size("head")
    for k in range(1, count):
        pairs = [(a, (a + k) % count) for a in range(count)]
        total = total + lax.ppermute(stem[k], "head", pairs).astype(F32)

    def quad_sum(value, low, high):
        held = lax.reduce_precision(value, 8, 7)
        sent = held.astype(BF16)
        near, far, both = (xor(sent, mask).astype(F32) for mask in (low, high, low + high))
        return (held + near) + (far + both)

    total, weight[1], weight[3] = lax.optimization_barrier((total, weight[1], weight[3]))
    total = quad_sum(total, 4, 8)
    total, weight[2] = lax.optimization_barrier((total, weight[2]))
    weight_total = sum(part.astype(F32) for part in weight)

    zhi = g % 4
    parts = []
    for k in range(4):
        part = lax.dynamic_index_in_dim(weight_total, (zhi + k) % 4, 0, keepdims=False)
        if k > 0:
            pairs = [(a, a - a % 16 + (a + 4 * k) % 16) for a in range(seq)]
            part = lax.ppermute(part.astype(BF16), "seq", pairs)
        parts.append(part)
    total = quad_sum(total, 16, 32)
    total, parts[1], parts[3] = lax.optimization_barrier((total, parts[1], parts[3]))
    weight_grad = sum(part.astype(F32) for part in parts)
    weight_grad = jnp.transpose(weight_grad.reshape(3, heads, rows, hd), (2, 0, 1, 3))

    held = total.astype(BF16)
    found = [held] + [xor(held, mask) for mask in (1, 2, 3)]
    low, high = j % 2 == 0, j < 2
    swapped = [jnp.where(low, found[m], found[m ^ 1]) for m in range(4)]
    full = jnp.stack([jnp.where(high, swapped[m], swapped[m ^ 2]) for m in range(4)])
    full = full.reshape(4, groups // 4, rows, 256)
    full = jnp.transpose(full, (1, 0, 2, 3)).reshape(width // 4, 256).T.astype(F32)
    base = 12 * channels
    stem_grad = full[:base]
    vector_grad = jnp.stack([full[base + 1], full[base + 2], full[base]])
    return (weight_grad, stem_grad, vector_grad)


def solution(mesh):
    return jax.shard_map(
        per_device,
        mesh=mesh,
        in_specs=(
            P("seq", None, None),
            P(),
            P(),
            P(),
            P(),
            P(None, None, "head", None),
            P(),
            P(),
            P(),
            P("seq", "head", None),
        ),
        out_specs=(P("seq", None, "head", None), P(None, "head"), P(None, "head")),
        check_vma=False,
    )
```

```python
import functools

import jax
import jax.numpy as jnp
from jax import lax
from jax.experimental import pallas as pl
from jax.experimental.pallas import tpu as pltpu
from jax.sharding import PartitionSpec as P

TT = 2
TS = 8
KNB = 4
HG = 32
WG = 16

ln_eps = 1e-06
LOG2E = 1.4426950408889634
F32 = jnp.float32
BF16 = jnp.bfloat16

NN = (((1,), (0,)), ((), ()))
NT = (((1,), (1,)), ((), ()))
TN = (((0,), (0,)), ((), ()))


def mm(a, b, dims=NN):
    return lax.dot_general(a, b, dims, preferred_element_type=F32)


def split2(v):
    hi = v.astype(BF16)
    return hi, (v - hi.astype(F32)).astype(BF16)


def split3(v):
    hi = v.astype(BF16)
    return (hi,) + split2(v - hi.astype(F32))


BLOCK = 512


def forward_kernel(
    ids, pext, stem, bias, scale, shift, w9, proj, hid, nrm, inv_out, wv, scale_out, emb, hid_all, sw, w, sc, sh, px, sums, sems
):
    width, block = emb.shape
    share = hid.shape[0]
    rows = share // 16
    pin = stem.shape[0]
    hd = w9.shape[2]
    j = ids[0]
    first = pl.program_id(0) == 0
    copies = [
        pltpu.make_async_copy(w9.at[n], w.at[:, n * hd : (n + 1) * hd], sems.at[n]) for n in range(w9.shape[0])
    ]

    @pl.when(first)
    def _():
        for copy in copies:
            copy.start()
        row = lax.broadcasted_iota(jnp.int32, (256 - pin, width), 0)
        parts = split3(bias[...])
        fill = jnp.zeros((256 - pin, width), F32)
        for n in range(3):
            fill = jnp.where(row == n, parts[n].astype(F32), fill)
        fill = jnp.where((row >= 8) & (row < 11), 1.0, fill)
        sw[0:pin, :] = stem[...]
        sw[pin:256, :] = fill.astype(BF16)
        total = mm(jnp.ones((8, width), BF16), sw[...], NT) * (-1.0 / width)
        row = lax.broadcasted_iota(jnp.int32, (8, 256), 0)
        lane = lax.broadcasted_iota(jnp.int32, (8, 256), 1)
        fill = jnp.zeros((8, 256), F32)
        for n, part in enumerate(split3(total)):
            fill = jnp.where(row == n, part.astype(F32), fill)
        sums[...] = jnp.where(lane < pin + 3, fill, 0.0).astype(BF16)
        ones = jnp.ones((8, 128), BF16)
        row = lax.broadcasted_iota(jnp.int32, (8, width), 0)
        for value, column in ((1.0 + scale[...], sc), (shift[...], sh)):
            parts = split3(value)
            fill = jnp.zeros((8, width), F32)
            for n in range(3):
                fill = jnp.where(row == n, parts[n].astype(F32), fill)
            column[...] = mm(fill.astype(BF16), ones, TN)
        for g in range(16):
            at = pl.ds(pl.multiple_of(4 * rows * g + rows * j, 16), rows)
            scale_out[g * rows : (g + 1) * rows, :] = sc[at, :]

    shift_row = jnp.sum(mm(sums[...], pext[...]), axis=0, keepdims=True)
    row = lax.broadcasted_iota(jnp.int32, (256 - pin, block), 0)
    tail = pext[pin:256, :].astype(F32)
    for n, part in enumerate(split3(shift_row)):
        tail = jnp.where(row == 8 + n, part.astype(F32), tail)
    px[0:pin, :] = pext[0:pin, :]
    px[pin:256, :] = tail.astype(BF16)
    step = width // 24
    total = jnp.zeros((8, block), F32)
    for n in range(24):
        x = mm(sw[:, n * step : (n + 1) * step], px[...], TN)
        emb[n * step : (n + 1) * step, :] = x
        total = total + jnp.sum((x * x).reshape(step // 8, 8, block), axis=0)
    inv = lax.rsqrt(jnp.sum(total, axis=0, keepdims=True) * (1.0 / width) + ln_eps)
    inv_out[...] = jnp.broadcast_to(inv, (8, block))
    chunk = 64

    def normalise(i, carry):
        at = pl.ds(pl.multiple_of(i * chunk, chunk), chunk)
        wide = lambda ref: jnp.concatenate([ref[at, :]] * (block // 128), 1)
        hid_all[at, :] = (emb[at, :] * inv * wide(sc) + wide(sh)).astype(BF16)
        return carry

    lax.fori_loop(0, width // chunk, normalise, 0, unroll=4)
    for g in range(16):
        at = pl.ds(pl.multiple_of(4 * rows * g + rows * j, 16), rows)
        hid[g * rows : (g + 1) * rows, :] = hid_all[at, :]
        nrm[g * rows : (g + 1) * rows, :] = (emb[at, :] * inv).astype(BF16)

    @pl.when(first)
    def _():
        for copy in copies:
            copy.wait()
        row = lax.broadcasted_iota(jnp.int32, (8, width), 0)
        fill = jnp.zeros((8, width), F32)
        for n, part in enumerate(split2(1.0 + scale[...]) + split2(shift[...])):
            fill = jnp.where(row == n, part.astype(F32), fill)
        wv[...] = mm(fill.astype(BF16), w[...])

    proj[...] = mm(hid_all[...], w[...], TN)


def forward(ids, pext, stem, bias, scale, shift, w9, block=BLOCK):
    tokens = pext.shape[1]
    count, width, hd = w9.shape
    columns = count * hd
    share = width // 4
    whole = lambda i, ids: (0, 0)
    rows = lambda i, ids: (i, 0)
    lanes = lambda i, ids: (0, i)
    once = pl.Buffered(1)
    vec = pl.BlockSpec((1, width), whole, pipeline_mode=once)
    return pl.pallas_call(
        forward_kernel,
        grid_spec=pltpu.PrefetchScalarGridSpec(
            num_scalar_prefetch=1,
            grid=(tokens // block,),
            in_specs=[
                pl.BlockSpec((256, block), lanes),
                pl.BlockSpec(stem.shape, whole, pipeline_mode=once),
                vec,
                vec,
                vec,
                pl.BlockSpec(memory_space=pl.ANY),
            ],
            out_specs=[
                pl.BlockSpec((block, columns), rows),
                pl.BlockSpec((share, block), lanes),
                pl.BlockSpec((share, block), lanes),
                pl.BlockSpec((8, block), lanes),
                pl.BlockSpec((8, columns), whole),
                pl.BlockSpec((share, 128), whole),
            ],
            scratch_shapes=[
                pltpu.VMEM((width, block), F32),
                pltpu.VMEM((width, block), BF16),
                pltpu.VMEM((256, width), BF16),
                pltpu.VMEM((width, columns), BF16),
                pltpu.VMEM((width, 128), F32),
                pltpu.VMEM((width, 128), F32),
                pltpu.VMEM((256, block), BF16),
                pltpu.VMEM((8, 256), BF16),
                pltpu.SemaphoreType.DMA((count,)),
            ],
        ),
        out_shape=[
            jax.ShapeDtypeStruct((tokens, columns), F32),
            jax.ShapeDtypeStruct((share, tokens), BF16),
            jax.ShapeDtypeStruct((share, tokens), BF16),
            jax.ShapeDtypeStruct((8, tokens), F32),
            jax.ShapeDtypeStruct((8, columns), F32),
            jax.ShapeDtypeStruct((share, 128), F32),
        ],
        compiler_params=pltpu.CompilerParams(vmem_limit_bytes=60 * 2**20),
        cost_estimate=pl.CostEstimate(
            flops=2 * tokens * width * (columns + 256), bytes_accessed=24 * 2**20, transcendentals=0
        ),
        name="forward",
    )(ids, pext, stem, bias, scale, shift, w9)


def attention_kernel(
    ids,
    lists,
    pq,
    pk,
    pv,
    og,
    qg,
    kg,
    wq,
    wk,
    wv,
    mixed,
    means,
    q_s,
    k_s,
    v_s,
    o_s,
    kt_s,
    iq_s,
    ik_s,
    dq_s,
    dk_s,
    dv_s,
    a1_s,
    a2_s,
):
    tokens, hd = pq.shape
    score_scale = hd ** (-0.5)
    j, g = ids[0], ids[1]
    tile = TT * TS * TS
    count = tokens // tile
    frame_tile = TS * TS
    first = pl.program_id(0) == 0
    last = pl.program_id(0) == pl.num_programs(0) - 1

    def rows(b):
        return pl.ds(pl.multiple_of(b * tile, tile), tile)

    def prepare(b, carry):
        at = rows(b)
        for raw, gain, keep, store in ((pq, qg, iq_s, q_s), (pk, kg, ik_s, k_s)):
            r = raw[at, :]
            inv = lax.rsqrt(jnp.mean(r * r, -1, keepdims=True) + ln_eps)
            keep[at, :] = inv
            value = r * inv * gain[...]
            store[at, :] = value.astype(BF16)
        kt_s[:, at] = jnp.transpose(value).astype(BF16)
        v_s[at, :] = pv[at, :].astype(BF16)
        half, t = b // (count // 2), b % (count // 2)
        for frame in range(2):
            to = pl.ds(pl.multiple_of(b * tile + frame * frame_tile, frame_tile), frame_tile)
            o_s[to, :] = og[jnp.bitwise_xor(j, 2 * frame + half), 0, t]
        dk_s[at, :] = jnp.zeros((tile, hd), F32)
        dv_s[at, :] = jnp.zeros((tile, hd), F32)
        return carry

    lax.fori_loop(0, count, prepare, 0, unroll=8)

    def visit(b, carry):
        mine = rows(b)
        q_b = q_s[mine, :]
        o_b = o_s[mine, :]
        near = [rows(lists[g * count + b, n] - g * count) for n in range(KNB)]
        keys = jnp.concatenate([k_s[at, :] for at in near], 0)
        keys_t = jnp.concatenate([kt_s[:, at] for at in near], 1)
        vals = jnp.concatenate([v_s[at, :] for at in near], 0)
        e = jnp.exp2(mm(keys, q_b, NT) * (score_scale * LOG2E))
        prob = e * (1.0 / jnp.sum(e, 0, keepdims=True))
        slope = mm(vals, o_b, NT)
        centre = jnp.sum(prob * slope, 0, keepdims=True)
        shaped = (prob * (slope - centre)).astype(BF16)
        rounded = prob.astype(BF16)
        dq_s[:, mine] = mm(keys_t, shaped)
        dk = mm(shaped, q_b)
        dv = mm(rounded, o_b)
        for n, at in enumerate(near):
            dk_s[at, :] += dk[n * tile : (n + 1) * tile, :]
            dv_s[at, :] += dv[n * tile : (n + 1) * tile, :]
        return carry

    lax.fori_loop(0, count, visit, 0, unroll=8)

    @pl.when(first)
    def _():
        a1_s[...] = jnp.zeros_like(a1_s)
        a2_s[...] = jnp.zeros_like(a2_s)

    def finish(b, carry):
        at = rows(b)
        m1 = a1_s[at, :]
        m2 = a2_s[at, :]
        for i, (raw, gain, keep, grad, vec) in enumerate(
            (
                (pq, qg, iq_s, jnp.transpose(dq_s[:, at]), wq),
                (pk, kg, ik_s, dk_s[at, :], wk),
                (pv, None, None, dv_s[at, :], wv),
            )
        ):
            r = raw[at, :]
            out = grad
            if gain is not None:
                inv = keep[at, :]
                u = grad * (gain[...] * score_scale)
                out = inv * (u - r * (inv * inv * jnp.mean(r * u, -1, keepdims=True)))
            out = out.astype(BF16)
            mixed[i, at, :] = out
            out = out.astype(F32)
            m1 = m1 + out * (vec[0:1, :] + vec[1:2, :])
            m2 = m2 + out * (r - (vec[2:3, :] + vec[3:4, :]))
        a1_s[at, :] = m1
        a2_s[at, :] = m2
        return carry

    lax.fori_loop(0, count, finish, 0, unroll=8)

    @pl.when(last)
    def _():
        for n, total in enumerate((a1_s, a2_s)):
            for b in range(count):
                at = slice(b * tile, (b + 1) * tile)
                row = jnp.sum(jnp.transpose(total[at, :]), axis=0, keepdims=True)
                means[n, :, at] = jnp.broadcast_to(row, (8, tile))


def attention(ids, lists, proj, og, q_gain, k_gain, wv):
    tokens, columns = proj.shape
    hd = q_gain.shape[-1]
    heads = columns // 3 // hd
    pick = lambda i: pl.BlockSpec((tokens, hd), lambda h, *_: (0, i * heads + h))
    vec = lambda i: pl.BlockSpec((8, hd), lambda h, *_: (0, i * heads + h))
    gain = pl.BlockSpec((1, hd), lambda h, *_: (0, 0))
    return pl.pallas_call(
        attention_kernel,
        grid_spec=pltpu.PrefetchScalarGridSpec(
            num_scalar_prefetch=2,
            grid=(heads,),
            in_specs=[
                pick(0),
                pick(1),
                pick(2),
                pl.BlockSpec((4, 1) + og.shape[2:], lambda h, *_: (0, h, 0, 0, 0)),
                gain,
                gain,
                vec(0),
                vec(1),
                vec(2),
            ],
            out_specs=[
                pl.BlockSpec((3, tokens, hd), lambda h, *_: (0, 0, h)),
                pl.BlockSpec((2, 8, tokens), lambda h, *_: (0, 0, 0)),
            ],
            scratch_shapes=[pltpu.VMEM((tokens, hd), BF16)] * 4
            + [pltpu.VMEM((hd, tokens), BF16)]
            + [pltpu.VMEM((tokens, 1), F32)] * 2
            + [pltpu.VMEM((hd, tokens), F32)]
            + [pltpu.VMEM((tokens, hd), F32)] * 4,
        ),
        out_shape=[
            jax.ShapeDtypeStruct((3, tokens, heads * hd), BF16),
            jax.ShapeDtypeStruct((2, 8, tokens), F32),
        ],
        compiler_params=pltpu.CompilerParams(vmem_limit_bytes=48 * 2**20),
        cost_estimate=pl.CostEstimate(
            flops=10 * tokens * 512 * hd * heads, bytes_accessed=10 * 2**20, transcendentals=tokens * 512 * heads
        ),
        name="attention",
    )(ids, lists, proj, proj, proj, og, q_gain, k_gain, wv, wv, wv)


def weight_kernel(ids, hid, mixed, *outs):
    rows, hd = outs[0].shape[2:]
    block = 4 * rows
    x = ids[1] // 4
    for k in range(4):
        at = pl.ds(pl.multiple_of((x + k) % 4 * block, block), block)
        mine = hid[at, :]
        for i in range(3):
            part = mm(mine, mixed[i]).astype(BF16)
            for n in range(3):
                for z in range(4):
                    outs[k][z, 3 * i + n] = part[z * rows : (z + 1) * rows, n * hd : (n + 1) * hd]


def weight_part(ids, hid, mixed, hd):
    share, tokens = hid.shape
    third = mixed.shape[2]
    out = jax.ShapeDtypeStruct((4, 3 * third // hd, share // 16, hd), BF16)
    vmem = pl.BlockSpec(memory_space=pltpu.VMEM)
    return pl.pallas_call(
        weight_kernel,
        in_specs=[pl.BlockSpec(memory_space=pltpu.SMEM), vmem, vmem],
        out_specs=[vmem] * 4,
        out_shape=[out] * 4,
        compiler_params=pltpu.CompilerParams(vmem_limit_bytes=40 * 2**20),
        cost_estimate=pl.CostEstimate(
            flops=2 * share * tokens * 3 * third, bytes_accessed=6 * 2**20, transcendentals=0
        ),
        name="weight_part",
    )(ids, hid, mixed)


def stem_kernel(ids, w9, mixed, nrm, sc, means, inv, pext, own, *rest):
    others, (mixed_t,) = rest[:3], rest[3:]
    third = mixed.shape[2]
    block, tokens = nrm.shape
    count, _, _, _, hd = w9.shape
    w = jnp.concatenate([w9[n, :, 0].reshape(block, hd) for n in range(count)], 1)

    @pl.when(pl.program_id(0) == 0)
    def _():
        for i in range(3):
            mixed_t[i * third : (i + 1) * third, :] = jnp.transpose(mixed[i])

    fg = mm(w, mixed_t[...])
    n = nrm[...].astype(F32)
    scale = 1.0 / (4 * 4 * block)
    m1 = means[0, 0:1, :] * scale
    m2 = means[1, 0:1, :] * scale
    eg = (fg * jnp.concatenate([sc[...]] * (tokens // 128), 1) - m1 - n * m2) * inv[0:1, :]
    hi, lo = split2(eg)
    grad = mm(hi, pext[...], NT) + mm(lo, pext[...], NT)
    shift_grad = jnp.sum(fg, -1, keepdims=True)
    scale_grad = jnp.sum(fg * n, -1, keepdims=True)
    lane = lax.broadcasted_iota(jnp.int32, grad.shape, 1)
    grad = jnp.where(lane == 193, shift_grad, grad)
    grad = jnp.where(lane == 194, scale_grad, grad)
    for k, out in enumerate((own,) + others):

        @pl.when(pl.program_id(0) == k)
        def _():
            out[...] = grad.astype(out.dtype)


def stem_part(ids, w9, mixed, nrm, sc, means, inv, pext):
    share, tokens = nrm.shape
    block = share // 4
    count, width, hd = w9.shape
    w9 = w9.reshape(count, 16, 4, share // 16, hd)
    rows = lambda i, ids: ((i + ids[2]) % 4, 0)
    once = pl.Buffered(1)
    shape = (block, 256)
    return pl.pallas_call(
        stem_kernel,
        grid_spec=pltpu.PrefetchScalarGridSpec(
            num_scalar_prefetch=1,
            grid=(4,),
            in_specs=[
                pl.BlockSpec((count, 4, 1, share // 16, hd), lambda i, ids: (0, (i + ids[2]) % 4, ids[0], 0, 0)),
                pl.BlockSpec(mixed.shape, lambda i, ids: (0, 0, 0), pipeline_mode=once),
                pl.BlockSpec((block, tokens), rows),
                pl.BlockSpec((block, 128), rows),
                pl.BlockSpec(means.shape, lambda i, ids: (0, 0, 0), pipeline_mode=once),
                pl.BlockSpec(inv.shape, lambda i, ids: (0, 0), pipeline_mode=once),
                pl.BlockSpec(pext.shape, lambda i, ids: (0, 0), pipeline_mode=once),
            ],
            out_specs=[pl.BlockSpec(shape, lambda i, ids: (0, 0))] * 4,
            scratch_shapes=[pltpu.VMEM((count * hd, tokens), BF16)],
        ),
        out_shape=[jax.ShapeDtypeStruct(shape, F32)] + [jax.ShapeDtypeStruct(shape, BF16)] * 3,
        compiler_params=pltpu.CompilerParams(vmem_limit_bytes=40 * 2**20),
        cost_estimate=pl.CostEstimate(
            flops=1000, bytes_accessed=1000, transcendentals=0
        ),
        name="stem_part",
    )(ids, w9, mixed, nrm, sc, means, inv, pext)


def per_device(
    latent,
    stem_weight,
    stem_bias,
    mod_shift,
    mod_scale,
    qkv_weight,
    q_gain,
    k_gain,
    tile_lists,
    out_grad,
):
    width = qkv_weight.shape[0]
    heads, hd = qkv_weight.shape[2:]
    columns = 3 * heads * hd
    channels = latent.shape[1]
    seq = lax.axis_size("seq")
    groups = seq // 4
    rows = width // seq
    s = lax.axis_index("seq")
    h = lax.axis_index("head")
    g, j = s // 4, s % 4
    half_rows = HG // 2
    tr, tc = half_rows // TS, WG // TS
    tiles = tr * tc
    cell = TS * TS

    def xor(value, mask):
        return lax.ppermute(value, "seq", [(a, a ^ mask) for a in range(seq)])

    is_low = s % 2 == 0
    even = j < 2
    piece = latent.reshape(channels, tr, TS, 2, tc, TS, 2)
    piece = jnp.transpose(piece, (0, 3, 6, 1, 4, 2, 5)).reshape(4 * channels, tiles * cell)
    border = [(a, a - 2 if a % 4 < 2 else a + 2) for a in range(seq)]
    outer = lax.ppermute(piece, "seq", [(a, b) for a, b in border if 0 <= b < seq])
    pair = jnp.stack([outer, piece])
    facing = xor(pair, 2)
    window = jnp.stack(
        [
            jnp.where(even, outer, facing[0]),
            jnp.where(even, piece, facing[1]),
            jnp.where(even, facing[1], piece),
            jnp.where(even, facing[0], outer),
        ]
    )
    grads = jnp.transpose(out_grad, (1, 0, 2)).reshape(heads, tr, TS, tc, TS, hd)
    grads = jnp.transpose(grads, (0, 1, 3, 2, 4, 5)).reshape(heads, tiles, cell, hd)
    grads = jnp.stack([grads, xor(grads, 1)])
    other = xor(window, 1)
    other, grads = lax.optimization_barrier((other, grads))
    grads = jnp.concatenate([grads, xor(grads, 2)])
    window = jnp.concatenate([jnp.where(is_low, window, other), jnp.where(is_low, other, window)], 2)
    fill = jnp.zeros((256 - 12 * channels, 2 * tiles * cell), BF16).at[:3].set(1)
    pext = jnp.stack(
        [
            jnp.concatenate([window[k], window[k + 1], window[k + 2], fill], 0).reshape(
                256, 2 * tiles, cell
            )
            for k in range(2)
        ],
        2,
    ).reshape(256, 4 * tiles * cell)

    w9 = jnp.transpose(qkv_weight, (1, 2, 0, 3)).reshape(3 * heads, width, hd)
    ids = jnp.stack([j, g, h]).astype(jnp.int32)

    proj, hid, nrm, inv, wv, sc = forward(
        ids, pext, stem_weight, stem_bias[None], mod_scale[None], mod_shift[None], w9
    )
    wv = pltpu.with_memory_space_constraint(wv, pltpu.HBM)
    mixed, means = attention(ids, tile_lists, proj, grads, q_gain[None], k_gain[None], wv)
    weight = list(weight_part(ids, hid, mixed, hd))
    stem = stem_part(ids, w9, mixed, nrm, sc, means, inv, pext)

    for k in range(1, 4):
        pairs = [(a, (a + 16 * k) % seq) for a in range(seq)]
        weight[k] = lax.ppermute(weight[k], "seq", pairs)

    total = stem[0]
    count = lax.axis_size("head")
    for k in range(1, count):
        pairs = [(a, (a + k) % count) for a in range(count)]
        total = total + lax.ppermute(stem[k], "head", pairs).astype(F32)

    def quad_sum(value, low, high):
        held = lax.reduce_precision(value, 8, 7)
        sent = held.astype(BF16)
        near, far, both = (xor(sent, mask).astype(F32) for mask in (low, high, low + high))
        return (held + near) + (far + both)

    total, weight[1], weight[3] = lax.optimization_barrier((total, weight[1], weight[3]))
    total = quad_sum(total, 4, 8)
    total, weight[2] = lax.optimization_barrier((total, weight[2]))
    weight_total = sum(part.astype(F32) for part in weight)

    zhi = g % 4
    parts = []
    for k in range(4):
        part = lax.dynamic_index_in_dim(weight_total, (zhi + k) % 4, 0, keepdims=False)
        if k > 0:
            pairs = [(a, a - a % 16 + (a + 4 * k) % 16) for a in range(seq)]
            part = lax.ppermute(part.astype(BF16), "seq", pairs)
        parts.append(part)
    total = quad_sum(total, 16, 32)
    total, parts[1] = lax.optimization_barrier((total, parts[1]))
    weight_grad = sum(part.astype(F32) for part in parts)
    weight_grad = jnp.transpose(weight_grad.reshape(3, heads, rows, hd), (2, 0, 1, 3))

    held = total.astype(BF16)
    found = [held] + [xor(held, mask) for mask in (1, 2, 3)]
    low, high = j % 2 == 0, j < 2
    swapped = [jnp.where(low, found[m], found[m ^ 1]) for m in range(4)]
    full = jnp.stack([jnp.where(high, swapped[m], swapped[m ^ 2]) for m in range(4)])
    full = full.reshape(4, groups // 4, rows, 256)
    full = jnp.transpose(full, (1, 0, 2, 3)).reshape(width // 4, 256).T.astype(F32)
    base = 12 * channels
    stem_grad = full[:base]
    vector_grad = jnp.stack([full[base + 1], full[base + 2], full[base]])
    return (weight_grad, stem_grad, vector_grad)


def solution(mesh):
    return jax.shard_map(
        per_device,
        mesh=mesh,
        in_specs=(
            P("seq", None, None),
            P(),
            P(),
            P(),
            P(),
            P(None, None, "head", None),
            P(),
            P(),
            P(),
            P("seq", "head", None),
        ),
        out_specs=(P("seq", None, "head", None), P(None, "head"), P(None, "head")),
        check_vma=False,
    )
```
